128 devices in a mesh: dp: 16 (over z, x), fsdp: 8 (over y, core).
Axes of the slice: x: 4, y: 4, z: 4, core: 2. Of those that a mesh axis runs over, the one named last changes fastest.
Arguments:
- frames: bfloat16 [1024, 64, 1024], P(('dp', 'fsdp')), may hold values from -6 to 6
- lengths: int32 [1024], replicated, may hold values from 8 to 64
- owner: int32 [1024], replicated, may hold values from 0 to 15, as said below
- slot: int32 [1024], replicated, may hold values from 0 to 7, as said below
- w_in: bfloat16 [1024, 2048], P('fsdp'), may hold values from -0.1875 to 0.1875
- kernel: float32 [31, 1024], replicated, may hold values from -1 to 1
- dw_gain: float32 [1024], replicated, may hold values from 0.5 to 1.5
- dw_bias: float32 [1024], replicated, may hold values from -3 to 3
- w_out: bfloat16 [1024, 1024], P('fsdp'), may hold values from -0.1875 to 0.1875
- cotangent: bfloat16 [1024, 64, 1024], P(('dp', 'fsdp')), may hold values from -6 to 6
Outputs:
- out_frames: bfloat16 [1024, 64, 1024], P(('dp', 'fsdp'))
- grad_frames: bfloat16 [1024, 64, 1024], P(('dp', 'fsdp'))
- grad_w_in: float32 [1024, 2048], P('fsdp')
- grad_kernel: float32 [31, 1024], replicated
- grad_gain: float32 [1024], replicated
- grad_bias: float32 [1024], replicated
- grad_w_out: float32 [1024, 1024], P('fsdp')
The draws below stay inside these ranges and needn't reach their ends.
Inputs may be any that keep to these rules, and one draw needn't show every extreme that they name: Block b lies on the device whose dp index is b // (8 * 8) and whose fsdp index is (b // 8) % 8; its owner has the same fsdp index. The 8 blocks of one device have 8 different owners, and every owner receives exactly 8 blocks. `slot`: the blocks that one owner receives have different slots.
All inputs are finite; a program needn't handle non-finite values.
Results may differ from the reference program's by a relative error of at most 0.014.
Values may be sent and summed in bfloat16 or wider, within the bound.
A program may use at most 128 MiB of HBM per device.

```python
import math
import jax
import jax.numpy as jnp
from jax import lax

D = 1024
K = 31
BLK = 64
SLOTS = 8
BLOCKS = 1024
N_DP = 16
N_FSDP = 8


def routing_tables(key):
    base = jax.random.fold_in(key, 4242)

    def one_column(column):
        column_key = jax.random.fold_in(base, column)
        order = jax.random.permutation(jax.random.fold_in(column_key, 1), N_DP).astype(jnp.int32)
        inverse = jnp.zeros((N_DP,), jnp.int32).at[order].set(jnp.arange(N_DP, dtype=jnp.int32))
        shifts = jax.random.permutation(jax.random.fold_in(column_key, 2), N_DP)[:SLOTS].astype(jnp.int32)
        source_keys = jax.random.split(jax.random.fold_in(column_key, 3), N_DP)
        picks = jax.vmap(lambda sub: jax.random.permutation(sub, SLOTS))(source_keys).astype(jnp.int32)
        target_keys = jax.random.split(jax.random.fold_in(column_key, 4), N_DP)
        labels = jax.vmap(lambda sub: jax.random.permutation(sub, SLOTS))(target_keys).astype(jnp.int32)
        owners = inverse[(order[:, None] + shifts[picks]) % N_DP]
        places = labels[owners, picks]
        return (owners, places)
    owners, places = jax.vmap(one_column)(jnp.arange(N_FSDP, dtype=jnp.int32))
    owners = jnp.transpose(owners, (1, 0, 2)).reshape(-1).astype(jnp.int32)
    places = jnp.transpose(places, (1, 0, 2)).reshape(-1).astype(jnp.int32)
    return (owners, places)


def draw_owner(key, part):
    return routing_tables(key)[0]


def draw_slot(key, part):
    return routing_tables(key)[1]


def plant(values, rng, low, high):
    spot = [jax.random.randint(jax.random.fold_in(rng, axis), (), 0, length) for axis, length in enumerate(values.shape)]
    main_axis = values.shape.index(max(values.shape))
    beside = spot[:main_axis] + [(spot[main_axis] + 1) % values.shape[main_axis]] + spot[main_axis + 1:]
    return values.at[tuple(spot)].set(low).at[tuple(beside)].set(high)


def shard_levels(rng, extent, cuts, smallest, high):
    gain = 1.0
    for position, blocks in cuts:
        heights = jax.random.uniform(jax.random.fold_in(jax.random.fold_in(rng, 6), position), (blocks,), jnp.float32, smallest / len(cuts), high / len(cuts))
        gain = gain * jnp.repeat(jnp.exp(heights), extent[position] // blocks).reshape((-1,) + (1,) * (len(extent) - 1 - position))
    return gain


def gaussian(stream_key, extent, deviation, limit, cuts=(), kind=jnp.bfloat16):
    level = shard_levels(stream_key, extent, cuts, -0.22, 0.18) if cuts else 1.0
    values = jax.random.normal(stream_key, extent, jnp.float32) * deviation * level
    return jnp.minimum(jnp.maximum(values, -limit), limit).astype(kind)


def setup_inputs(seed: int = 0) -> dict:
    key_list = jax.random.split(jax.random.key(seed), 11)
    frames = gaussian(key_list[0], (BLOCKS, BLK, D), 1.0, 6.0, ((0, 128),))
    lengths = plant(jax.random.randint(key_list[1], (BLOCKS,), 8, BLK + 1), jax.random.fold_in(key_list[1], 1), 8, BLK).astype(jnp.int32)
    owner = draw_owner(jax.random.fold_in(key_list[10], 71), 0)
    slot = draw_slot(jax.random.fold_in(key_list[10], 71), 0)
    w_in = gaussian(key_list[4], (D, 2 * D), D ** -0.5, 0.1875, ((0, 8),))
    kernel = gaussian(key_list[5], (K, D), K ** -0.5, 1.0, (), jnp.float32)
    dw_gain = jnp.clip(jax.random.uniform(key_list[6], (D,), jnp.float32, 0.5, 1.5), 0.5, 1.5)
    dw_bias = gaussian(key_list[7], (D,), 0.5, 3.0, (), jnp.float32)
    w_out = gaussian(key_list[8], (D, D), D ** -0.5, 0.1875, ((0, 8),))
    cotangent = gaussian(key_list[9], (BLOCKS, BLK, D), 1.0, 6.0, ((0, 128),))
    return {"frames": frames, "lengths": lengths, "owner": owner, "slot": slot, "w_in": w_in, "kernel": kernel, "dw_gain": dw_gain, "dw_bias": dw_bias, "w_out": w_out, "cotangent": cotangent}


def layer_statistics(values):
    center = values - lax.optimization_barrier(jnp.mean(values, axis=-1, keepdims=True))
    rstd = lax.rsqrt(lax.optimization_barrier(jnp.mean(center * center, axis=-1, keepdims=True)) + 1e-05)
    return (center * rstd, rstd)

def forward_blocks(frames, lengths, w_in, kernel, dw_gain, dw_bias, w_out):
    element_count, block_number, kernel_width = frames.shape
    frame_mask = (jnp.arange(block_number, dtype=jnp.int32)[None, :] < lengths[:, None]).astype(jnp.float32)[..., None]
    full_input = frames.astype(jnp.float32)
    normalized_input, inverse_std_input = layer_statistics(full_input)
    input_normed = normalized_input.astype(jnp.bfloat16)
    act = jnp.dot(input_normed.reshape(element_count * block_number, kernel_width), w_in, preferred_element_type=jnp.float32)
    act = act.reshape(element_count, block_number, 2 * kernel_width)
    left_context = act[..., :kernel_width]
    sigmoid_values = jax.nn.sigmoid(act[..., kernel_width:])
    glu = left_context * sigmoid_values * frame_mask
    taps = kernel.shape[0]
    half = (taps - 1) // 2
    padded_frames = jnp.pad(glu, ((0, 0), (half, half), (0, 0)))
    conv = jnp.zeros_like(glu)
    for k in range(taps):
        conv = conv + padded_frames[:, k:k + block_number] * kernel[k]
    centered_normalized, inverse_std_conv = layer_statistics(conv)
    conv_values = centered_normalized * dw_gain + dw_bias
    swish_output = (conv_values * jax.nn.sigmoid(conv_values)).astype(jnp.bfloat16)
    mixed = jnp.dot(swish_output.reshape(element_count * block_number, kernel_width), w_out, preferred_element_type=jnp.float32)
    result = ((full_input + mixed.reshape(element_count, block_number, kernel_width)) * frame_mask).astype(jnp.bfloat16)
    saved_residuals = (frame_mask, normalized_input, inverse_std_input, input_normed, left_context, sigmoid_values, padded_frames, centered_normalized, inverse_std_conv, conv_values, swish_output)
    return (result, saved_residuals)

def backward_blocks(cotangent, saved_residuals, w_in, kernel, dw_gain, w_out):
    frame_mask, normalized_input, inverse_std_input, input_normed, left_context, sigmoid_values, padded_frames, centered_normalized, inverse_std_conv, conv_values, swish_output = saved_residuals
    element_count, block_number, kernel_width = normalized_input.shape
    taps = kernel.shape[0]
    half = (taps - 1) // 2
    gfull = cotangent.astype(jnp.float32) * frame_mask
    masked = gfull.astype(jnp.bfloat16)
    dswish = lax.dot_general(masked.reshape(element_count * block_number, kernel_width), w_out, (((1,), (1,)), ((), ())), preferred_element_type=jnp.float32)
    sigz = jax.nn.sigmoid(conv_values)
    dzval = dswish.reshape(element_count, block_number, kernel_width) * sigz * (1.0 + conv_values * (1.0 - sigz))
    d_gain = lax.optimization_barrier(jnp.sum(dzval * centered_normalized, axis=(0, 1)))
    d_bias = lax.optimization_barrier(jnp.sum(dzval, axis=(0, 1)))
    dchat = dzval * dw_gain
    dconv = inverse_std_conv * (dchat - lax.optimization_barrier(jnp.mean(dchat, axis=-1, keepdims=True)) - centered_normalized * lax.optimization_barrier(jnp.mean(dchat * centered_normalized, axis=-1, keepdims=True)))
    d_kernel = jnp.stack([lax.optimization_barrier(jnp.sum(dconv * padded_frames[:, k:k + block_number], axis=(0, 1))) for k in range(taps)])
    dpadded = jnp.pad(dconv, ((0, 0), (half, half), (0, 0)))
    dglu = jnp.zeros_like(dconv)
    for k in range(taps):
        dglu = dglu + dpadded[:, 2 * half - k:2 * half - k + block_number] * kernel[k]
    dglu = dglu * frame_mask
    dact = jnp.concatenate([dglu * sigmoid_values, dglu * left_context * sigmoid_values * (1.0 - sigmoid_values)], axis=-1).astype(jnp.bfloat16)
    normalized_input_gradient = lax.dot_general(dact.reshape(element_count * block_number, 2 * kernel_width), w_in, (((1,), (1,)), ((), ())), preferred_element_type=jnp.float32)
    normalized_input_gradient = normalized_input_gradient.reshape(element_count, block_number, kernel_width)
    norm_gradient = inverse_std_input * (normalized_input_gradient - lax.optimization_barrier(jnp.mean(normalized_input_gradient, axis=-1, keepdims=True)) - normalized_input * lax.optimization_barrier(jnp.mean(normalized_input_gradient * normalized_input, axis=-1, keepdims=True)))
    grad_frames = (norm_gradient + gfull).astype(jnp.bfloat16)
    return (grad_frames, input_normed, dact, swish_output, masked, d_kernel, d_gain, d_bias)

def reference(frames, lengths, owner, slot, w_in, kernel, dw_gain, dw_bias, w_out, cotangent):
    blocks, block_number, kernel_width = frames.shape
    column = jnp.arange(blocks, dtype=jnp.int32) // SLOTS % N_FSDP
    dest = ((owner * N_FSDP + column) * SLOTS + slot).astype(jnp.int32)
    g_source = cotangent[dest]
    groups = blocks // SLOTS
    items = (frames.reshape(groups, SLOTS, block_number, kernel_width), lengths.reshape(groups, SLOTS), g_source.reshape(groups, SLOTS, block_number, kernel_width))

    def step(carry, item):
        xblock, lblock, gblock = item
        result, saved_residuals = forward_blocks(xblock, lblock, w_in, kernel, dw_gain, dw_bias, w_out)
        dx, input_normed, dact, swish_output, masked, d_kernel, d_gain, d_bias = backward_blocks(gblock, saved_residuals, w_in, kernel, dw_gain, w_out)
        term_in = lax.dot_general(input_normed.reshape(-1, kernel_width), dact.reshape(-1, 2 * kernel_width), (((0,), (0,)), ((), ())), preferred_element_type=jnp.float32)
        term_out = lax.dot_general(swish_output.reshape(-1, kernel_width), masked.reshape(-1, kernel_width), (((0,), (0,)), ((), ())), preferred_element_type=jnp.float32)
        carry = (carry[0] + term_in, carry[1] + d_kernel, carry[2] + d_gain, carry[3] + d_bias, carry[4] + term_out)
        return (carry, (result, dx))
    start = (jnp.zeros((kernel_width, 2 * kernel_width), jnp.float32), jnp.zeros(kernel.shape, jnp.float32), jnp.zeros((kernel_width,), jnp.float32), jnp.zeros((kernel_width,), jnp.float32), jnp.zeros((kernel_width, kernel_width), jnp.float32))
    sums, outs = lax.scan(step, start, items)
    result_src = outs[0].reshape(blocks, block_number, kernel_width)
    grad_frames = outs[1].reshape(blocks, block_number, kernel_width)
    out_frames = jnp.zeros_like(frames).at[dest].set(result_src)
    scale = 1.0 / math.sqrt(blocks * block_number)
    return (out_frames, grad_frames, sums[0] * scale, sums[1] * scale, sums[2] * scale, sums[3] * scale, sums[4] * scale)
```

```python
import functools
import math

import jax
import jax.numpy as jnp
from jax import lax
from jax.experimental import pallas as pl
from jax.experimental.pallas import tpu as pltpu
from jax.sharding import PartitionSpec as P

MESH = pl.DeviceIdType.MESH


def layer_statistics(values):
    center = values - jnp.mean(values, axis=-1, keepdims=True)
    rstd = lax.rsqrt(jnp.mean(center * center, axis=-1, keepdims=True) + 1e-05)
    return (center * rstd, rstd)


def forward_blocks(frames, lengths, w_in, kernel, dw_gain, dw_bias, w_out):
    element_count, block_number, kernel_width = frames.shape
    frame_mask = (jnp.arange(block_number, dtype=jnp.int32)[None, :] < lengths[:, None]).astype(
        jnp.float32
    )[..., None]
    full_input = frames.astype(jnp.float32)
    normalized_input, inverse_std_input = layer_statistics(full_input)
    input_normed = normalized_input.astype(jnp.bfloat16)
    act = jnp.dot(
        input_normed.reshape(element_count * block_number, kernel_width),
        w_in,
        preferred_element_type=jnp.float32,
    )
    act = act.reshape(element_count, block_number, 2 * kernel_width)
    left_context = act[..., :kernel_width]
    sigmoid_values = jax.nn.sigmoid(act[..., kernel_width:])
    glu = left_context * sigmoid_values * frame_mask
    taps = kernel.shape[0]
    half = (taps - 1) // 2
    padded_frames = jnp.pad(glu, ((0, 0), (half, half), (0, 0)))
    conv = jnp.zeros_like(glu)
    for k in range(taps):
        conv = conv + padded_frames[:, k : k + block_number] * kernel[k]
    centered_normalized, inverse_std_conv = layer_statistics(conv)
    conv_values = centered_normalized * dw_gain + dw_bias
    swish_output = (conv_values * jax.nn.sigmoid(conv_values)).astype(jnp.bfloat16)
    mixed = jnp.dot(
        swish_output.reshape(element_count * block_number, kernel_width),
        w_out,
        preferred_element_type=jnp.float32,
    )
    result = (
        (full_input + mixed.reshape(element_count, block_number, kernel_width)) * frame_mask
    ).astype(jnp.bfloat16)
    saved_residuals = (
        frame_mask,
        normalized_input,
        inverse_std_input,
        input_normed,
        left_context,
        sigmoid_values,
        padded_frames,
        centered_normalized,
        inverse_std_conv,
        conv_values,
        swish_output,
    )
    return (result, saved_residuals)


def backward_blocks(cotangent, saved_residuals, w_in, kernel, dw_gain, w_out):
    (
        frame_mask,
        normalized_input,
        inverse_std_input,
        input_normed,
        left_context,
        sigmoid_values,
        padded_frames,
        centered_normalized,
        inverse_std_conv,
        conv_values,
        swish_output,
    ) = saved_residuals
    element_count, block_number, kernel_width = normalized_input.shape
    taps = kernel.shape[0]
    half = (taps - 1) // 2
    gfull = cotangent.astype(jnp.float32) * frame_mask
    masked = gfull.astype(jnp.bfloat16)
    dswish = lax.dot_general(
        masked.reshape(element_count * block_number, kernel_width),
        w_out,
        (((1,), (1,)), ((), ())),
        preferred_element_type=jnp.float32,
    )
    sigz = jax.nn.sigmoid(conv_values)
    dzval = (
        dswish.reshape(element_count, block_number, kernel_width)
        * sigz
        * (1.0 + conv_values * (1.0 - sigz))
    )
    d_gain = jnp.sum(dzval * centered_normalized, axis=(0, 1))
    d_bias = jnp.sum(dzval, axis=(0, 1))
    dchat = dzval * dw_gain
    dconv = inverse_std_conv * (
        dchat
        - jnp.mean(dchat, axis=-1, keepdims=True)
        - centered_normalized * jnp.mean(dchat * centered_normalized, axis=-1, keepdims=True)
    )
    d_kernel = jnp.stack(
        [jnp.sum(dconv * padded_frames[:, k : k + block_number], axis=(0, 1)) for k in range(taps)]
    )
    dpadded = jnp.pad(dconv, ((0, 0), (half, half), (0, 0)))
    dglu = jnp.zeros_like(dconv)
    for k in range(taps):
        dglu = dglu + dpadded[:, 2 * half - k : 2 * half - k + block_number] * kernel[k]
    dglu = dglu * frame_mask
    dact = jnp.concatenate(
        [dglu * sigmoid_values, dglu * left_context * sigmoid_values * (1.0 - sigmoid_values)],
        axis=-1,
    ).astype(jnp.bfloat16)
    normalized_input_gradient = lax.dot_general(
        dact.reshape(element_count * block_number, 2 * kernel_width),
        w_in,
        (((1,), (1,)), ((), ())),
        preferred_element_type=jnp.float32,
    )
    normalized_input_gradient = normalized_input_gradient.reshape(
        element_count, block_number, kernel_width
    )
    norm_gradient = inverse_std_input * (
        normalized_input_gradient
        - jnp.mean(normalized_input_gradient, axis=-1, keepdims=True)
        - normalized_input
        * jnp.mean(normalized_input_gradient * normalized_input, axis=-1, keepdims=True)
    )
    grad_frames = (norm_gradient + gfull).astype(jnp.bfloat16)
    return (grad_frames, input_normed, dact, swish_output, masked, d_kernel, d_gain, d_bias)


def route(pattern, form, data):
    return jnp.einsum(form, pattern, data, preferred_element_type=jnp.float32).astype(jnp.bfloat16)


RING = 4


def sum_kernel(scale, h_ref, s_ref, in_ref, out_ref, small_ref, rc, cur1, r1, cur2, r2, cur3, r3,
               cur4, fin, sc_r, sc, sy_r, sz_r, sx_r, fs, send, recv, ssend, srecv):
    data = lax.axis_index("dp")
    shard = lax.axis_index("fsdp")
    z, x = data // RING, data % RING
    y, core = shard // 2, shard % 2
    me = {"y": y, "z": z, "x": x}

    def peer(axis, offset):
        if axis == "core":
            return (data, y * 2 + (1 - core))
        other = lax.rem(me[axis] + offset, RING)
        if axis == "y":
            return (data, other * 2 + core)
        if axis == "z":
            return (other * RING + x, shard)
        return (z * RING + other, shard)

    barrier = pltpu.get_barrier_semaphore()
    pl.semaphore_signal(barrier, inc=1, device_id=peer("core", 0), device_id_type=MESH)
    for axis in ("y", "z", "x"):
        for offset in range(1, RING):
            pl.semaphore_signal(barrier, inc=1, device_id=peer(axis, offset), device_id_type=MESH)
    pl.semaphore_wait(barrier, 10)

    pending = []

    def push(src, dst, send_sem, recv_sem, device):
        copy = pltpu.make_async_remote_copy(
            src_ref=src, dst_ref=dst, send_sem=send_sem, recv_sem=recv_sem,
            device_id=device, device_id_type=MESH)
        copy.start()
        pending.append(copy)
        return copy

    orders = (("y", "z", "x"), ("z", "x", "y"), ("x", "y", "z"))

    def at(ref, axes, axis, index):
        place = axes.index(axis)
        return ref.at[(slice(None),) * place + (index,)]

    def narrow(a):
        return a.astype(jnp.float32)

    first = [push(h_ref.at[1 - core, k], rc.at[k], send.at[0, k, 0], recv.at[0, k, 0], peer("core", 0))
             for k in range(3)]
    small = push(s_ref.at[1 - core], sc_r, ssend.at[0, 0], srecv.at[0, 0], peer("core", 0))

    def start_stage(k, stage, buf, dst):
        axes = [a for a in ("y", "z", "x") if a not in orders[k][: stage - 1]]
        axis = orders[k][stage - 1]
        copies = []
        for offset in range(1, RING):
            other = lax.rem(me[axis] + offset, RING)
            copies.append(push(at(buf, axes, axis, other), dst.at[k, offset - 1],
                               send.at[stage, k, offset - 1], recv.at[stage, k, offset - 1],
                               peer(axis, offset)))
        return copies, at(buf, axes, axis, me[axis])

    live = [None] * 3
    for k in range(3):
        first[k].wait_recv()

        @pl.loop(0, RING * RING)
        def _(i, k=k):
            a, b = i // RING, i % RING
            cur1[k, a, b] = (narrow(h_ref[core, k, a, b]) + narrow(rc[k, a, b])).astype(cur1.dtype)

        live[k] = start_stage(k, 1, cur1.at[k], r1)

    small.wait_recv()
    sc[...] = s_ref[core] + sc_r[...]
    sy_r[y] = sc[y]
    small = []
    for offset in range(1, RING):
        other = lax.rem(y + offset, RING)
        small.append(push(sc.at[other], sy_r.at[y], ssend.at[1, offset - 1], srecv.at[1, offset - 1],
                          peer("y", offset)))

    def gather_small(copies):
        for copy in copies:
            copy.wait_recv()

    def total(ref):
        return (ref[0] + ref[1]) + (ref[2] + ref[3])

    for k in range(3):
        copies, mine = live[k]
        for copy in copies:
            copy.wait_recv()

        @pl.loop(0, RING)
        def _(a, k=k, mine=mine):
            acc = narrow(mine[a])
            for o in range(RING - 1):
                acc = acc + narrow(r1[k, o, a])
            cur2[k, a] = acc.astype(cur2.dtype)

        live[k] = start_stage(k, 2, cur2.at[k], r2)

    gather_small(small)
    sz_r[z] = total(sy_r)
    small = [push(sz_r.at[z], sz_r.at[z], ssend.at[2, o - 1], srecv.at[2, o - 1], peer("z", o))
             for o in range(1, RING)]

    for k in range(3):
        copies, mine = live[k]
        for copy in copies:
            copy.wait_recv()
        acc = narrow(mine[...])
        for o in range(RING - 1):
            acc = acc + narrow(r2[k, o])
        cur3[k] = acc.astype(cur3.dtype)
        live[k] = start_stage(k, 3, cur3.at[k], r3)

    gather_small(small)
    sx_r[x] = total(sz_r)
    small = [push(sx_r.at[x], sx_r.at[x], ssend.at[3, o - 1], srecv.at[3, o - 1], peer("x", o))
             for o in range(1, RING)]

    for k in range(3):
        copies, mine = live[k]
        for copy in copies:
            copy.wait_recv()
        acc = narrow(mine[...])
        for o in range(RING - 1):
            acc = acc + narrow(r3[k, o])
        fin[k, z, x] = acc.astype(fin.dtype)
        axis = "x" if k != 1 else "z"
        live[k] = [push(fin.at[k, z, x], fin.at[k, z, x], send.at[4, k, o - 1], recv.at[4, k, o - 1],
                        peer(axis, o)) for o in range(1, RING)]

    gather_small(small)
    fs[core, y] = total(sx_r)
    small = [push(fs.at[core, y], fs.at[core, y], ssend.at[4, o - 1], srecv.at[4, o - 1], peer("y", o))
             for o in range(1, RING)]

    for k in range(3):
        for copy in live[k]:
            copy.wait_recv()
        axis = "z" if k != 1 else "x"
        mine = fin.at[k, z] if k != 1 else fin.at[k, :, x]
        live[k] = [push(mine, mine, send.at[5, k, o - 1], recv.at[5, k, o - 1], peer(axis, o))
                   for o in range(1, RING)]

    gather_small(small)
    small = push(fs.at[core], fs.at[core], ssend.at[5, 0], srecv.at[5, 0], peer("core", 0))

    rows, cols = fin.shape[3], fin.shape[4]
    for k in range(3):
        for copy in live[k]:
            copy.wait_recv()
        for a in range(RING):
            for b in range(RING):
                piece = narrow(fin[k, a, b]) * scale
                r = pl.ds(a * rows, rows)
                if k < 2:
                    in_ref[r, pl.ds((k * RING + b) * cols, cols)] = piece
                else:
                    out_ref[r, pl.ds(b * cols, cols)] = piece
    small.wait_recv()
    lanes = fs.shape[3]
    for a in range(2):
        for b in range(RING):
            small_ref[:, pl.ds((a * RING + b) * lanes, lanes)] = fs[a, b] * scale
    for copy in pending:
        copy.wait_send()


def sum_all(pieces, small, scale):
    bf, f32 = jnp.bfloat16, jnp.float32
    _, _, _, _, _, rows, cols = pieces.shape
    _, _, lines, lanes = small.shape
    r = RING
    tile = (rows, cols)
    vmem = pl.BlockSpec(memory_space=pltpu.VMEM)
    return pl.pallas_call(
        functools.partial(sum_kernel, scale),
        out_shape=(
            jax.ShapeDtypeStruct((r * rows, 2 * r * cols), f32),
            jax.ShapeDtypeStruct((r * rows, r * cols), f32),
            jax.ShapeDtypeStruct((lines, 2 * r * lanes), f32),
        ),
        in_specs=[vmem, vmem],
        out_specs=(vmem, vmem, vmem),
        scratch_shapes=[
            pltpu.VMEM((3, r, r, r) + tile, bf),
            pltpu.VMEM((3, r, r, r) + tile, bf),
            pltpu.VMEM((3, r - 1, r, r) + tile, bf),
            pltpu.VMEM((3, r, r) + tile, bf),
            pltpu.VMEM((3, r - 1, r) + tile, bf),
            pltpu.VMEM((3, r) + tile, bf),
            pltpu.VMEM((3, r - 1) + tile, bf),
            pltpu.VMEM((3,) + tile, bf),
            pltpu.VMEM((3, r, r) + tile, bf),
            pltpu.VMEM((r, lines, lanes), f32),
            pltpu.VMEM((r, lines, lanes), f32),
            pltpu.VMEM((r, lines, lanes), f32),
            pltpu.VMEM((r, lines, lanes), f32),
            pltpu.VMEM((r, lines, lanes), f32),
            pltpu.VMEM((2, r, lines, lanes), f32),
            pltpu.SemaphoreType.DMA((6, 3, r - 1)),
            pltpu.SemaphoreType.DMA((6, 3, r - 1)),
            pltpu.SemaphoreType.DMA((6, r - 1)),
            pltpu.SemaphoreType.DMA((6, r - 1)),
        ],
        compiler_params=pltpu.CompilerParams(
            collective_id=0, has_side_effects=True, vmem_limit_bytes=48 * 2**20),
        name="sum_all",
    )(pieces, small)


def shards(frames, lengths, owner, slot, w_in, kernel, dw_gain, dw_bias, w_out, cotangent):
    n_data = lax.axis_size("dp")
    n_shard = lax.axis_size("fsdp")
    my_data = lax.axis_index("dp")
    my_shard = lax.axis_index("fsdp")
    slots, block_number, kernel_width = frames.shape

    def column_of(table):
        grid = table.reshape(n_data, n_shard, slots)
        return lax.dynamic_index_in_dim(grid, my_shard, 1, keepdims=False)

    owner_col = column_of(owner)
    slot_col = column_of(slot)
    length_col = column_of(lengths)
    owner_mine = lax.dynamic_index_in_dim(owner_col, my_data, 0, keepdims=False)
    peers = jnp.arange(n_data, dtype=jnp.int32)
    outgoing = (owner_mine[None, :] == peers[:, None]).astype(jnp.bfloat16)
    slot_ids = jnp.arange(slots, dtype=jnp.int32)
    matches = (owner_col == my_data)[None, :, :] & (slot_col[None, :, :] == slot_ids[:, None, None])
    incoming = jnp.sum(matches.astype(jnp.int32), axis=2).astype(jnp.bfloat16)
    length_slot = jnp.sum(jnp.where(matches, length_col[None, :, :], 0), axis=(1, 2))
    full_in, full_out = (
        lax.all_gather(w_in, "fsdp", axis=0, tiled=True),
        lax.all_gather(w_out, "fsdp", axis=0, tiled=True),
    )
    arrived = lax.all_to_all(
        route(outgoing, "pj,jtd->ptd", frames), "dp", split_axis=0, concat_axis=0, tiled=True
    )
    local = route(incoming, "sp,ptd->std", arrived)
    out_frames, saved_residuals = forward_blocks(
        local, length_slot, full_in, kernel, dw_gain, dw_bias, full_out
    )
    grad_here, input_normed, dact, swish_output, masked, d_kernel, d_gain, d_bias = backward_blocks(
        cotangent, saved_residuals, full_in, kernel, dw_gain, full_out
    )
    returned = lax.all_to_all(
        route(incoming, "sp,std->ptd", grad_here), "dp", split_axis=0, concat_axis=0, tiled=True
    )
    grad_frames = route(outgoing, "pj,ptd->jtd", returned)
    xn_flat = input_normed.reshape(-1, kernel_width)
    dact_flat = dact.reshape(-1, 2 * kernel_width)
    swish_flat = swish_output.reshape(-1, kernel_width)
    masked_flat = masked.reshape(-1, kernel_width)
    scale = 1.0 / math.sqrt(slots * block_number * n_data * n_shard)
    contract = (((0,), (0,)), ((), ()))
    part_in = lax.dot_general(xn_flat, dact_flat, contract, preferred_element_type=jnp.float32)
    part_out = lax.dot_general(swish_flat, masked_flat, contract, preferred_element_type=jnp.float32)
    whole = jnp.concatenate([part_in, part_out], axis=1).astype(jnp.bfloat16)
    pieces = whole.reshape(RING, 2, RING, 32, 3, RING, 256).transpose(1, 4, 0, 2, 5, 3, 6)
    lines = jnp.concatenate([d_kernel, d_gain[None], d_bias[None], jnp.zeros((7, kernel_width), jnp.float32)], axis=0)
    lines = lines.reshape(40, 2, RING, 128).transpose(1, 2, 0, 3)
    grad_in, grad_out, small = sum_all(pieces, lines, scale)
    taps = d_kernel.shape[0]
    return (
        out_frames,
        grad_frames,
        grad_in,
        small[:taps],
        small[taps],
        small[taps + 1],
        grad_out,
    )


def solution(mesh):
    placed = (
        P(("dp", "fsdp"), None, None),
        P(),
        P(),
        P(),
        P("fsdp", None),
        P(),
        P(),
        P(),
        P("fsdp", None),
        P(("dp", "fsdp"), None, None),
    )
    return jax.shard_map(
        shards,
        mesh=mesh,
        in_specs=placed,
        out_specs=(
            P(("dp", "fsdp"), None, None),
            P(("dp", "fsdp"), None, None),
            P("fsdp", None),
            P(),
            P(),
            P(),
            P("fsdp", None),
        ),
        check_vma=False,
    )
```

```python
import functools
import math

import jax
import jax.numpy as jnp
from jax import lax
from jax.experimental import pallas as pl
from jax.experimental.pallas import tpu as pltpu
from jax.sharding import PartitionSpec as P

MESH = pl.DeviceIdType.MESH


LANES = 128
CHUNK = 16
EPS = 1e-05


def lanes_of(i, width=LANES):
    return pl.ds(pl.multiple_of(i * width, width), width)


def statistics(values):
    center = values - jnp.mean(values, axis=-1, keepdims=True)
    rstd = lax.rsqrt(jnp.mean(center * center, axis=-1, keepdims=True) + EPS)
    return center * rstd, rstd


def logistic(v):
    return 1.0 / (1.0 + jnp.exp(-v))


def order_matrix(rows, start, size, slots, to_time):
    r = lax.broadcasted_iota(jnp.int32, (size, rows), 0) + start
    c = lax.broadcasted_iota(jnp.int32, (size, rows), 1)
    frames = rows // slots
    if to_time:
        place = (r % slots) * frames + r // slots
    else:
        place = (r % frames) * slots + r // frames
    return jnp.where(c == place, 1.0, 0.0).astype(jnp.bfloat16)


def spread_taps(taps_ref, spread_ref):
    taps, slots, width = spread_ref.shape
    for k in range(taps):
        spread_ref[k] = jnp.broadcast_to(taps_ref[k : k + 1, :], (slots, width))


def slide(padded_ref, spread_ref, start, lanes, flip):
    taps, slots, _ = spread_ref.shape
    weights = [spread_ref[taps - 1 - k if flip else k, :, lanes] for k in range(taps)]
    acc = [None] * CHUNK
    for j in range(CHUNK + taps - 1):
        row = padded_ref[start + j, :, lanes]
        for i in range(max(0, j - taps + 1), min(CHUNK, j + 1)):
            term = weights[j - i] * row
            acc[i] = term if acc[i] is None else acc[i] + term
    return acc


def forward_kernel(pick_ref, x_ref, len_ref, w_in_ref, taps_ref, gain_ref, bias_ref, w_out_ref,
                   send_ref, xp_ref, xn_ref, left_ref, sig_ref, chat_ref, rstd_ref, sw_ref,
                   glu_ref, spread_ref, out_ref):
    rows, width = x_ref.shape
    taps, slots, _ = spread_ref.shape
    frames = rows // slots
    half = (taps - 1) // 2
    block = 64

    spread_taps(taps_ref, spread_ref)
    edge = jnp.zeros((half, slots, width), jnp.float32)
    glu_ref[pl.ds(0, half)] = edge
    glu_ref[pl.ds(half + frames, half)] = edge

    @pl.loop(0, rows // block)
    def _(i):
        r = pl.ds(pl.multiple_of(i * block, block), block)
        order = order_matrix(rows, i * block, block, slots, True)
        mixed = jnp.dot(order, x_ref[...], preferred_element_type=jnp.float32)
        xp_ref[r, :] = mixed.astype(jnp.bfloat16)
        xn_ref[r, :] = statistics(mixed)[0].astype(jnp.bfloat16)

    piece = 256

    @pl.loop(0, width // piece)
    def _(j):
        c = lanes_of(j, piece)
        left_ref[:, c] = jnp.dot(xn_ref[...], w_in_ref[:, c], preferred_element_type=jnp.float32)
        gate = jnp.dot(xn_ref[...], w_in_ref[:, lanes_of(j + width // piece, piece)],
                       preferred_element_type=jnp.float32)
        sig_ref[:, c] = logistic(gate)

    @pl.loop(0, width // LANES)
    def _(l):
        c = lanes_of(l)
        limit = len_ref[...]
        time = lax.broadcasted_iota(jnp.int32, (frames, slots, LANES), 0)
        glu = (left_ref[:, c] * sig_ref[:, c]).reshape(frames, slots, LANES)
        glu_ref[pl.ds(half, frames), :, c] = jnp.where(time < limit[None], glu, 0.0)

        @pl.loop(0, frames // CHUNK)
        def _(t):
            acc = slide(glu_ref, spread_ref, t * CHUNK, c, False)
            for i in range(CHUNK):
                chat_ref[pl.ds(pl.multiple_of((t * CHUNK + i) * slots, slots), slots), c] = acc[i]

    @pl.loop(0, rows // block)
    def _(i):
        r = pl.ds(pl.multiple_of(i * block, block), block)
        chat, rstd = statistics(chat_ref[r, :])
        chat_ref[r, :] = chat
        rstd_ref[r, :] = jnp.broadcast_to(rstd, (block, LANES))
        z = chat * gain_ref[...] + bias_ref[...]
        sw_ref[r, :] = (z * logistic(z)).astype(jnp.bfloat16)

    @pl.loop(0, width // piece)
    def _(j):
        c = lanes_of(j, piece)
        mixed = jnp.dot(sw_ref[...], w_out_ref[:, c], preferred_element_type=jnp.float32)
        time = lax.broadcasted_iota(jnp.int32, (frames, slots, piece), 0)
        limit = jnp.concatenate([len_ref[...]] * (piece // LANES), axis=1)
        out = (xp_ref[:, c].astype(jnp.float32) + mixed).reshape(frames, slots, piece)
        out = jnp.where(time < limit[None], out, 0.0).reshape(rows, piece)
        out_ref[:, c] = out.astype(jnp.bfloat16)

    @pl.loop(0, slots)
    def _(b):
        order = order_matrix(rows, b * frames, frames, slots, False)
        line = jnp.dot(order, out_ref[...], preferred_element_type=jnp.float32)
        send_ref[pick_ref[b]] = line.astype(jnp.bfloat16)


def backward_kernel(from_ref, g_ref, len_ref, xp_ref, xn_ref, left_ref, sig_ref, chat_ref, rstd_ref,
                    sw_ref, w_in_ref, taps_ref, gain_ref, bias_ref, w_out_ref,
                    gx_ref, pieces_ref, small_ref,
                    cot_ref, glu_ref, dconv_ref, spread_ref, gm_ref, da_ref, dx_ref):
    rows, width = xp_ref.shape
    taps, slots, _ = spread_ref.shape
    frames = rows // slots
    half = (taps - 1) // 2
    block = 64
    nt = (((1,), (1,)), ((), ()))
    tn = (((0,), (0,)), ((), ()))
    f32 = jnp.float32

    spread_taps(taps_ref, spread_ref)
    edge = jnp.zeros((half, slots, width), f32)
    for ref in (glu_ref, dconv_ref):
        ref[pl.ds(0, half)] = edge
        ref[pl.ds(half + frames, half)] = edge
    small_ref[...] = jnp.zeros_like(small_ref)

    for b in range(slots):
        cot_ref[pl.ds(b * frames, frames), :] = g_ref[from_ref[b]]

    @pl.loop(0, rows // block)
    def _(i):
        r = pl.ds(pl.multiple_of(i * block, block), block)
        order = order_matrix(rows, i * block, block, slots, True)
        g = jnp.dot(order, cot_ref[...], preferred_element_type=f32)
        time = lax.broadcasted_iota(jnp.int32, (block // slots, slots, width), 0) + i * (block // slots)
        limit = jnp.concatenate([len_ref[...]] * (width // LANES), axis=1)
        g = jnp.where(time < limit[None], g.reshape(block // slots, slots, width), 0.0)
        gm = g.reshape(block, width).astype(jnp.bfloat16)
        gm_ref[r, :] = gm
        ds = lax.dot_general(gm, w_out_ref[...], nt, preferred_element_type=f32)
        chat = chat_ref[r, :]
        gain = gain_ref[...]
        z = chat * gain + bias_ref[...]
        sigz = logistic(z)
        dz = ds * sigz * (1.0 + z * (1.0 - sigz))
        dzc = dz * chat
        for l in range(width // LANES):
            c = pl.ds(l * LANES, LANES)
            at = (l // 4, l % 4)
            small_ref[at[0], at[1], pl.ds(taps, 1), :] += jnp.sum(dzc[:, l * LANES : (l + 1) * LANES], axis=0, keepdims=True)
            small_ref[at[0], at[1], pl.ds(taps + 1, 1), :] += jnp.sum(dz[:, l * LANES : (l + 1) * LANES], axis=0, keepdims=True)
        dchat = dz * gain
        m1 = jnp.mean(dchat, axis=-1, keepdims=True)
        m2 = jnp.mean(dchat * chat, axis=-1, keepdims=True)
        dconv = rstd_ref[r, :][:, :1] * (dchat - m1 - chat * m2)
        dconv_ref[pl.ds(half + i * (block // slots), block // slots)] = dconv.reshape(block // slots, slots, width)

    @pl.loop(0, width // LANES)
    def _(l):
        c = lanes_of(l)
        limit = len_ref[...]
        time = lax.broadcasted_iota(jnp.int32, (frames, slots, LANES), 0)
        glu = (left_ref[:, c] * sig_ref[:, c]).reshape(frames, slots, LANES)
        glu_ref[pl.ds(half, frames), :, c] = jnp.where(time < limit[None], glu, 0.0)

        @pl.loop(0, frames // CHUNK)
        def _(t):
            acc = slide(dconv_ref, spread_ref, t * CHUNK, c, True)
            r = pl.ds(pl.multiple_of(t * CHUNK * slots, CHUNK * slots), CHUNK * slots)
            near = lax.broadcasted_iota(jnp.int32, (CHUNK, slots, LANES), 0) + t * CHUNK
            dglu = jnp.where(near < limit[None], jnp.stack(acc), 0.0).reshape(CHUNK * slots, LANES)
            sig = sig_ref[r, c]
            da_ref[r, c] = (dglu * sig).astype(jnp.bfloat16)
            da_ref[r, lanes_of(l + width // LANES)] = (
                dglu * left_ref[r, c] * sig * (1.0 - sig)).astype(jnp.bfloat16)

        step = 8
        for low in range(0, taps, 16):
            count = min(16, taps - low)

            def body(t, acc, low=low, count=count):
                base = t * step
                d = [dconv_ref[half + base + i, :, c] for i in range(step)]
                acc = list(acc)
                for j in range(step + count - 1):
                    row = glu_ref[base + low + j, :, c]
                    for i in range(max(0, j - count + 1), min(step, j + 1)):
                        acc[j - i] = acc[j - i] + d[i] * row
                return tuple(acc)

            acc = lax.fori_loop(0, frames // step, body,
                                tuple(jnp.zeros((slots, LANES), f32) for _ in range(count)))
            for k in range(count):
                small_ref[l // 4, l % 4, pl.ds(low + k, 1), :] = jnp.sum(acc[k], axis=0, keepdims=True)

    @pl.loop(0, rows // block)
    def _(i):
        r = pl.ds(pl.multiple_of(i * block, block), block)
        dxn = lax.dot_general(da_ref[r, :], w_in_ref[...], nt, preferred_element_type=f32)
        xhat, rstd = statistics(xp_ref[r, :].astype(f32))
        m1 = jnp.mean(dxn, axis=-1, keepdims=True)
        m2 = jnp.mean(dxn * xhat, axis=-1, keepdims=True)
        dx = rstd * (dxn - m1 - xhat * m2) + gm_ref[r, :].astype(f32)
        dx_ref[r, :] = dx.astype(jnp.bfloat16)

    @pl.loop(0, slots)
    def _(b):
        order = order_matrix(rows, b * frames, frames, slots, False)
        line = jnp.dot(order, dx_ref[...], preferred_element_type=f32)
        gx_ref[b] = line.astype(jnp.bfloat16)

    rpiece, cpiece = pieces_ref.shape[5], pieces_ref.shape[6]
    per_shard = width // 8

    @pl.loop(0, 8)
    def _(s):
        lhs_lanes = lanes_of(s, per_shard)

        def save(k, b, part):
            for a in range(4):
                pieces_ref[s % 2, k, s // 2, a, b] = part[a * rpiece : (a + 1) * rpiece, :]

        xn = xn_ref[:, lhs_lanes]
        for k in range(2):
            for b in range(4):
                part = lax.dot_general(xn, da_ref[:, pl.ds((k * 4 + b) * cpiece, cpiece)], tn,
                                       preferred_element_type=f32)
                save(k, b, part.astype(jnp.bfloat16))
        sw = sw_ref[:, lhs_lanes]
        for b in range(4):
            part = lax.dot_general(sw, gm_ref[:, pl.ds(b * cpiece, cpiece)], tn,
                                   preferred_element_type=f32)
            save(2, b, part.astype(jnp.bfloat16))


VMEM_LIMIT = 56 * 2**20


def forward_call(pick, x, limit, w_in, taps, gain, bias, w_out, peers, interpret=False):
    rows, width = x.shape
    slots = limit.shape[0]
    frames = rows // slots
    k = taps.shape[0]
    bf, f32 = jnp.bfloat16, jnp.float32
    vmem = pl.BlockSpec(memory_space=pltpu.VMEM)
    shape = jax.ShapeDtypeStruct
    return pl.pallas_call(
        forward_kernel,
        out_shape=(
            shape((peers, frames, width), bf),
            shape((rows, width), bf),
            shape((rows, width), bf),
            shape((rows, width), f32),
            shape((rows, width), f32),
            shape((rows, width), f32),
            shape((rows, LANES), f32),
            shape((rows, width), bf),
        ),
        in_specs=[pl.BlockSpec(memory_space=pltpu.SMEM)] + [vmem] * 7,
        out_specs=(vmem,) * 8,
        scratch_shapes=[
            pltpu.VMEM((frames + k - 1, slots, width), f32),
            pltpu.VMEM((k, slots, width), f32),
            pltpu.VMEM((rows, width), bf),
        ],
        compiler_params=pltpu.CompilerParams(vmem_limit_bytes=VMEM_LIMIT),
        name="forward",
        interpret=interpret,
    )(pick, x, limit, w_in, taps, gain, bias, w_out)


def backward_call(origin, g, limit, saved, w_in, taps, gain, bias, w_out, interpret=False):
    xp = saved[0]
    rows, width = xp.shape
    slots = limit.shape[0]
    frames = rows // slots
    k = taps.shape[0]
    bf, f32 = jnp.bfloat16, jnp.float32
    vmem = pl.BlockSpec(memory_space=pltpu.VMEM)
    shape = jax.ShapeDtypeStruct
    lines = -(-(k + 2) // 8) * 8
    return pl.pallas_call(
        backward_kernel,
        out_shape=(
            shape((slots, frames, width), bf),
            shape((2, 3, 4, 4, 4, width // 32, width // 4), bf),
            shape((2, 4, lines, width // 8), f32),
        ),
        in_specs=[pl.BlockSpec(memory_space=pltpu.SMEM)] + [vmem] * 14,
        out_specs=(vmem,) * 3,
        scratch_shapes=[
            pltpu.VMEM((rows, width), bf),
            pltpu.VMEM((frames + k - 1, slots, width), f32),
            pltpu.VMEM((frames + k - 1, slots, width), f32),
            pltpu.VMEM((k, slots, width), f32),
            pltpu.VMEM((rows, width), bf),
            pltpu.VMEM((rows, 2 * width), bf),
            pltpu.VMEM((rows, width), bf),
        ],
        compiler_params=pltpu.CompilerParams(vmem_limit_bytes=VMEM_LIMIT),
        name="backward",
        interpret=interpret,
    )(origin, g, limit, *saved, w_in, taps, gain, bias, w_out)


RING = 4


def sum_kernel(scale, h_ref, s_ref, in_ref, out_ref, small_ref, rc, cur1, r1, cur2, r2, cur3, r3,
               cur4, fin, sc_r, sc, sy_r, sz_r, sx_r, fs, send, recv, ssend, srecv):
    data = lax.axis_index("dp")
    shard = lax.axis_index("fsdp")
    z, x = data // RING, data % RING
    y, core = shard // 2, shard % 2
    me = {"y": y, "z": z, "x": x}

    def peer(axis, offset):
        if axis == "core":
            return (data, y * 2 + (1 - core))
        other = lax.rem(me[axis] + offset, RING)
        if axis == "y":
            return (data, other * 2 + core)
        if axis == "z":
            return (other * RING + x, shard)
        return (z * RING + other, shard)

    barrier = pltpu.get_barrier_semaphore()
    pl.semaphore_signal(barrier, inc=1, device_id=peer("core", 0), device_id_type=MESH)
    for axis in ("y", "z", "x"):
        for offset in range(1, RING):
            pl.semaphore_signal(barrier, inc=1, device_id=peer(axis, offset), device_id_type=MESH)
    pl.semaphore_wait(barrier, 10)

    pending = []

    def push(src, dst, send_sem, recv_sem, device):
        copy = pltpu.make_async_remote_copy(
            src_ref=src, dst_ref=dst, send_sem=send_sem, recv_sem=recv_sem,
            device_id=device, device_id_type=MESH)
        copy.start()
        pending.append(copy)
        return copy

    orders = (("y", "z", "x"), ("z", "x", "y"), ("x", "y", "z"))

    def at(ref, axes, axis, index):
        place = axes.index(axis)
        return ref.at[(slice(None),) * place + (index,)]

    def narrow(a):
        return a.astype(jnp.float32)

    first = [push(h_ref.at[1 - core, k], rc.at[k], send.at[0, k, 0], recv.at[0, k, 0], peer("core", 0))
             for k in range(3)]
    small = push(s_ref.at[1 - core], sc_r, ssend.at[0, 0], srecv.at[0, 0], peer("core", 0))

    def start_stage(k, stage, buf, dst):
        axes = [a for a in ("y", "z", "x") if a not in orders[k][: stage - 1]]
        axis = orders[k][stage - 1]
        copies = []
        for offset in range(1, RING):
            other = lax.rem(me[axis] + offset, RING)
            copies.append(push(at(buf, axes, axis, other), dst.at[k, offset - 1],
                               send.at[stage, k, offset - 1], recv.at[stage, k, offset - 1],
                               peer(axis, offset)))
        return copies, at(buf, axes, axis, me[axis])

    live = [None] * 3
    for k in range(3):
        first[k].wait_recv()

        @pl.loop(0, RING * RING)
        def _(i, k=k):
            a, b = i // RING, i % RING
            cur1[k, a, b] = (narrow(h_ref[core, k, a, b]) + narrow(rc[k, a, b])).astype(cur1.dtype)

        live[k] = start_stage(k, 1, cur1.at[k], r1)

    small.wait_recv()
    sc[...] = s_ref[core] + sc_r[...]
    sy_r[y] = sc[y]
    small = []
    for offset in range(1, RING):
        other = lax.rem(y + offset, RING)
        small.append(push(sc.at[other], sy_r.at[y], ssend.at[1, offset - 1], srecv.at[1, offset - 1],
                          peer("y", offset)))

    def gather_small(copies):
        for copy in copies:
            copy.wait_recv()

    def total(ref):
        return (ref[0] + ref[1]) + (ref[2] + ref[3])

    for k in range(3):
        copies, mine = live[k]
        for copy in copies:
            copy.wait_recv()

        @pl.loop(0, RING)
        def _(a, k=k, mine=mine):
            acc = narrow(mine[a])
            for o in range(RING - 1):
                acc = acc + narrow(r1[k, o, a])
            cur2[k, a] = acc.astype(cur2.dtype)

        live[k] = start_stage(k, 2, cur2.at[k], r2)

    gather_small(small)
    sz_r[z] = total(sy_r)
    small = [push(sz_r.at[z], sz_r.at[z], ssend.at[2, o - 1], srecv.at[2, o - 1], peer("z", o))
             for o in range(1, RING)]

    for k in range(3):
        copies, mine = live[k]
        for copy in copies:
            copy.wait_recv()
        acc = narrow(mine[...])
        for o in range(RING - 1):
            acc = acc + narrow(r2[k, o])
        cur3[k] = acc.astype(cur3.dtype)
        live[k] = start_stage(k, 3, cur3.at[k], r3)

    gather_small(small)
    sx_r[x] = total(sz_r)
    small = [push(sx_r.at[x], sx_r.at[x], ssend.at[3, o - 1], srecv.at[3, o - 1], peer("x", o))
             for o in range(1, RING)]

    for k in range(3):
        copies, mine = live[k]
        for copy in copies:
            copy.wait_recv()
        acc = narrow(mine[...])
        for o in range(RING - 1):
            acc = acc + narrow(r3[k, o])
        fin[k, z, x] = acc.astype(fin.dtype)
        axis = "x" if k != 1 else "z"
        live[k] = [push(fin.at[k, z, x], fin.at[k, z, x], send.at[4, k, o - 1], recv.at[4, k, o - 1],
                        peer(axis, o)) for o in range(1, RING)]

    gather_small(small)
    fs[core, y] = total(sx_r)
    small = [push(fs.at[core, y], fs.at[core, y], ssend.at[4, o - 1], srecv.at[4, o - 1], peer("y", o))
             for o in range(1, RING)]

    for k in range(3):
        for copy in live[k]:
            copy.wait_recv()
        axis = "z" if k != 1 else "x"
        mine = fin.at[k, z] if k != 1 else fin.at[k, :, x]
        live[k] = [push(mine, mine, send.at[5, k, o - 1], recv.at[5, k, o - 1], peer(axis, o))
                   for o in range(1, RING)]

    gather_small(small)
    small = push(fs.at[core], fs.at[core], ssend.at[5, 0], srecv.at[5, 0], peer("core", 0))

    rows, cols = fin.shape[3], fin.shape[4]
    for k in range(3):
        for copy in live[k]:
            copy.wait_recv()
        for a in range(RING):
            for b in range(RING):
                piece = narrow(fin[k, a, b]) * scale
                r = pl.ds(a * rows, rows)
                if k < 2:
                    in_ref[r, pl.ds((k * RING + b) * cols, cols)] = piece
                else:
                    out_ref[r, pl.ds(b * cols, cols)] = piece
    small.wait_recv()
    lanes = fs.shape[3]
    for a in range(2):
        for b in range(RING):
            small_ref[:, pl.ds((a * RING + b) * lanes, lanes)] = fs[a, b] * scale
    for copy in pending:
        copy.wait_send()


def sum_all(pieces, small, scale):
    bf, f32 = jnp.bfloat16, jnp.float32
    _, _, _, _, _, rows, cols = pieces.shape
    _, _, lines, lanes = small.shape
    r = RING
    tile = (rows, cols)
    vmem = pl.BlockSpec(memory_space=pltpu.VMEM)
    return pl.pallas_call(
        functools.partial(sum_kernel, scale),
        out_shape=(
            jax.ShapeDtypeStruct((r * rows, 2 * r * cols), f32),
            jax.ShapeDtypeStruct((r * rows, r * cols), f32),
            jax.ShapeDtypeStruct((lines, 2 * r * lanes), f32),
        ),
        in_specs=[vmem, vmem],
        out_specs=(vmem, vmem, vmem),
        scratch_shapes=[
            pltpu.VMEM((3, r, r, r) + tile, bf),
            pltpu.VMEM((3, r, r, r) + tile, bf),
            pltpu.VMEM((3, r - 1, r, r) + tile, bf),
            pltpu.VMEM((3, r, r) + tile, bf),
            pltpu.VMEM((3, r - 1, r) + tile, bf),
            pltpu.VMEM((3, r) + tile, bf),
            pltpu.VMEM((3, r - 1) + tile, bf),
            pltpu.VMEM((3,) + tile, bf),
            pltpu.VMEM((3, r, r) + tile, bf),
            pltpu.VMEM((r, lines, lanes), f32),
            pltpu.VMEM((r, lines, lanes), f32),
            pltpu.VMEM((r, lines, lanes), f32),
            pltpu.VMEM((r, lines, lanes), f32),
            pltpu.VMEM((r, lines, lanes), f32),
            pltpu.VMEM((2, r, lines, lanes), f32),
            pltpu.SemaphoreType.DMA((6, 3, r - 1)),
            pltpu.SemaphoreType.DMA((6, 3, r - 1)),
            pltpu.SemaphoreType.DMA((6, r - 1)),
            pltpu.SemaphoreType.DMA((6, r - 1)),
        ],
        compiler_params=pltpu.CompilerParams(
            collective_id=0, has_side_effects=True, vmem_limit_bytes=48 * 2**20),
        name="sum_all",
    )(pieces, small)


def pick_kernel(index_ref, src_ref, dst_ref, sems):
    copies = []
    for i in range(dst_ref.shape[0]):
        copy = pltpu.make_async_copy(src_ref.at[index_ref[i]], dst_ref.at[i], sems.at[i])
        copy.start()
        copies.append(copy)
    for copy in copies:
        copy.wait()


def pick_blocks(index, blocks):
    count = index.shape[0]
    hbm = pl.BlockSpec(memory_space=pl.ANY)
    return pl.pallas_call(
        pick_kernel,
        out_shape=jax.ShapeDtypeStruct((count,) + blocks.shape[1:], blocks.dtype),
        in_specs=[pl.BlockSpec(memory_space=pltpu.SMEM), hbm],
        out_specs=hbm,
        scratch_shapes=[pltpu.SemaphoreType.DMA((count,))],
        name="pick_blocks",
    )(index, blocks)


def shards(frames, lengths, owner, slot, w_in, kernel, dw_gain, dw_bias, w_out, cotangent):
    n_data = lax.axis_size("dp")
    n_shard = lax.axis_size("fsdp")
    my_data = lax.axis_index("dp")
    my_shard = lax.axis_index("fsdp")
    slots, block_number, width = frames.shape

    def column_of(table):
        grid = table.reshape(n_data, n_shard, slots)
        return lax.dynamic_index_in_dim(grid, my_shard, 1, keepdims=False)

    owner_col = column_of(owner)
    slot_col = column_of(slot)
    owner_mine = lax.dynamic_index_in_dim(owner_col, my_data, 0, keepdims=False)
    length_mine = lax.dynamic_index_in_dim(column_of(lengths), my_data, 0, keepdims=False)
    here = owner_col == my_data
    slot_for = jnp.sum(jnp.where(here, slot_col, 0), axis=1)
    slot_ids = jnp.arange(slots, dtype=jnp.int32)
    peers = jnp.arange(n_data, dtype=jnp.int32)
    matches = here[None, :, :] & (slot_col[None, :, :] == slot_ids[:, None, None])
    source_of = jnp.sum(jnp.where(matches, peers[None, :, None], 0), axis=(1, 2))
    limit = jnp.broadcast_to(length_mine[:, None], (slots, LANES))

    swap = functools.partial(lax.all_to_all, axis_name="dp", split_axis=0, concat_axis=0, tiled=True)
    returned = swap(pick_blocks(slot_for, cotangent))
    full_in = lax.all_gather(w_in, "fsdp", axis=0, tiled=True)
    full_out = lax.all_gather(w_out, "fsdp", axis=0, tiled=True)
    gain, bias = dw_gain[None], dw_bias[None]
    send, *saved = forward_call(
        owner_mine, frames.reshape(slots * block_number, width), limit, full_in, kernel, gain, bias,
        full_out, n_data)
    arrived = swap(send)
    grad_frames, pieces, small = backward_call(
        owner_mine, returned, limit, saved, full_in, kernel, gain, bias, full_out)
    scale = 1.0 / math.sqrt(slots * block_number * n_data * n_shard)
    grad_in, grad_out, small = sum_all(pieces, small, scale)
    out_frames = pick_blocks(source_of, arrived)
    taps = kernel.shape[0]
    return (
        out_frames,
        grad_frames,
        grad_in,
        small[:taps],
        small[taps],
        small[taps + 1],
        grad_out,
    )


def solution(mesh):
    placed = (
        P(("dp", "fsdp"), None, None),
        P(),
        P(),
        P(),
        P("fsdp", None),
        P(),
        P(),
        P(),
        P("fsdp", None),
        P(("dp", "fsdp"), None, None),
    )
    return jax.shard_map(
        shards,
        mesh=mesh,
        in_specs=placed,
        out_specs=(
            P(("dp", "fsdp"), None, None),
            P(("dp", "fsdp"), None, None),
            P("fsdp", None),
            P(),
            P(),
            P(),
            P("fsdp", None),
        ),
        check_vma=False,
    )
```

```python
import math
import types

import jax
import jax.numpy as jnp
from jax import lax
from jax.experimental import pallas as pl
from jax.experimental.pallas import tpu as pltpu
from jax.sharding import PartitionSpec as P

MESH = pl.DeviceIdType.MESH

LANES = 128
CHUNK = 16
PIECE = 256
BLOCK = 64
RING = 4
EPS = 1e-05
NT = (((1,), (1,)), ((), ()))
TN = (((0,), (0,)), ((), ()))
BF16 = jnp.bfloat16
F32 = jnp.float32


def lanes_of(i, width=LANES):
    return pl.ds(pl.multiple_of(i * width, width), width)


def statistics(values):
    center = values - jnp.mean(values, axis=-1, keepdims=True)
    rstd = lax.rsqrt(jnp.mean(center * center, axis=-1, keepdims=True) + EPS)
    return center * rstd, rstd


def logistic(v):
    return 1.0 / (1.0 + jnp.exp(-v))


def order_matrix(rows, slots, to_time):
    r = lax.broadcasted_iota(jnp.int32, (rows, rows), 0)
    c = lax.broadcasted_iota(jnp.int32, (rows, rows), 1)
    frames = rows // slots
    if to_time:
        place = (r % slots) * frames + r // slots
    else:
        place = (r % frames) * slots + r // frames
    return jnp.where(c == place, 1.0, 0.0).astype(BF16)


def prepare(m):
    m.small[...] = jnp.zeros_like(m.small)
    taps, slots, width = m.spread.shape
    half = (taps - 1) // 2
    frames = m.glu.shape[0] - 2 * half
    for k in range(taps):
        m.spread[k] = jnp.broadcast_to(m.taps[k : k + 1, :], (slots, width))
    m.to_time[...] = order_matrix(m.xn.shape[0], slots, True)
    m.to_block[...] = order_matrix(m.xn.shape[0], slots, False)
    edge = jnp.zeros((half, slots, width), F32)
    for ref in (m.glu, m.dconv):
        ref[pl.ds(0, half)] = edge
        ref[pl.ds(half + frames, half)] = edge


def norm_input(m):
    rows, width = m.xp.shape

    @pl.loop(0, width // PIECE)
    def _(j):
        c = lanes_of(j, PIECE)
        m.xp[:, c] = jnp.dot(m.to_time[...], m.x[:, c], preferred_element_type=F32).astype(BF16)

    @pl.loop(0, rows // BLOCK)
    def _(i):
        r = pl.ds(pl.multiple_of(i * BLOCK, BLOCK), BLOCK)
        m.xn[r, :] = statistics(m.xp[r, :].astype(F32))[0].astype(BF16)


def gate_chunk(m, j):
    rows, width = m.xn.shape
    slots = m.limit.shape[0]
    frames = rows // slots
    half = (m.spread.shape[0] - 1) // 2
    c = pl.ds(j * PIECE, PIECE)
    left = jnp.dot(m.xn[...], m.w_in[:, pl.ds(2 * j * PIECE, PIECE)], preferred_element_type=F32)
    gate = jnp.dot(m.xn[...], m.w_in[:, pl.ds((2 * j + 1) * PIECE, PIECE)], preferred_element_type=F32)
    sig = logistic(gate)
    m.sig[:, c] = sig
    time = lax.broadcasted_iota(jnp.int32, (frames, slots, PIECE), 0)
    limit = jnp.concatenate([m.limit[...]] * (PIECE // LANES), axis=1)
    glu = (left * sig).reshape(frames, slots, PIECE)
    m.glu[pl.ds(half, frames), :, c] = jnp.where(time < limit[None], glu, 0.0)


def slide(padded, spread, start, lanes, flip):
    taps = spread.shape[0]
    acc = None
    for k in range(taps):
        weight = spread[taps - 1 - k if flip else k, :, lanes]
        term = weight[None] * padded[pl.ds(start + k, CHUNK), :, lanes]
        acc = term if acc is None else acc + term
    return acc


def conv_chunk(m, j):
    rows, width = m.xn.shape
    slots = m.limit.shape[0]
    steps = rows // slots // CHUNK

    @pl.loop(0, PIECE // LANES * steps)
    def _(i):
        c = lanes_of(j * (PIECE // LANES) + i // steps)
        t = i % steps
        acc = slide(m.glu, m.spread, t * CHUNK, c, False)
        r = pl.ds(pl.multiple_of(t * CHUNK * slots, CHUNK * slots), CHUNK * slots)
        m.chat[r, c] = acc.reshape(CHUNK * slots, LANES)


def norm_conv(m):
    rows, width = m.xn.shape

    @pl.loop(0, rows // BLOCK)
    def _(i):
        r = pl.ds(pl.multiple_of(i * BLOCK, BLOCK), BLOCK)
        chat, rstd = statistics(m.chat[r, :])
        m.chat[r, :] = chat
        m.rstd[r, :] = jnp.broadcast_to(rstd, (BLOCK, LANES))
        z = chat * m.gain[...] + m.bias[...]
        m.sw[r, :] = (z * logistic(z)).astype(BF16)


def mix_out(m):
    rows, width = m.xn.shape
    slots = m.limit.shape[0]
    frames = rows // slots

    @pl.loop(0, width // PIECE)
    def _(j):
        c = lanes_of(j, PIECE)
        mixed = jnp.dot(m.sw[...], m.w_out[:, c], preferred_element_type=F32)
        time = lax.broadcasted_iota(jnp.int32, (frames, slots, PIECE), 0)
        limit = jnp.concatenate([m.limit[...]] * (PIECE // LANES), axis=1)
        out = (m.xp[:, c].astype(F32) + mixed).reshape(frames, slots, PIECE)
        m.dx[:, c] = jnp.where(time < limit[None], out, 0.0).reshape(rows, PIECE).astype(BF16)


def untime(m, dst):
    slots, frames, width = dst.shape

    @pl.loop(0, width // PIECE)
    def _(j):
        c = lanes_of(j, PIECE)
        line = jnp.dot(m.to_block[...], m.dx[:, c], preferred_element_type=F32).astype(BF16)
        for b in range(slots):
            dst[b, :, c] = line[b * frames : (b + 1) * frames, :]


def mask_cotangent(m):
    rows, width = m.xn.shape
    slots = m.limit.shape[0]
    frames = rows // slots

    @pl.loop(0, width // PIECE)
    def _(j):
        c = lanes_of(j, PIECE)
        g = jnp.dot(m.to_time[...], m.dx[:, c], preferred_element_type=F32)
        time = lax.broadcasted_iota(jnp.int32, (frames, slots, PIECE), 0)
        limit = jnp.concatenate([m.limit[...]] * (PIECE // LANES), axis=1)
        g = jnp.where(time < limit[None], g.reshape(frames, slots, PIECE), 0.0)
        m.gm[:, c] = g.reshape(rows, PIECE).astype(BF16)


def norm_conv_back(m):
    rows, width = m.xn.shape
    taps, slots, _ = m.spread.shape
    half = (taps - 1) // 2
    steps = BLOCK // slots
    m.sums[...] = jnp.zeros_like(m.sums)

    @pl.loop(0, width // PIECE)
    def _(j):
        c = lanes_of(j, PIECE)
        m.wide[:, c] = lax.dot_general(m.gm[...], m.w_out[c, :], NT, preferred_element_type=F32)

    @pl.loop(0, rows // BLOCK)
    def _(i):
        r = pl.ds(pl.multiple_of(i * BLOCK, BLOCK), BLOCK)
        ds = m.wide[r, :]
        chat = m.chat[r, :]
        gain = m.gain[...]
        z = chat * gain + m.bias[...]
        sigz = logistic(z)
        dz = ds * sigz * (1.0 + z * (1.0 - sigz))
        m.sums[0] += jnp.sum((dz * chat).reshape(steps, slots, width), axis=0)
        m.sums[1] += jnp.sum(dz.reshape(steps, slots, width), axis=0)
        dchat = dz * gain
        m1 = jnp.mean(dchat, axis=-1, keepdims=True)
        m2 = jnp.mean(dchat * chat, axis=-1, keepdims=True)
        dconv = m.rstd[r, :][:, :1] * (dchat - m1 - chat * m2)
        m.dconv[pl.ds(half + i * steps, steps)] = dconv.reshape(steps, slots, width)


def conv_back(m):
    rows, width = m.xn.shape
    taps, slots, _ = m.spread.shape
    frames = rows // slots
    half = (taps - 1) // 2
    steps = frames // CHUNK

    @pl.loop(0, width // LANES * steps)
    def _(i):
        l = i // steps
        t = i % steps
        c = lanes_of(l)
        acc = slide(m.dconv, m.spread, t * CHUNK, c, True)
        r = pl.ds(pl.multiple_of(t * CHUNK * slots, CHUNK * slots), CHUNK * slots)
        near = lax.broadcasted_iota(jnp.int32, (CHUNK, slots, LANES), 0) + t * CHUNK
        dglu = jnp.where(near < m.limit[...][None], acc, 0.0).reshape(CHUNK * slots, LANES)
        sig = m.sig[r, c]
        glu = m.glu[pl.ds(half + t * CHUNK, CHUNK), :, c].reshape(CHUNK * slots, LANES)
        place = (l // 2) * 4 + l % 2
        m.da[r, lanes_of(place)] = (dglu * sig).astype(BF16)
        m.da[r, lanes_of(place + 2)] = (dglu * glu * (1.0 - sig)).astype(BF16)


def taps_back(m):
    rows, width = m.xn.shape
    taps, slots, _ = m.spread.shape
    frames = rows // slots
    half = (taps - 1) // 2
    lanes_q = width // 8 // LANES
    step = 8

    @pl.loop(0, width // LANES)
    def _(l):
        c = lanes_of(l)
        for low in range(0, taps, 16):
            count = min(16, taps - low)

            def body(t, acc, low=low, count=count):
                base = t * step
                out = []
                d = m.dconv[pl.ds(half + base, step), :, c]
                for k in range(count):
                    row = m.glu[pl.ds(base + low + k, step), :, c]
                    out.append(acc[k] + jnp.sum(d * row, axis=0))
                return tuple(out)

            acc = lax.fori_loop(0, frames // step, body,
                                tuple(jnp.zeros((slots, LANES), F32) for _ in range(count)))
            for k in range(count):
                m.small[l // 4, l % 4, pl.ds(low + k, 1), :] = jnp.sum(acc[k], axis=0, keepdims=True)
        for k in range(2):
            m.small[l // 4, l % 4, pl.ds(taps + k, 1), :] = jnp.sum(m.sums[k, :, c], axis=0, keepdims=True)


def norm_input_back(m):
    rows, width = m.xn.shape

    @pl.loop(0, width // PIECE)
    def _(j):
        c = lanes_of(j, PIECE)
        m.wide[:, c] = lax.dot_general(m.da[...], m.w_in[c, :], NT, preferred_element_type=F32)

    @pl.loop(0, rows // BLOCK)
    def _(i):
        r = pl.ds(pl.multiple_of(i * BLOCK, BLOCK), BLOCK)
        dxn = m.wide[r, :]
        xhat, rstd = statistics(m.xp[r, :].astype(F32))
        m1 = jnp.mean(dxn, axis=-1, keepdims=True)
        m2 = jnp.mean(dxn * xhat, axis=-1, keepdims=True)
        dx = rstd * (dxn - m1 - xhat * m2) + m.gm[r, :].astype(F32)
        m.dx[r, :] = dx.astype(BF16)


def save_pieces(m, y, k, b, part):
    size = m.pieces.shape[4]
    for core in range(2):
        for a in range(RING):
            low = (core * RING + a) * size
            m.pieces[core, k, y, a * RING + b] = part[low : low + size, :]


def weight_in_grad(m):
    @pl.loop(0, RING)
    def _(y):
        xn = m.xn[:, lanes_of(y, PIECE)]
        for q in range(8):
            part = lax.dot_general(xn, m.da[:, pl.ds(q * PIECE, PIECE)], TN, preferred_element_type=F32)
            save_pieces(m, y, q % 2, q // 2, part.astype(BF16))


def weight_out_grad(m):
    @pl.loop(0, RING)
    def _(y):
        sw = m.sw[:, lanes_of(y, PIECE)]
        for b in range(RING):
            part = lax.dot_general(sw, m.gm[:, pl.ds(b * PIECE, PIECE)], TN, preferred_element_type=F32)
            save_pieces(m, y, 2, b, part.astype(BF16))


def module_kernel(scale, names, *refs):
    m = types.SimpleNamespace(**dict(zip(names, refs)))
    data = lax.axis_index("dp")
    shard = lax.axis_index("fsdp")
    y, core = shard // 2, shard % 2
    n_data = m.sendb.shape[0]
    slots, frames, width = m.cot.shape
    rows = slots * frames
    per = m.w_in_shard.shape[0]
    ring_y = range(1, RING)
    ring_d = range(1, n_data)

    def at_y(offset):
        return lax.rem(y + offset, RING)

    def at_d(offset):
        return lax.rem(data + offset, n_data)

    partner = (data, y * 2 + (1 - core))

    def peer_y(offset):
        return (data, at_y(offset) * 2 + core)

    def peer_d(offset):
        return (at_d(offset), shard)

    barrier = pltpu.get_barrier_semaphore()
    pl.semaphore_signal(barrier, inc=1, device_id=partner, device_id_type=MESH)
    for o in ring_y:
        pl.semaphore_signal(barrier, inc=1, device_id=peer_y(o), device_id_type=MESH)
    for o in ring_d:
        pl.semaphore_signal(barrier, inc=1, device_id=peer_d(o), device_id_type=MESH)

    pending = []

    def push(src, dst, sems, place, device, keep=True):
        copy = pltpu.make_async_remote_copy(
            src_ref=src, dst_ref=dst, send_sem=sems[0].at[place], recv_sem=sems[1].at[place],
            device_id=device, device_id_type=MESH)
        copy.start()
        if keep:
            pending.append(copy)
        return copy

    def arrive(copies):
        for copy in copies:
            copy.wait_recv()

    def wide(a):
        return a.astype(F32)

    mine = pl.ds(pl.multiple_of(shard * per, per), per)
    chunks = width // PIECE
    for j in range(chunks):
        m.w_in[mine, pl.ds(2 * j * PIECE, PIECE)] = m.w_in_shard[:, pl.ds(j * PIECE, PIECE)]
        m.w_in[mine, pl.ds((2 * j + 1) * PIECE, PIECE)] = m.w_in_shard[:, pl.ds(width + j * PIECE, PIECE)]
    m.w_out[mine, :] = m.w_out_shard[...]

    @pl.loop(0, n_data)
    def _(p):
        m.sendb[p] = m.cot[m.slot_for[p]]

    pl.semaphore_wait(barrier, 1 + len(ring_y) + len(ring_d))

    def part(j, owner_y):
        r = pl.ds(pl.multiple_of((owner_y * 2 + core) * per, per), per)
        if j < chunks:
            return m.w_in.at[r, pl.ds(2 * j * PIECE, 2 * PIECE)]
        return m.w_out.at[r, :]

    weights, passed = [], []
    for j in range(chunks + 1):
        src = part(j, y)
        weights.append([push(src, src, m.weight_sems, (j, o - 1), peer_y(o)) for o in ring_y])
        passed.append([push(src, src, m.pass_sems, (j, 0), partner)])

    def exchange(dst, sems):
        copies = [push(m.sendb.at[at_d(o)], dst.at[data], sems, o - 1, peer_d(o), False) for o in ring_d]
        dst[data] = m.sendb[data]
        return copies

    cot_copies = exchange(m.cot_recv, m.cot_sems)

    prepare(m)
    norm_input(m)

    def weights_ready(j):
        for o in ring_y:
            weights[j][o - 1].wait_recv()
            src = part(j, lax.rem(y + RING - o, RING))
            passed[j].append(push(src, src, m.pass_sems, (j, o), partner))
        arrive(passed[j])

    for j in range(chunks):
        weights_ready(j)
        gate_chunk(m, j)
        conv_chunk(m, j)
    norm_conv(m)

    arrive(cot_copies)
    for b in range(slots):
        m.dx[pl.ds(b * frames, frames), :] = m.cot_recv[m.owner[b]]
    mask_cotangent(m)

    weights_ready(chunks)
    mix_out(m)
    untime(m, m.lines)
    for copy in cot_copies:
        copy.wait_send()

    @pl.loop(0, n_data)
    def _(p):
        m.sendb[p] = m.lines[m.block_for[p]]

    out_copies = exchange(m.out_recv, m.out_sems)
    pending.extend(out_copies)

    def core_start(k):
        return [push(m.pieces.at[1 - core, k], m.core_recv.at[k], m.core_sems, k, partner)]

    def first(k, copies):
        arrive(copies)

        @pl.loop(0, RING)
        def _(a):
            m.pieces[core, k, a] = (wide(m.pieces[core, k, a]) + wide(m.core_recv[k, a])).astype(BF16)

        if k != 1:
            return [push(m.pieces.at[core, k, at_y(o)], m.recv_y.at[k // 2, o - 1], m.sum_y_sems,
                         (k, o - 1), peer_y(o)) for o in ring_y]
        return [push(m.pieces.at[core, k, :, at_d(o)], m.recv_d.at[o - 1], m.sum_d_sems,
                     (k, o - 1), peer_d(o)) for o in ring_d]

    def second(k, copies):
        arrive(copies)
        if k != 1:
            @pl.loop(0, n_data)
            def _(d):
                acc = wide(m.pieces[core, k, y, d])
                for o in ring_y:
                    acc = acc + wide(m.recv_y[k // 2, o - 1, d])
                m.pieces[core, k, y, d] = acc.astype(BF16)

            return [push(m.pieces.at[core, k, y, at_d(o)], m.last_d.at[k // 2, o - 1], m.sum_d_sems,
                         (k, o - 1), peer_d(o)) for o in ring_d]

        @pl.loop(0, RING)
        def _(a):
            acc = wide(m.pieces[core, k, a, data])
            for o in ring_d:
                acc = acc + wide(m.recv_d[o - 1, a])
            m.pieces[core, k, a, data] = acc.astype(BF16)

        return [push(m.pieces.at[core, k, at_y(o), data], m.last_y.at[o - 1], m.sum_y_sems,
                     (k, o - 1), peer_y(o)) for o in ring_y]

    def third(k, copies):
        arrive(copies)
        acc = wide(m.pieces[core, k, y, data])
        if k != 1:
            for o in ring_d:
                acc = acc + wide(m.last_d[k // 2, o - 1])
        else:
            for o in ring_y:
                acc = acc + wide(m.last_y[o - 1])
        m.fin[k, data] = acc.astype(BF16)
        return [push(m.fin.at[k, data], m.fin.at[k, data], m.fin_sems, (k, o - 1), peer_d(o)) for o in ring_d]

    def last(k, copies):
        arrive(copies)
        size, cols = m.fin.shape[2], m.fin.shape[3]
        for a in range(RING):
            for b in range(RING):
                piece = wide(m.fin[k, a * RING + b]) * scale
                r = pl.ds(a * size, size)
                if k < 2:
                    m.grad_in[r, pl.ds((k * RING + b) * cols, cols)] = piece
                else:
                    m.grad_out[r, pl.ds(b * cols, cols)] = piece

    weight_out_grad(m)
    two = core_start(2)
    norm_conv_back(m)
    two = first(2, two)
    conv_back(m)
    two = second(2, two)
    taps_back(m)

    small = [push(m.small.at[1 - core], m.small_core, m.small_sems, 0, partner)]
    two = third(2, two)
    weight_in_grad(m)
    zero, one = core_start(0), core_start(1)

    arrive(small)
    m.small_core[...] = m.small_core[...] + m.small[core]
    m.small_y[y] = m.small_core[y]
    small = [push(m.small_core.at[at_y(o)], m.small_y.at[y], m.small_sems, o, peer_y(o)) for o in ring_y]

    zero = first(0, zero)
    one = first(1, one)

    arrive(small)
    m.small_d[data] = (m.small_y[0] + m.small_y[1]) + (m.small_y[2] + m.small_y[3])
    small = [push(m.small_d.at[data], m.small_d.at[data], m.small_d_sems, o - 1, peer_d(o)) for o in ring_d]

    norm_input_back(m)
    untime(m, m.grad_frames)
    last(2, two)

    arrive(small)
    total = m.small_d[0]
    for d in range(1, n_data):
        total = total + m.small_d[d]
    m.small_all[core, y] = total
    mine = m.small_all.at[core, y]
    small = [push(mine, mine, m.small_sems, RING + o, peer_y(o)) for o in ring_y]

    zero = second(0, zero)
    one = second(1, one)
    arrive(small)
    half = m.small_all.at[core]
    small = [push(half, half, m.small_sems, 2 * RING, partner)]

    zero = third(0, zero)
    one = third(1, one)

    arrive(out_copies)

    @pl.loop(0, slots)
    def _(s):
        m.out_frames[s] = m.out_recv[m.source_of[s]]

    arrive(small)
    lanes = m.small_all.shape[3]
    for a in range(2):
        for b in range(RING):
            m.small_out[:, pl.ds((a * RING + b) * lanes, lanes)] = m.small_all[a, b] * scale
    last(0, zero)
    last(1, one)
    for copy in pending:
        copy.wait_send()


def module_call(scale, tables, frames, cotangent, limit, w_in, taps, gain, bias, w_out, n_data):
    slots, count, width = frames.shape
    rows = slots * count
    k = taps.shape[0]
    lines = -(-(k + 2) // 8) * 8
    size, cols = width // 32, width // RING
    lanes = width // 8
    shape = jax.ShapeDtypeStruct
    dma = pltpu.SemaphoreType.DMA
    inputs = dict(
        slot_for=tables[0], owner=tables[1], block_for=tables[2], source_of=tables[3],
        x=frames.reshape(rows, width), cot=cotangent, limit=limit, w_in_shard=w_in, taps=taps,
        gain=gain, bias=bias, w_out_shard=w_out)
    outputs = dict(
        out_frames=shape((slots, count, width), BF16),
        grad_frames=shape((slots, count, width), BF16),
        grad_in=shape((width // 8, 2 * width), F32),
        grad_out=shape((width // 8, width), F32),
        small_out=shape((lines, width), F32))
    buffers = dict(
        w_in=((width, 2 * width), BF16), w_out=((width, width), BF16),
        xp=((rows, width), BF16), xn=((rows, width), BF16), sig=((rows, width), F32),
        chat=((rows, width), F32), rstd=((rows, LANES), F32), sw=((rows, width), BF16),
        glu=((count + k - 1, slots, width), F32), dconv=((count + k - 1, slots, width), F32),
        spread=((k, slots, width), F32), gm=((rows, width), BF16), da=((rows, 2 * width), BF16),
        dx=((rows, width), BF16), wide=((rows, width), F32), sums=((2, slots, width), F32),
        to_time=((rows, rows), BF16), to_block=((rows, rows), BF16),
        lines=((slots, count, width), BF16), sendb=((n_data, count, width), BF16),
        cot_recv=((n_data, count, width), BF16), out_recv=((n_data, count, width), BF16),
        pieces=((2, 3, RING, n_data, size, cols), BF16),
        core_recv=((3, RING, n_data, size, cols), BF16),
        recv_y=((2, RING - 1, n_data, size, cols), BF16),
        recv_d=((n_data - 1, RING, size, cols), BF16),
        last_d=((2, n_data - 1, size, cols), BF16), last_y=((RING - 1, size, cols), BF16),
        fin=((3, n_data, size, cols), BF16),
        small=((2, RING, lines, lanes), F32), small_core=((RING, lines, lanes), F32),
        small_y=((RING, lines, lanes), F32), small_d=((n_data, lines, lanes), F32),
        small_all=((2, RING, lines, lanes), F32))
    pairs = dict(
        weight_sems=(5, RING - 1), pass_sems=(5, RING), cot_sems=(n_data - 1,), out_sems=(n_data - 1,),
        core_sems=(3,), sum_y_sems=(3, RING - 1), sum_d_sems=(3, n_data - 1), fin_sems=(3, n_data - 1),
        small_sems=(2 * RING + 1,), small_d_sems=(n_data - 1,))
    names = list(inputs) + list(outputs) + list(buffers)
    vmem = pl.BlockSpec(memory_space=pltpu.VMEM)
    smem = pl.BlockSpec(memory_space=pltpu.SMEM)

    def body(*refs):
        plain, sems = refs[: len(names)], refs[len(names) :]
        both = [(sems[2 * i], sems[2 * i + 1]) for i in range(len(pairs))]
        module_kernel(scale, names + list(pairs), *plain, *both)

    return pl.pallas_call(
        body,
        out_shape=tuple(outputs.values()),
        in_specs=[smem] * 4 + [vmem] * (len(inputs) - 4),
        out_specs=(vmem,) * len(outputs),
        scratch_shapes=[pltpu.VMEM(*b) for b in buffers.values()]
        + [dma(s) for s in pairs.values() for _ in range(2)],
        compiler_params=pltpu.CompilerParams(
            collective_id=0, has_side_effects=True, vmem_limit_bytes=VMEM_LIMIT),
        name="conv_module",
    )(*inputs.values())


VMEM_LIMIT = 63 * 2**20


def shards(frames, lengths, owner, slot, w_in, kernel, dw_gain, dw_bias, w_out, cotangent):
    n_data = lax.axis_size("dp")
    n_shard = lax.axis_size("fsdp")
    my_data = lax.axis_index("dp")
    my_shard = lax.axis_index("fsdp")
    slots, count, width = frames.shape

    def column_of(table):
        grid = table.reshape(n_data, n_shard, slots)
        return lax.dynamic_index_in_dim(grid, my_shard, 1, keepdims=False)

    owner_col = column_of(owner)
    slot_col = column_of(slot)
    owner_mine = lax.dynamic_index_in_dim(owner_col, my_data, 0, keepdims=False)
    length_mine = lax.dynamic_index_in_dim(column_of(lengths), my_data, 0, keepdims=False)
    here = owner_col == my_data
    slot_for = jnp.sum(jnp.where(here, slot_col, 0), axis=1)
    slot_ids = jnp.arange(slots, dtype=jnp.int32)
    peers = jnp.arange(n_data, dtype=jnp.int32)
    block_for = jnp.sum(jnp.where(owner_mine[None, :] == peers[:, None], slot_ids[None, :], 0), axis=1)
    matches = here[None, :, :] & (slot_col[None, :, :] == slot_ids[:, None, None])
    source_of = jnp.sum(jnp.where(matches, peers[None, :, None], 0), axis=(1, 2))
    limit = jnp.broadcast_to(length_mine[:, None], (slots, LANES))
    scale = 1.0 / math.sqrt(slots * count * n_data * n_shard)
    tables = (slot_for, owner_mine, block_for, source_of)
    out_frames, grad_frames, grad_in, grad_out, small = module_call(
        scale, tables, frames, cotangent, limit, w_in, kernel, dw_gain[None], dw_bias[None], w_out, n_data)
    taps = kernel.shape[0]
    return (
        out_frames,
        grad_frames,
        grad_in,
        small[:taps],
        small[taps],
        small[taps + 1],
        grad_out,
    )


def solution(mesh):
    placed = (
        P(("dp", "fsdp"), None, None),
        P(),
        P(),
        P(),
        P("fsdp", None),
        P(),
        P(),
        P(),
        P("fsdp", None),
        P(("dp", "fsdp"), None, None),
    )
    return jax.shard_map(
        shards,
        mesh=mesh,
        in_specs=placed,
        out_specs=(
            P(("dp", "fsdp"), None, None),
            P(("dp", "fsdp"), None, None),
            P("fsdp", None),
            P(),
            P(),
            P(),
            P("fsdp", None),
        ),
        check_vma=False,
    )
```

```python
import math
import types

import jax
import jax.numpy as jnp
from jax import lax
from jax.experimental import pallas as pl
from jax.experimental.pallas import tpu as pltpu
from jax.sharding import PartitionSpec as P

MESH = pl.DeviceIdType.MESH

LANES = 128
CHUNK = 16
PIECE = 256
BLOCK = 64
RING = 4
EPS = 1e-05
NT = (((1,), (1,)), ((), ()))
TN = (((0,), (0,)), ((), ()))
BF16 = jnp.bfloat16
F32 = jnp.float32


def lanes_of(i, width=LANES):
    return pl.ds(pl.multiple_of(i * width, width), width)


def statistics(values):
    center = values - jnp.mean(values, axis=-1, keepdims=True)
    rstd = lax.rsqrt(jnp.mean(center * center, axis=-1, keepdims=True) + EPS)
    return center * rstd, rstd


def logistic(v):
    return 1.0 / (1.0 + jnp.exp(-v))


def order_matrix(rows, slots, to_time):
    r = lax.broadcasted_iota(jnp.int32, (rows, rows), 0)
    c = lax.broadcasted_iota(jnp.int32, (rows, rows), 1)
    frames = rows // slots
    if to_time:
        place = (r % slots) * frames + r // slots
    else:
        place = (r % frames) * slots + r // frames
    return jnp.where(c == place, 1.0, 0.0).astype(BF16)


def prepare(m):
    m.small[...] = jnp.zeros_like(m.small)
    taps, slots, width = m.spread.shape
    half = (taps - 1) // 2
    frames = m.glu.shape[0] - 2 * half
    for k in range(taps):
        m.spread[k] = jnp.broadcast_to(m.taps[k : k + 1, :], (slots, width))
    m.to_time[...] = order_matrix(m.xn.shape[0], slots, True)
    m.to_block[...] = order_matrix(m.xn.shape[0], slots, False)
    edge = jnp.zeros((half, slots, width), F32)
    for ref in (m.glu, m.dconv):
        ref[pl.ds(0, half)] = edge
        ref[pl.ds(half + frames, half)] = edge


def norm_input(m):
    rows, width = m.xp.shape

    @pl.loop(0, width // PIECE)
    def _(j):
        c = lanes_of(j, PIECE)
        m.xp[:, c] = jnp.dot(m.to_time[...], m.x[:, c], preferred_element_type=F32).astype(BF16)

    @pl.loop(0, rows // BLOCK)
    def _(i):
        r = pl.ds(pl.multiple_of(i * BLOCK, BLOCK), BLOCK)
        m.xn[r, :] = statistics(m.xp[r, :].astype(F32))[0].astype(BF16)


def gate_chunk(m, j):
    rows, width = m.xn.shape
    slots = m.limit.shape[0]
    frames = rows // slots
    half = (m.spread.shape[0] - 1) // 2
    c = pl.ds(j * PIECE, PIECE)
    left = jnp.dot(m.xn[...], m.w_in[:, pl.ds(2 * j * PIECE, PIECE)], preferred_element_type=F32)
    gate = jnp.dot(m.xn[...], m.w_in[:, pl.ds((2 * j + 1) * PIECE, PIECE)], preferred_element_type=F32)
    sig = logistic(gate)
    m.sig[:, c] = sig
    time = lax.broadcasted_iota(jnp.int32, (frames, slots, PIECE), 0)
    limit = jnp.concatenate([m.limit[...]] * (PIECE // LANES), axis=1)
    glu = (left * sig).reshape(frames, slots, PIECE)
    m.glu[pl.ds(half, frames), :, c] = jnp.where(time < limit[None], glu, 0.0)


def slide(padded, spread, start, lanes, flip):
    taps = spread.shape[0]
    acc = None
    for k in range(taps):
        weight = spread[taps - 1 - k if flip else k, :, lanes]
        term = weight[None] * padded[pl.ds(start + k, CHUNK), :, lanes]
        acc = term if acc is None else acc + term
    return acc


def conv_chunk(m, j):
    rows, width = m.xn.shape
    slots = m.limit.shape[0]
    steps = rows // slots // CHUNK

    @pl.loop(0, PIECE // LANES * steps)
    def _(i):
        c = lanes_of(j * (PIECE // LANES) + i // steps)
        t = i % steps
        acc = slide(m.glu, m.spread, t * CHUNK, c, False)
        r = pl.ds(pl.multiple_of(t * CHUNK * slots, CHUNK * slots), CHUNK * slots)
        m.chat[r, c] = acc.reshape(CHUNK * slots, LANES)


def norm_conv(m):
    rows, width = m.xn.shape

    @pl.loop(0, rows // BLOCK)
    def _(i):
        r = pl.ds(pl.multiple_of(i * BLOCK, BLOCK), BLOCK)
        chat, rstd = statistics(m.chat[r, :])
        m.chat[r, :] = chat
        m.rstd[r, :] = jnp.broadcast_to(rstd, (BLOCK, LANES))
        z = chat * m.gain[...] + m.bias[...]
        m.sw[r, :] = (z * logistic(z)).astype(BF16)


def mix_out(m):
    rows, width = m.xn.shape
    slots = m.limit.shape[0]
    frames = rows // slots

    @pl.loop(0, width // PIECE)
    def _(j):
        c = lanes_of(j, PIECE)
        mixed = jnp.dot(m.sw[...], m.w_out[:, c], preferred_element_type=F32)
        time = lax.broadcasted_iota(jnp.int32, (frames, slots, PIECE), 0)
        limit = jnp.concatenate([m.limit[...]] * (PIECE // LANES), axis=1)
        out = (m.xp[:, c].astype(F32) + mixed).reshape(frames, slots, PIECE)
        m.dx[:, c] = jnp.where(time < limit[None], out, 0.0).reshape(rows, PIECE).astype(BF16)


def untime(m, dst):
    slots, frames, width = dst.shape

    @pl.loop(0, width // PIECE)
    def _(j):
        c = lanes_of(j, PIECE)
        line = jnp.dot(m.to_block[...], m.dx[:, c], preferred_element_type=F32).astype(BF16)
        for b in range(slots):
            dst[b, :, c] = line[b * frames : (b + 1) * frames, :]


def mask_cotangent(m):
    rows, width = m.xn.shape
    slots = m.limit.shape[0]
    frames = rows // slots

    @pl.loop(0, width // PIECE)
    def _(j):
        c = lanes_of(j, PIECE)
        g = jnp.dot(m.to_time[...], m.dx[:, c], preferred_element_type=F32)
        time = lax.broadcasted_iota(jnp.int32, (frames, slots, PIECE), 0)
        limit = jnp.concatenate([m.limit[...]] * (PIECE // LANES), axis=1)
        g = jnp.where(time < limit[None], g.reshape(frames, slots, PIECE), 0.0)
        m.gm[:, c] = g.reshape(rows, PIECE).astype(BF16)


def norm_conv_back(m):
    rows, width = m.xn.shape
    taps, slots, _ = m.spread.shape
    half = (taps - 1) // 2
    steps = BLOCK // slots
    m.sums[...] = jnp.zeros_like(m.sums)

    @pl.loop(0, width // PIECE)
    def _(j):
        c = lanes_of(j, PIECE)
        m.wide[:, c] = lax.dot_general(m.gm[...], m.w_out[c, :], NT, preferred_element_type=F32)

    @pl.loop(0, rows // BLOCK)
    def _(i):
        r = pl.ds(pl.multiple_of(i * BLOCK, BLOCK), BLOCK)
        ds = m.wide[r, :]
        chat = m.chat[r, :]
        gain = m.gain[...]
        z = chat * gain + m.bias[...]
        sigz = logistic(z)
        dz = ds * sigz * (1.0 + z * (1.0 - sigz))
        m.sums[0] += jnp.sum((dz * chat).reshape(steps, slots, width), axis=0)
        m.sums[1] += jnp.sum(dz.reshape(steps, slots, width), axis=0)
        dchat = dz * gain
        m1 = jnp.mean(dchat, axis=-1, keepdims=True)
        m2 = jnp.mean(dchat * chat, axis=-1, keepdims=True)
        dconv = m.rstd[r, :][:, :1] * (dchat - m1 - chat * m2)
        m.dconv[pl.ds(half + i * steps, steps)] = dconv.reshape(steps, slots, width)


def conv_back(m, side):
    rows, width = m.xn.shape
    taps, slots, _ = m.spread.shape
    frames = rows // slots
    half = (taps - 1) // 2
    steps = frames // CHUNK
    tiles = width // LANES // 2

    @pl.loop(0, tiles * steps)
    def _(i):
        l = side * tiles + i // steps
        t = i % steps
        c = lanes_of(l)
        acc = slide(m.dconv, m.spread, t * CHUNK, c, True)
        r = pl.ds(pl.multiple_of(t * CHUNK * slots, CHUNK * slots), CHUNK * slots)
        near = lax.broadcasted_iota(jnp.int32, (CHUNK, slots, LANES), 0) + t * CHUNK
        dglu = jnp.where(near < m.limit[...][None], acc, 0.0).reshape(CHUNK * slots, LANES)
        sig = m.sig[r, c]
        glu = m.glu[pl.ds(half + t * CHUNK, CHUNK), :, c].reshape(CHUNK * slots, LANES)
        place = (l // 2) * 4 + l % 2
        m.da[r, lanes_of(place)] = (dglu * sig).astype(BF16)
        m.da[r, lanes_of(place + 2)] = (dglu * glu * (1.0 - sig)).astype(BF16)


def taps_back(m):
    rows, width = m.xn.shape
    taps, slots, _ = m.spread.shape
    frames = rows // slots
    half = (taps - 1) // 2
    lanes_q = width // 8 // LANES
    step = 8

    @pl.loop(0, width // LANES)
    def _(l):
        c = lanes_of(l)
        for low in range(0, taps, 16):
            count = min(16, taps - low)

            def body(t, acc, low=low, count=count):
                base = t * step
                out = []
                d = m.dconv[pl.ds(half + base, step), :, c]
                for k in range(count):
                    row = m.glu[pl.ds(base + low + k, step), :, c]
                    out.append(acc[k] + jnp.sum(d * row, axis=0))
                return tuple(out)

            acc = lax.fori_loop(0, frames // step, body,
                                tuple(jnp.zeros((slots, LANES), F32) for _ in range(count)))
            for k in range(count):
                m.small[l // 4, l % 4, pl.ds(low + k, 1), :] = jnp.sum(acc[k], axis=0, keepdims=True)
        for k in range(2):
            m.small[l // 4, l % 4, pl.ds(taps + k, 1), :] = jnp.sum(m.sums[k, :, c], axis=0, keepdims=True)


def project_back(m):
    width = m.xn.shape[1]

    @pl.loop(0, width // PIECE)
    def _(j):
        c = lanes_of(j, PIECE)
        m.wide[:, c] = lax.dot_general(m.da[...], m.w_in[c, :], NT, preferred_element_type=F32)


def norm_input_back(m):
    rows, width = m.xn.shape

    @pl.loop(0, rows // BLOCK)
    def _(i):
        r = pl.ds(pl.multiple_of(i * BLOCK, BLOCK), BLOCK)
        dxn = m.wide[r, :]
        xhat, rstd = statistics(m.xp[r, :].astype(F32))
        m1 = jnp.mean(dxn, axis=-1, keepdims=True)
        m2 = jnp.mean(dxn * xhat, axis=-1, keepdims=True)
        dx = rstd * (dxn - m1 - xhat * m2) + m.gm[r, :].astype(F32)
        m.dx[r, :] = dx.astype(BF16)


def save_pieces(m, y, k, b, part):
    size = m.pieces.shape[4]
    for core in range(2):
        for a in range(RING):
            low = (core * RING + a) * size
            m.pieces[core, k, y, a * RING + b] = part[low : low + size, :]


def weight_in_grad(m, side):
    @pl.loop(0, RING)
    def _(y):
        xn = m.xn[:, lanes_of(y, PIECE)]
        for b in range(RING):
            cols = m.da[:, pl.ds((side * RING + b) * PIECE, PIECE)]
            part = lax.dot_general(xn, cols, TN, preferred_element_type=F32)
            save_pieces(m, y, side, b, part.astype(BF16))


def weight_out_grad(m):
    @pl.loop(0, RING)
    def _(y):
        sw = m.sw[:, lanes_of(y, PIECE)]
        for b in range(RING):
            part = lax.dot_general(sw, m.gm[:, pl.ds(b * PIECE, PIECE)], TN, preferred_element_type=F32)
            save_pieces(m, y, 2, b, part.astype(BF16))


def module_kernel(scale, names, *refs):
    m = types.SimpleNamespace(**dict(zip(names, refs)))
    data = lax.axis_index("dp")
    shard = lax.axis_index("fsdp")
    y, core = shard // 2, shard % 2
    n_data = m.sendb.shape[0]
    slots, frames, width = m.cot.shape
    rows = slots * frames
    per = m.w_in_shard.shape[0]
    ring_y = range(1, RING)
    ring_d = range(1, n_data)

    def at_y(offset):
        return lax.rem(y + offset, RING)

    def at_d(offset):
        return lax.rem(data + offset, n_data)

    partner = (data, y * 2 + (1 - core))

    def peer_y(offset):
        return (data, at_y(offset) * 2 + core)

    def peer_d(offset):
        return (at_d(offset), shard)

    barrier = pltpu.get_barrier_semaphore()
    pl.semaphore_signal(barrier, inc=1, device_id=partner, device_id_type=MESH)
    for o in ring_y:
        pl.semaphore_signal(barrier, inc=1, device_id=peer_y(o), device_id_type=MESH)
    for o in ring_d:
        pl.semaphore_signal(barrier, inc=1, device_id=peer_d(o), device_id_type=MESH)

    pending = []

    def push(src, dst, sems, place, device, keep=True):
        copy = pltpu.make_async_remote_copy(
            src_ref=src, dst_ref=dst, send_sem=sems[0].at[place], recv_sem=sems[1].at[place],
            device_id=device, device_id_type=MESH)
        copy.start()
        if keep:
            pending.append(copy)
        return copy

    def arrive(copies):
        for copy in copies:
            copy.wait_recv()

    def wide(a):
        return a.astype(F32)

    mine = pl.ds(pl.multiple_of(shard * per, per), per)
    chunks = width // PIECE
    for j in range(chunks):
        m.w_in[mine, pl.ds(2 * j * PIECE, PIECE)] = m.w_in_shard[:, pl.ds(j * PIECE, PIECE)]
        m.w_in[mine, pl.ds((2 * j + 1) * PIECE, PIECE)] = m.w_in_shard[:, pl.ds(width + j * PIECE, PIECE)]
    m.w_out[mine, :] = m.w_out_shard[...]

    n_shard = 2 * RING

    def base(p):
        return (p * n_shard + shard) * slots

    @pl.loop(0, n_data)
    def _(p):
        found, place, out_block = 0, 0, 0
        for j in range(slots):
            hit = m.owner[base(p) + j] == data
            found = found + jnp.where(hit, 1, 0)
            place = place + jnp.where(hit, m.slot[base(p) + j], 0)
            out_block = out_block + jnp.where(m.owner[base(data) + j] == p, j, 0)
        m.place[p] = place - slots * (1 - found)
        m.block_for[p] = jnp.minimum(out_block, slots - 1)
        m.sendb[p] = m.cot[jnp.minimum(place, slots - 1)]

    pl.semaphore_wait(barrier, 1 + len(ring_y) + len(ring_d))

    def part(j, owner_y):
        r = pl.ds(pl.multiple_of((owner_y * 2 + core) * per, per), per)
        if j < chunks:
            return m.w_in.at[r, pl.ds(2 * j * PIECE, 2 * PIECE)]
        return m.w_out.at[r, :]

    weights, passed = [], []
    right, left = 1, RING - 1

    def send_weights(j):
        src = part(j, y)
        weights.append([push(src, src, m.weight_sems, (j, i), peer_y(o)) for i, o in enumerate((right, left))])
        passed.append([push(src, src, m.pass_sems, (j, 0), partner)])

    ahead = 3
    for j in range(ahead):
        send_weights(j)

    def exchange(dst, sems):
        copies = [push(m.sendb.at[at_d(o)], dst.at[data], sems, o - 1, peer_d(o), False) for o in ring_d]
        dst[data] = m.sendb[data]
        return copies

    cot_copies = exchange(m.cot_recv, m.cot_sems)

    for b in range(slots):
        m.limit[pl.ds(b, 1), :] = jnp.full((1, LANES), m.lengths[base(data) + b], jnp.int32)
    prepare(m)
    norm_input(m)

    @pl.loop(0, slots)
    def _(s):
        source = 0
        for p in range(n_data):
            source = source + jnp.where(m.place[p] == s, p, 0)
        m.source_of[s] = jnp.minimum(source, n_data - 1)

    def weights_near(j):
        for i, (far, near) in enumerate(((left, right), (right, left))):
            weights[j][i].wait_recv()
            src = part(j, at_y(far))
            piece = src.at[pl.ds(i * (per // 2), per // 2), :]
            weights[j].append(push(piece, piece, m.weight_sems, (j, 2 + i), peer_y(near)))
            passed[j].append(push(src, src, m.pass_sems, (j, 1 + i), partner))
        if j + ahead <= chunks:
            send_weights(j + ahead)

    def weights_far(j):
        arrive(weights[j][2:])
        src = part(j, at_y(2))
        passed[j].append(push(src, src, m.pass_sems, (j, 3), partner))
        arrive(passed[j])

    weights_near(0)
    for j in range(chunks):
        weights_near(j + 1)
        weights_far(j)
        gate_chunk(m, j)
        conv_chunk(m, j)
    norm_conv(m)

    arrive(cot_copies)
    for b in range(slots):
        m.dx[pl.ds(b * frames, frames), :] = m.cot_recv[m.owner[base(data) + b]]
    mask_cotangent(m)

    weights_far(chunks)
    mix_out(m)
    untime(m, m.lines)
    for copy in cot_copies:
        copy.wait_send()

    @pl.loop(0, n_data)
    def _(p):
        m.sendb[p] = m.lines[m.block_for[p]]

    out_copies = exchange(m.out_recv, m.out_sems)
    pending.extend(out_copies)

    def core_start(k):
        return [push(m.pieces.at[1 - core, k], m.core_recv.at[k], m.core_sems, k, partner)]

    def first(k, copies):
        arrive(copies)

        @pl.loop(0, RING)
        def _(a):
            m.pieces[core, k, a] = (wide(m.pieces[core, k, a]) + wide(m.core_recv[k, a])).astype(BF16)

        if k != 1:
            return [push(m.pieces.at[core, k, at_y(o)], m.recv_y.at[k // 2, o - 1], m.sum_y_sems,
                         (k, o - 1), peer_y(o)) for o in ring_y]
        return [push(m.pieces.at[core, k, :, at_d(o)], m.recv_d.at[o - 1], m.sum_d_sems,
                     (k, o - 1), peer_d(o)) for o in ring_d]

    def second(k, copies):
        arrive(copies)
        if k != 1:
            @pl.loop(0, n_data)
            def _(d):
                acc = wide(m.pieces[core, k, y, d])
                for o in ring_y:
                    acc = acc + wide(m.recv_y[k // 2, o - 1, d])
                m.pieces[core, k, y, d] = acc.astype(BF16)

            return [push(m.pieces.at[core, k, y, at_d(o)], m.last_d.at[k // 2, o - 1], m.sum_d_sems,
                         (k, o - 1), peer_d(o)) for o in ring_d]

        @pl.loop(0, RING)
        def _(a):
            acc = wide(m.pieces[core, k, a, data])
            for o in ring_d:
                acc = acc + wide(m.recv_d[o - 1, a])
            m.pieces[core, k, a, data] = acc.astype(BF16)

        return [push(m.pieces.at[core, k, at_y(o), data], m.last_y.at[o - 1], m.sum_y_sems,
                     (k, o - 1), peer_y(o)) for o in ring_y]

    def third(k, copies):
        arrive(copies)
        acc = wide(m.pieces[core, k, y, data])
        if k != 1:
            for o in ring_d:
                acc = acc + wide(m.last_d[k // 2, o - 1])
        else:
            for o in ring_y:
                acc = acc + wide(m.last_y[o - 1])
        m.fin[k, data] = acc.astype(BF16)
        return [push(m.fin.at[k, data], m.fin.at[k, data], m.fin_sems, (k, o - 1), peer_d(o)) for o in ring_d]

    def last(k, copies):
        arrive(copies)
        size, cols = m.fin.shape[2], m.fin.shape[3]
        for a in range(RING):
            for b in range(RING):
                piece = wide(m.fin[k, a * RING + b]) * scale
                r = pl.ds(a * size, size)
                if k < 2:
                    m.grad_in[r, pl.ds((b % 2 * RING + k * 2 + b // 2) * cols, cols)] = piece
                else:
                    m.grad_out[r, pl.ds(b * cols, cols)] = piece

    weight_out_grad(m)
    two = core_start(2)
    norm_conv_back(m)
    two = first(2, two)
    conv_back(m, 0)
    weight_in_grad(m, 0)
    zero = core_start(0)
    two = second(2, two)
    conv_back(m, 1)
    weight_in_grad(m, 1)
    one = core_start(1)
    zero = first(0, zero)
    project_back(m)
    one = first(1, one)
    two = third(2, two)
    taps_back(m)

    small = [push(m.small.at[1 - core], m.small_core, m.small_sems, 0, partner)]
    norm_input_back(m)

    arrive(small)
    m.small_core[...] = m.small_core[...] + m.small[core]
    m.small_y[y] = m.small_core[y]
    small = [push(m.small_core.at[at_y(o)], m.small_y.at[y], m.small_sems, o, peer_y(o)) for o in ring_y]

    untime(m, m.grad_frames)
    zero = second(0, zero)

    arrive(small)
    m.small_d[data] = (m.small_y[0] + m.small_y[1]) + (m.small_y[2] + m.small_y[3])
    small = [push(m.small_d.at[data], m.small_d.at[data], m.small_d_sems, o - 1, peer_d(o)) for o in ring_d]

    arrive(out_copies)

    @pl.loop(0, slots)
    def _(s):
        m.out_frames[s] = m.out_recv[m.source_of[s]]

    last(2, two)
    one = second(1, one)

    arrive(small)
    total = m.small_d[0]
    for d in range(1, n_data):
        total = total + m.small_d[d]
    m.small_all[core, y] = total
    own = m.small_all.at[core, y]
    small = [push(own, own, m.small_sems, RING + o, peer_y(o)) for o in ring_y]

    zero = third(0, zero)
    one = third(1, one)
    arrive(small)
    half = m.small_all.at[core]
    small = [push(half, half, m.small_sems, 2 * RING, partner)]
    last(0, zero)
    last(1, one)

    arrive(small)
    lanes = m.small_all.shape[3]
    taps = m.taps.shape[0]
    for a in range(2):
        for b in range(RING):
            c = pl.ds((a * RING + b) * lanes, lanes)
            m.grad_taps[:, c] = m.small_all[a, b, pl.ds(0, taps), :] * scale
            m.grad_gain[:, c] = m.small_all[a, b, pl.ds(taps, 1), :] * scale
            m.grad_bias[:, c] = m.small_all[a, b, pl.ds(taps + 1, 1), :] * scale
    for copy in pending:
        copy.wait_send()


def module_call(scale, owner, slot, lengths, frames, cotangent, w_in, taps, gain, bias, w_out, n_data):
    slots, count, width = frames.shape
    rows = slots * count
    k = taps.shape[0]
    lines = -(-(k + 2) // 8) * 8
    size, cols = width // 32, width // RING
    lanes = width // 8
    shape = jax.ShapeDtypeStruct
    dma = pltpu.SemaphoreType.DMA
    inputs = dict(
        owner=owner, slot=slot, lengths=lengths,
        x=frames.reshape(rows, width), cot=cotangent, w_in_shard=w_in, taps=taps,
        gain=gain, bias=bias, w_out_shard=w_out)
    outputs = dict(
        out_frames=shape((slots, count, width), BF16),
        grad_frames=shape((slots, count, width), BF16),
        grad_in=shape((width // 8, 2 * width), F32),
        grad_out=shape((width // 8, width), F32),
        grad_taps=shape((k, width), F32),
        grad_gain=shape((1, width), F32),
        grad_bias=shape((1, width), F32))
    tables = dict(place=(n_data,), block_for=(n_data,), source_of=(slots,))
    buffers = dict(
        limit=((slots, LANES), jnp.int32),
        w_in=((width, 2 * width), BF16), w_out=((width, width), BF16),
        xp=((rows, width), BF16), xn=((rows, width), BF16), sig=((rows, width), F32),
        chat=((rows, width), F32), rstd=((rows, LANES), F32), sw=((rows, width), BF16),
        glu=((count + k - 1, slots, width), F32), dconv=((count + k - 1, slots, width), F32),
        spread=((k, slots, width), F32), gm=((rows, width), BF16), da=((rows, 2 * width), BF16),
        dx=((rows, width), BF16), wide=((rows, width), F32), sums=((2, slots, width), F32),
        to_time=((rows, rows), BF16), to_block=((rows, rows), BF16),
        lines=((slots, count, width), BF16), sendb=((n_data, count, width), BF16),
        cot_recv=((n_data, count, width), BF16), out_recv=((n_data, count, width), BF16),
        pieces=((2, 3, RING, n_data, size, cols), BF16),
        core_recv=((3, RING, n_data, size, cols), BF16),
        recv_y=((2, RING - 1, n_data, size, cols), BF16),
        recv_d=((n_data - 1, RING, size, cols), BF16),
        last_d=((2, n_data - 1, size, cols), BF16), last_y=((RING - 1, size, cols), BF16),
        fin=((3, n_data, size, cols), BF16),
        small=((2, RING, lines, lanes), F32), small_core=((RING, lines, lanes), F32),
        small_y=((RING, lines, lanes), F32), small_d=((n_data, lines, lanes), F32),
        small_all=((2, RING, lines, lanes), F32))
    pairs = dict(
        weight_sems=(5, 4), pass_sems=(5, RING), cot_sems=(n_data - 1,), out_sems=(n_data - 1,),
        core_sems=(3,), sum_y_sems=(3, RING - 1), sum_d_sems=(3, n_data - 1), fin_sems=(3, n_data - 1),
        small_sems=(2 * RING + 1,), small_d_sems=(n_data - 1,))
    names = list(inputs) + list(outputs) + list(tables) + list(buffers)
    vmem = pl.BlockSpec(memory_space=pltpu.VMEM)
    smem = pl.BlockSpec(memory_space=pltpu.SMEM)

    def body(*refs):
        plain, sems = refs[: len(names)], refs[len(names) :]
        both = [(sems[2 * i], sems[2 * i + 1]) for i in range(len(pairs))]
        module_kernel(scale, names + list(pairs), *plain, *both)

    return pl.pallas_call(
        body,
        out_shape=tuple(outputs.values()),
        in_specs=[smem] * 3 + [vmem] * (len(inputs) - 3),
        out_specs=(vmem,) * len(outputs),
        scratch_shapes=[pltpu.SMEM(t, jnp.int32) for t in tables.values()]
        + [pltpu.VMEM(*b) for b in buffers.values()]
        + [dma(s) for s in pairs.values() for _ in range(2)],
        compiler_params=pltpu.CompilerParams(
            collective_id=0, has_side_effects=True, vmem_limit_bytes=VMEM_LIMIT),
        name="conv_module",
    )(*inputs.values())


VMEM_LIMIT = 63 * 2**20


def shards(frames, lengths, owner, slot, w_in, kernel, dw_gain, dw_bias, w_out, cotangent):
    n_data = lax.axis_size("dp")
    n_shard = lax.axis_size("fsdp")
    slots, count, width = frames.shape
    scale = 1.0 / math.sqrt(slots * count * n_data * n_shard)
    out_frames, grad_frames, grad_in, grad_out, grad_taps, grad_gain, grad_bias = module_call(
        scale, owner, slot, lengths, frames, cotangent, w_in, kernel, dw_gain[None], dw_bias[None], w_out,
        n_data)
    return (
        out_frames,
        grad_frames,
        grad_in,
        grad_taps,
        grad_gain[0],
        grad_bias[0],
        grad_out,
    )


def solution(mesh):
    placed = (
        P(("dp", "fsdp"), None, None),
        P(),
        P(),
        P(),
        P("fsdp", None),
        P(),
        P(),
        P(),
        P("fsdp", None),
        P(("dp", "fsdp"), None, None),
    )
    return jax.shard_map(
        shards,
        mesh=mesh,
        in_specs=placed,
        out_specs=(
            P(("dp", "fsdp"), None, None),
            P(("dp", "fsdp"), None, None),
            P("fsdp", None),
            P(),
            P(),
            P(),
            P("fsdp", None),
        ),
        check_vma=False,
    )
```

```python
import math
import types

import jax
import jax.numpy as jnp
from jax import lax
from jax.experimental import pallas as pl
from jax.experimental.pallas import tpu as pltpu
from jax.sharding import PartitionSpec as P

MESH = pl.DeviceIdType.MESH

LANES = 128
CHUNK = 16
PIECE = 256
BLOCK = 64
RING = 4
EPS = 1e-05
NT = (((1,), (1,)), ((), ()))
TN = (((0,), (0,)), ((), ()))
BF16 = jnp.bfloat16
F32 = jnp.float32


def lanes_of(i, width=LANES):
    return pl.ds(pl.multiple_of(i * width, width), width)


def statistics(values):
    center = values - jnp.mean(values, axis=-1, keepdims=True)
    rstd = lax.rsqrt(jnp.mean(center * center, axis=-1, keepdims=True) + EPS)
    return center * rstd, rstd


def logistic(v):
    return 1.0 / (1.0 + jnp.exp(-v))


def order_matrix(rows, slots, to_time):
    r = lax.broadcasted_iota(jnp.int32, (rows, rows), 0)
    c = lax.broadcasted_iota(jnp.int32, (rows, rows), 1)
    frames = rows // slots
    if to_time:
        place = (r % slots) * frames + r // slots
    else:
        place = (r % frames) * slots + r // frames
    return jnp.where(c == place, 1.0, 0.0).astype(BF16)


def prepare(m):
    m.small[...] = jnp.zeros_like(m.small)
    taps, slots, width = m.spread.shape
    half = (taps - 1) // 2
    frames = m.glu.shape[0] - 2 * half
    for k in range(taps):
        m.spread[k] = jnp.broadcast_to(m.taps[k : k + 1, :], (slots, width))
    m.to_time[...] = order_matrix(m.xn.shape[0], slots, True)
    m.to_block[...] = order_matrix(m.xn.shape[0], slots, False)
    edge = jnp.zeros((half, slots, width), F32)
    for ref in (m.glu, m.dconv):
        ref[pl.ds(0, half)] = edge
        ref[pl.ds(half + frames, half)] = edge


def norm_input(m):
    rows, width = m.xp.shape

    @pl.loop(0, width // PIECE)
    def _(j):
        c = lanes_of(j, PIECE)
        m.xp[:, c] = jnp.dot(m.to_time[...], m.x[:, c], preferred_element_type=F32).astype(BF16)

    @pl.loop(0, rows // BLOCK)
    def _(i):
        r = pl.ds(pl.multiple_of(i * BLOCK, BLOCK), BLOCK)
        m.xn[r, :] = statistics(m.xp[r, :].astype(F32))[0].astype(BF16)


def gate_chunk(m, j):
    rows, width = m.xn.shape
    slots = m.limit.shape[0]
    frames = rows // slots
    half = (m.spread.shape[0] - 1) // 2
    c = pl.ds(j * PIECE, PIECE)
    left = jnp.dot(m.xn[...], m.w_in[:, pl.ds(2 * j * PIECE, PIECE)], preferred_element_type=F32)
    gate = jnp.dot(m.xn[...], m.w_in[:, pl.ds((2 * j + 1) * PIECE, PIECE)], preferred_element_type=F32)
    sig = logistic(gate)
    m.sig[:, c] = sig
    time = lax.broadcasted_iota(jnp.int32, (frames, slots, PIECE), 0)
    limit = jnp.concatenate([m.limit[...]] * (PIECE // LANES), axis=1)
    glu = (left * sig).reshape(frames, slots, PIECE)
    m.glu[pl.ds(half, frames), :, c] = jnp.where(time < limit[None], glu, 0.0)


def slide(padded, spread, start, lanes, flip):
    taps = spread.shape[0]
    acc = None
    for k in range(taps):
        weight = spread[taps - 1 - k if flip else k, :, lanes]
        term = weight[None] * padded[pl.ds(start + k, CHUNK), :, lanes]
        acc = term if acc is None else acc + term
    return acc


def conv_chunk(m, j):
    rows, width = m.xn.shape
    slots = m.limit.shape[0]
    steps = rows // slots // CHUNK

    @pl.loop(0, PIECE // LANES * steps)
    def _(i):
        c = lanes_of(j * (PIECE // LANES) + i // steps)
        t = i % steps
        acc = slide(m.glu, m.spread, t * CHUNK, c, False)
        r = pl.ds(pl.multiple_of(t * CHUNK * slots, CHUNK * slots), CHUNK * slots)
        m.chat[r, c] = acc.reshape(CHUNK * slots, LANES)


def norm_conv(m):
    rows, width = m.xn.shape

    @pl.loop(0, rows // BLOCK)
    def _(i):
        r = pl.ds(pl.multiple_of(i * BLOCK, BLOCK), BLOCK)
        chat, rstd = statistics(m.chat[r, :])
        m.chat[r, :] = chat
        m.rstd[r, :] = jnp.broadcast_to(rstd, (BLOCK, LANES))
        z = chat * m.gain[...] + m.bias[...]
        m.sw[r, :] = (z * logistic(z)).astype(BF16)


def mix_out(m):
    rows, width = m.xn.shape
    slots = m.limit.shape[0]
    frames = rows // slots

    @pl.loop(0, width // PIECE)
    def _(j):
        c = lanes_of(j, PIECE)
        mixed = jnp.dot(m.sw[...], m.w_out[:, c], preferred_element_type=F32)
        time = lax.broadcasted_iota(jnp.int32, (frames, slots, PIECE), 0)
        limit = jnp.concatenate([m.limit[...]] * (PIECE // LANES), axis=1)
        out = (m.xp[:, c].astype(F32) + mixed).reshape(frames, slots, PIECE)
        m.dx[:, c] = jnp.where(time < limit[None], out, 0.0).reshape(rows, PIECE).astype(BF16)


def untime(m, dst):
    slots, frames, width = dst.shape

    @pl.loop(0, width // PIECE)
    def _(j):
        c = lanes_of(j, PIECE)
        line = jnp.dot(m.to_block[...], m.dx[:, c], preferred_element_type=F32).astype(BF16)
        for b in range(slots):
            dst[b, :, c] = line[b * frames : (b + 1) * frames, :]


def mask_cotangent(m):
    rows, width = m.xn.shape
    slots = m.limit.shape[0]
    frames = rows // slots

    @pl.loop(0, width // PIECE)
    def _(j):
        c = lanes_of(j, PIECE)
        g = jnp.dot(m.to_time[...], m.dx[:, c], preferred_element_type=F32)
        time = lax.broadcasted_iota(jnp.int32, (frames, slots, PIECE), 0)
        limit = jnp.concatenate([m.limit[...]] * (PIECE // LANES), axis=1)
        g = jnp.where(time < limit[None], g.reshape(frames, slots, PIECE), 0.0)
        m.gm[:, c] = g.reshape(rows, PIECE).astype(BF16)


def norm_conv_back(m):
    rows, width = m.xn.shape
    taps, slots, _ = m.spread.shape
    half = (taps - 1) // 2
    steps = BLOCK // slots
    m.sums[...] = jnp.zeros_like(m.sums)

    @pl.loop(0, width // PIECE)
    def _(j):
        c = lanes_of(j, PIECE)
        m.wide[:, c] = lax.dot_general(m.gm[...], m.w_out[c, :], NT, preferred_element_type=F32)

    @pl.loop(0, rows // BLOCK)
    def _(i):
        r = pl.ds(pl.multiple_of(i * BLOCK, BLOCK), BLOCK)
        ds = m.wide[r, :]
        chat = m.chat[r, :]
        gain = m.gain[...]
        z = chat * gain + m.bias[...]
        sigz = logistic(z)
        dz = ds * sigz * (1.0 + z * (1.0 - sigz))
        m.sums[0] += jnp.sum((dz * chat).reshape(steps, slots, width), axis=0)
        m.sums[1] += jnp.sum(dz.reshape(steps, slots, width), axis=0)
        dchat = dz * gain
        m1 = jnp.mean(dchat, axis=-1, keepdims=True)
        m2 = jnp.mean(dchat * chat, axis=-1, keepdims=True)
        dconv = m.rstd[r, :][:, :1] * (dchat - m1 - chat * m2)
        m.dconv[pl.ds(half + i * steps, steps)] = dconv.reshape(steps, slots, width)


def conv_back(m, side):
    rows, width = m.xn.shape
    taps, slots, _ = m.spread.shape
    frames = rows // slots
    half = (taps - 1) // 2
    steps = frames // CHUNK
    tiles = width // LANES // 2

    @pl.loop(0, tiles * steps)
    def _(i):
        l = side * tiles + i // steps
        t = i % steps
        c = lanes_of(l)
        acc = slide(m.dconv, m.spread, t * CHUNK, c, True)
        r = pl.ds(pl.multiple_of(t * CHUNK * slots, CHUNK * slots), CHUNK * slots)
        near = lax.broadcasted_iota(jnp.int32, (CHUNK, slots, LANES), 0) + t * CHUNK
        dglu = jnp.where(near < m.limit[...][None], acc, 0.0).reshape(CHUNK * slots, LANES)
        sig = m.sig[r, c]
        glu = m.glu[pl.ds(half + t * CHUNK, CHUNK), :, c].reshape(CHUNK * slots, LANES)
        place = (l // 2) * 4 + l % 2
        m.da[r, lanes_of(place)] = (dglu * sig).astype(BF16)
        m.da[r, lanes_of(place + 2)] = (dglu * glu * (1.0 - sig)).astype(BF16)


def taps_back(m):
    rows, width = m.xn.shape
    taps, slots, _ = m.spread.shape
    frames = rows // slots
    half = (taps - 1) // 2
    lanes_q = width // 8 // LANES
    step = 8

    @pl.loop(0, width // LANES)
    def _(l):
        c = lanes_of(l)
        for low in range(0, taps, 16):
            count = min(16, taps - low)

            def body(t, acc, low=low, count=count):
                base = t * step
                out = []
                d = m.dconv[pl.ds(half + base, step), :, c]
                for k in range(count):
                    row = m.glu[pl.ds(base + low + k, step), :, c]
                    out.append(acc[k] + jnp.sum(d * row, axis=0))
                return tuple(out)

            acc = lax.fori_loop(0, frames // step, body,
                                tuple(jnp.zeros((slots, LANES), F32) for _ in range(count)))
            for k in range(count):
                m.small[l // 4, l % 4, pl.ds(low + k, 1), :] = jnp.sum(acc[k], axis=0, keepdims=True)
        for k in range(2):
            m.small[l // 4, l % 4, pl.ds(taps + k, 1), :] = jnp.sum(m.sums[k, :, c], axis=0, keepdims=True)


def project_back(m):
    width = m.xn.shape[1]

    @pl.loop(0, width // PIECE)
    def _(j):
        c = lanes_of(j, PIECE)
        m.wide[:, c] = lax.dot_general(m.da[...], m.w_in[c, :], NT, preferred_element_type=F32)


def norm_input_back(m):
    rows, width = m.xn.shape

    @pl.loop(0, rows // BLOCK)
    def _(i):
        r = pl.ds(pl.multiple_of(i * BLOCK, BLOCK), BLOCK)
        dxn = m.wide[r, :]
        xhat, rstd = statistics(m.xp[r, :].astype(F32))
        m1 = jnp.mean(dxn, axis=-1, keepdims=True)
        m2 = jnp.mean(dxn * xhat, axis=-1, keepdims=True)
        dx = rstd * (dxn - m1 - xhat * m2) + m.gm[r, :].astype(F32)
        m.dx[r, :] = dx.astype(BF16)


def save_pieces(m, y, k, b, part):
    size = m.pieces.shape[4]
    for core in range(2):
        for a in range(RING):
            low = (core * RING + a) * size
            m.pieces[core, k, y, a * RING + b] = part[low : low + size, :]


def weight_in_grad(m, side):
    @pl.loop(0, RING)
    def _(y):
        xn = m.xn[:, lanes_of(y, PIECE)]
        for b in range(RING):
            cols = m.da[:, pl.ds((side * RING + b) * PIECE, PIECE)]
            part = lax.dot_general(xn, cols, TN, preferred_element_type=F32)
            save_pieces(m, y, side, b, part.astype(BF16))


def weight_out_grad(m):
    @pl.loop(0, RING)
    def _(y):
        sw = m.sw[:, lanes_of(y, PIECE)]
        for b in range(RING):
            part = lax.dot_general(sw, m.gm[:, pl.ds(b * PIECE, PIECE)], TN, preferred_element_type=F32)
            save_pieces(m, y, 2, b, part.astype(BF16))


def module_kernel(scale, names, *refs):
    m = types.SimpleNamespace(**dict(zip(names, refs)))
    data = lax.axis_index("dp")
    shard = lax.axis_index("fsdp")
    y, core = shard // 2, shard % 2
    n_data = m.sendb.shape[0]
    slots, frames, width = m.cot.shape
    rows = slots * frames
    per = m.w_in_shard.shape[0]
    ring_y = range(1, RING)
    ring_d = range(1, n_data)

    def at_y(offset):
        return lax.rem(y + offset, RING)

    def at_d(offset):
        return lax.rem(data + offset, n_data)

    partner = (data, y * 2 + (1 - core))

    def peer_y(offset):
        return (data, at_y(offset) * 2 + core)

    def peer_d(offset):
        return (at_d(offset), shard)

    barrier = pltpu.get_barrier_semaphore()
    pl.semaphore_signal(barrier, inc=1, device_id=partner, device_id_type=MESH)
    for o in ring_y:
        pl.semaphore_signal(barrier, inc=1, device_id=peer_y(o), device_id_type=MESH)
    for o in ring_d:
        pl.semaphore_signal(barrier, inc=1, device_id=peer_d(o), device_id_type=MESH)

    pending = []

    def push(src, dst, sems, place, device, keep=True):
        copy = pltpu.make_async_remote_copy(
            src_ref=src, dst_ref=dst, send_sem=sems[0].at[place], recv_sem=sems[1].at[place],
            device_id=device, device_id_type=MESH)
        copy.start()
        if keep:
            pending.append(copy)
        return copy

    def arrive(copies):
        for copy in copies:
            copy.wait_recv()

    def wide(a):
        return a.astype(F32)

    mine = pl.ds(pl.multiple_of(shard * per, per), per)
    chunks = width // PIECE
    for j in range(chunks):
        m.w_in[mine, pl.ds(2 * j * PIECE, PIECE)] = m.w_in_shard[:, pl.ds(j * PIECE, PIECE)]
        m.w_in[mine, pl.ds((2 * j + 1) * PIECE, PIECE)] = m.w_in_shard[:, pl.ds(width + j * PIECE, PIECE)]
    m.w_out[mine, :] = m.w_out_shard[...]

    n_shard = 2 * RING

    def base(p):
        return (p * n_shard + shard) * slots

    @pl.loop(0, n_data)
    def _(p):
        found, place, out_block = 0, 0, 0
        for j in range(slots):
            hit = m.owner[base(p) + j] == data
            found = found + jnp.where(hit, 1, 0)
            place = place + jnp.where(hit, m.slot[base(p) + j], 0)
            out_block = out_block + jnp.where(m.owner[base(data) + j] == p, j, 0)
        m.place[p] = place - slots * (1 - found)
        m.block_for[p] = jnp.minimum(out_block, slots - 1)
        m.sendb[p] = m.cot[jnp.minimum(place, slots - 1)]

    pl.semaphore_wait(barrier, 1 + len(ring_y) + len(ring_d))

    def part(j, owner_y):
        r = pl.ds(pl.multiple_of((owner_y * 2 + core) * per, per), per)
        if j < chunks:
            return m.w_in.at[r, pl.ds(2 * j * PIECE, 2 * PIECE)]
        return m.w_out.at[r, :]

    weights, passed = [], []
    right, left = 1, RING - 1

    def send_weights(j):
        src = part(j, y)
        weights.append([push(src, src, m.weight_sems, (j, i), peer_y(o)) for i, o in enumerate((right, left))])
        passed.append([push(src, src, m.pass_sems, (j, 0), partner)])

    ahead = 3
    for j in range(ahead):
        send_weights(j)

    def exchange(dst, sems):
        copies = [push(m.sendb.at[at_d(o)], dst.at[data], sems, o - 1, peer_d(o), False) for o in ring_d]
        dst[data] = m.sendb[data]
        return copies

    cot_copies = exchange(m.cot_recv, m.cot_sems)

    for b in range(slots):
        m.limit[pl.ds(b, 1), :] = jnp.full((1, LANES), m.lengths[base(data) + b], jnp.int32)
    prepare(m)
    norm_input(m)

    @pl.loop(0, slots)
    def _(s):
        source = 0
        for p in range(n_data):
            source = source + jnp.where(m.place[p] == s, p, 0)
        m.source_of[s] = jnp.minimum(source, n_data - 1)

    def weights_near(j):
        for i, (far, near) in enumerate(((left, right), (right, left))):
            weights[j][i].wait_recv()
            src = part(j, at_y(far))
            piece = src.at[pl.ds(i * (per // 2), per // 2), :]
            weights[j].append(push(piece, piece, m.weight_sems, (j, 2 + i), peer_y(near)))
            passed[j].append(push(src, src, m.pass_sems, (j, 1 + i), partner))
        if j + ahead <= chunks:
            send_weights(j + ahead)

    def weights_far(j):
        arrive(weights[j][2:])
        src = part(j, at_y(2))
        passed[j].append(push(src, src, m.pass_sems, (j, 3), partner))
        arrive(passed[j])

    weights_near(0)
    for j in range(chunks):
        weights_near(j + 1)
        weights_far(j)
        gate_chunk(m, j)
        conv_chunk(m, j)
    norm_conv(m)

    arrive(cot_copies)
    for b in range(slots):
        m.dx[pl.ds(b * frames, frames), :] = m.cot_recv[m.owner[base(data) + b]]
    mask_cotangent(m)

    weights_far(chunks)
    mix_out(m)
    untime(m, m.lines)
    for copy in cot_copies:
        copy.wait_send()

    @pl.loop(0, n_data)
    def _(p):
        m.sendb[p] = m.lines[m.block_for[p]]

    out_copies = exchange(m.out_recv, m.out_sems)
    pending.extend(out_copies)

    def core_start(k):
        return [push(m.pieces.at[1 - core, k], m.core_recv.at[k], m.core_sems, k, partner)]

    def first(k, copies):
        arrive(copies)

        @pl.loop(0, RING)
        def _(a):
            m.pieces[core, k, a] = (wide(m.pieces[core, k, a]) + wide(m.core_recv[k, a])).astype(BF16)

        return [push(m.pieces.at[core, k, at_y(o)], m.recv_y.at[k, o - 1], m.sum_y_sems,
                     (k, o - 1), peer_y(o)) for o in ring_y]

    def second(k, copies):
        arrive(copies)

        @pl.loop(0, n_data)
        def _(d):
            acc = wide(m.pieces[core, k, y, d])
            for o in ring_y:
                acc = acc + wide(m.recv_y[k, o - 1, d])
            m.pieces[core, k, y, d] = acc.astype(BF16)

        return [push(m.pieces.at[core, k, y, at_d(o)], m.last_d.at[k, o - 1], m.sum_d_sems,
                     (k, o - 1), peer_d(o)) for o in ring_d]

    def third(k, copies):
        arrive(copies)
        acc = wide(m.pieces[core, k, y, data])
        for o in ring_d:
            acc = acc + wide(m.last_d[k, o - 1])
        m.fin[k, data] = acc.astype(BF16)
        return [push(m.fin.at[k, data], m.fin.at[k, data], m.fin_sems, (k, o - 1), peer_d(o)) for o in ring_d]

    def last(k, copies):
        arrive(copies)
        size, cols = m.fin.shape[2], m.fin.shape[3]
        for a in range(RING):
            for b in range(RING):
                piece = wide(m.fin[k, a * RING + b]) * scale
                r = pl.ds(a * size, size)
                if k < 2:
                    m.grad_in[r, pl.ds((b % 2 * RING + k * 2 + b // 2) * cols, cols)] = piece
                else:
                    m.grad_out[r, pl.ds(b * cols, cols)] = piece

    weight_out_grad(m)
    two = core_start(2)
    norm_conv_back(m)
    two = first(2, two)
    conv_back(m, 0)
    weight_in_grad(m, 0)
    zero = core_start(0)
    two = second(2, two)
    conv_back(m, 1)
    weight_in_grad(m, 1)
    one = core_start(1)
    zero = first(0, zero)
    project_back(m)
    one = first(1, one)
    two = third(2, two)
    taps_back(m)

    small = [push(m.small.at[1 - core], m.small_core, m.small_sems, 0, partner)]
    norm_input_back(m)

    arrive(small)
    m.small_core[...] = m.small_core[...] + m.small[core]
    m.small_y[y] = m.small_core[y]
    small = [push(m.small_core.at[at_y(o)], m.small_y.at[y], m.small_sems, o, peer_y(o)) for o in ring_y]

    untime(m, m.grad_frames)
    zero = second(0, zero)

    arrive(small)
    m.small_d[data] = (m.small_y[0] + m.small_y[1]) + (m.small_y[2] + m.small_y[3])
    small = [push(m.small_d.at[data], m.small_d.at[data], m.small_d_sems, o - 1, peer_d(o)) for o in ring_d]

    arrive(out_copies)

    @pl.loop(0, slots)
    def _(s):
        m.out_frames[s] = m.out_recv[m.source_of[s]]

    last(2, two)
    one = second(1, one)

    arrive(small)
    total = m.small_d[0]
    for d in range(1, n_data):
        total = total + m.small_d[d]
    m.small_all[core, y] = total
    own = m.small_all.at[core, y]
    small = [push(own, own, m.small_sems, RING + o, peer_y(o)) for o in ring_y]

    zero = third(0, zero)
    one = third(1, one)
    arrive(small)
    half = m.small_all.at[core]
    small = [push(half, half, m.small_sems, 2 * RING, partner)]
    last(0, zero)
    last(1, one)

    arrive(small)
    lanes = m.small_all.shape[3]
    taps = m.taps.shape[0]
    for a in range(2):
        for b in range(RING):
            c = pl.ds((a * RING + b) * lanes, lanes)
            m.grad_taps[:, c] = m.small_all[a, b, pl.ds(0, taps), :] * scale
            m.grad_gain[:, c] = m.small_all[a, b, pl.ds(taps, 1), :] * scale
            m.grad_bias[:, c] = m.small_all[a, b, pl.ds(taps + 1, 1), :] * scale
    for copy in pending:
        copy.wait_send()


def module_call(scale, owner, slot, lengths, frames, cotangent, w_in, taps, gain, bias, w_out, n_data):
    slots, count, width = frames.shape
    rows = slots * count
    k = taps.shape[0]
    lines = -(-(k + 2) // 8) * 8
    size, cols = width // 32, width // RING
    lanes = width // 8
    shape = jax.ShapeDtypeStruct
    dma = pltpu.SemaphoreType.DMA
    inputs = dict(
        owner=owner, slot=slot, lengths=lengths,
        x=frames.reshape(rows, width), cot=cotangent, w_in_shard=w_in, taps=taps,
        gain=gain, bias=bias, w_out_shard=w_out)
    outputs = dict(
        out_frames=shape((slots, count, width), BF16),
        grad_frames=shape((slots, count, width), BF16),
        grad_in=shape((width // 8, 2 * width), F32),
        grad_out=shape((width // 8, width), F32),
        grad_taps=shape((k, width), F32),
        grad_gain=shape((1, width), F32),
        grad_bias=shape((1, width), F32))
    tables = dict(place=(n_data,), block_for=(n_data,), source_of=(slots,))
    buffers = dict(
        limit=((slots, LANES), jnp.int32),
        w_in=((width, 2 * width), BF16), w_out=((width, width), BF16),
        xp=((rows, width), BF16), xn=((rows, width), BF16), sig=((rows, width), F32),
        chat=((rows, width), F32), rstd=((rows, LANES), F32), sw=((rows, width), BF16),
        glu=((count + k - 1, slots, width), F32), dconv=((count + k - 1, slots, width), F32),
        spread=((k, slots, width), F32), gm=((rows, width), BF16), da=((rows, 2 * width), BF16),
        dx=((rows, width), BF16), wide=((rows, width), F32), sums=((2, slots, width), F32),
        to_time=((rows, rows), BF16), to_block=((rows, rows), BF16),
        lines=((slots, count, width), BF16), sendb=((n_data, count, width), BF16),
        cot_recv=((n_data, count, width), BF16), out_recv=((n_data, count, width), BF16),
        pieces=((2, 3, RING, n_data, size, cols), BF16),
        core_recv=((3, RING, n_data, size, cols), BF16),
        recv_y=((3, RING - 1, n_data, size, cols), BF16),
        last_d=((3, n_data - 1, size, cols), BF16),
        fin=((3, n_data, size, cols), BF16),
        small=((2, RING, lines, lanes), F32), small_core=((RING, lines, lanes), F32),
        small_y=((RING, lines, lanes), F32), small_d=((n_data, lines, lanes), F32),
        small_all=((2, RING, lines, lanes), F32))
    pairs = dict(
        weight_sems=(5, 4), pass_sems=(5, RING), cot_sems=(n_data - 1,), out_sems=(n_data - 1,),
        core_sems=(3,), sum_y_sems=(3, RING - 1), sum_d_sems=(3, n_data - 1), fin_sems=(3, n_data - 1),
        small_sems=(2 * RING + 1,), small_d_sems=(n_data - 1,))
    names = list(inputs) + list(outputs) + list(tables) + list(buffers)
    vmem = pl.BlockSpec(memory_space=pltpu.VMEM)
    smem = pl.BlockSpec(memory_space=pltpu.SMEM)

    def body(*refs):
        plain, sems = refs[: len(names)], refs[len(names) :]
        both = [(sems[2 * i], sems[2 * i + 1]) for i in range(len(pairs))]
        module_kernel(scale, names + list(pairs), *plain, *both)

    return pl.pallas_call(
        body,
        out_shape=tuple(outputs.values()),
        in_specs=[smem] * 3 + [vmem] * (len(inputs) - 3),
        out_specs=(vmem,) * len(outputs),
        scratch_shapes=[pltpu.SMEM(t, jnp.int32) for t in tables.values()]
        + [pltpu.VMEM(*b) for b in buffers.values()]
        + [dma(s) for s in pairs.values() for _ in range(2)],
        compiler_params=pltpu.CompilerParams(
            collective_id=0, has_side_effects=True, vmem_limit_bytes=VMEM_LIMIT),
        name="conv_module",
    )(*inputs.values())


VMEM_LIMIT = 63 * 2**20


def finish_kernel(*refs):
    count = len(refs) // 4
    plain, sems = refs[: 3 * count], refs[3 * count :]
    loads, stores = [], []
    for i in range(count):
        loads.append(pltpu.make_async_copy(plain[i], plain[2 * count + i], sems[i].at[0]))
        loads[-1].start()
    for i in range(count):
        loads[i].wait()
        stores.append(pltpu.make_async_copy(plain[2 * count + i], plain[count + i], sems[i].at[1]))
        stores[-1].start()
    for copy in stores:
        copy.wait()


def finish(arrays):
    hbm = pl.BlockSpec(memory_space=pl.ANY)
    return pl.pallas_call(
        finish_kernel,
        out_shape=tuple(jax.ShapeDtypeStruct(a.shape, a.dtype) for a in arrays),
        in_specs=[hbm] * len(arrays),
        out_specs=(hbm,) * len(arrays),
        scratch_shapes=[pltpu.VMEM(a.shape, a.dtype) for a in arrays]
        + [pltpu.SemaphoreType.DMA((2,)) for _ in arrays],
        compiler_params=pltpu.CompilerParams(vmem_limit_bytes=VMEM_LIMIT),
        name="finish",
    )(*arrays)


def shards(frames, lengths, owner, slot, w_in, kernel, dw_gain, dw_bias, w_out, cotangent):
    n_data = lax.axis_size("dp")
    n_shard = lax.axis_size("fsdp")
    slots, count, width = frames.shape
    scale = 1.0 / math.sqrt(slots * count * n_data * n_shard)
    results = module_call(
        scale, owner, slot, lengths, frames, cotangent, w_in, kernel, dw_gain[None], dw_bias[None], w_out,
        n_data)
    out_frames, grad_frames, grad_in, grad_out, grad_taps, grad_gain, grad_bias = finish(results)
    return (
        out_frames,
        grad_frames,
        grad_in,
        grad_taps,
        grad_gain[0],
        grad_bias[0],
        grad_out,
    )


def solution(mesh):
    placed = (
        P(("dp", "fsdp"), None, None),
        P(),
        P(),
        P(),
        P("fsdp", None),
        P(),
        P(),
        P(),
        P("fsdp", None),
        P(("dp", "fsdp"), None, None),
    )
    return jax.shard_map(
        shards,
        mesh=mesh,
        in_specs=placed,
        out_specs=(
            P(("dp", "fsdp"), None, None),
            P(("dp", "fsdp"), None, None),
            P("fsdp", None),
            P(),
            P(),
            P(),
            P("fsdp", None),
        ),
        check_vma=False,
    )
```

```python
import math
import types

import jax
import jax.numpy as jnp
from jax import lax
from jax.experimental import pallas as pl
from jax.experimental.pallas import tpu as pltpu
from jax.sharding import PartitionSpec as P

MESH = pl.DeviceIdType.MESH

LANES = 128
CHUNK = 16
PIECE = 256
BLOCK = 64
RING = 4
EPS = 1e-05
NT = (((1,), (1,)), ((), ()))
TN = (((0,), (0,)), ((), ()))
BF16 = jnp.bfloat16
F32 = jnp.float32


def lanes_of(i, width=LANES):
    return pl.ds(pl.multiple_of(i * width, width), width)


def statistics(values):
    center = values - jnp.mean(values, axis=-1, keepdims=True)
    rstd = lax.rsqrt(jnp.mean(center * center, axis=-1, keepdims=True) + EPS)
    return center * rstd, rstd


def logistic(v):
    return 1.0 / (1.0 + jnp.exp(-v))


def order_matrix(rows, slots, to_time):
    r = lax.broadcasted_iota(jnp.int32, (rows, rows), 0)
    c = lax.broadcasted_iota(jnp.int32, (rows, rows), 1)
    frames = rows // slots
    if to_time:
        place = (r % slots) * frames + r // slots
    else:
        place = (r % frames) * slots + r // frames
    return jnp.where(c == place, 1.0, 0.0).astype(BF16)


def prepare(m):
    m.small[...] = jnp.zeros_like(m.small)
    taps, slots, width = m.spread.shape
    half = (taps - 1) // 2
    frames = m.glu.shape[0] - 2 * half
    for k in range(taps):
        m.spread[k] = jnp.broadcast_to(m.taps[k : k + 1, :], (slots, width))
    m.to_time[...] = order_matrix(m.xn.shape[0], slots, True)
    m.to_block[...] = order_matrix(m.xn.shape[0], slots, False)
    edge = jnp.zeros((half, slots, width), F32)
    for ref in (m.glu, m.dconv):
        ref[pl.ds(0, half)] = edge
        ref[pl.ds(half + frames, half)] = edge


def norm_input(m):
    rows, width = m.xp.shape

    @pl.loop(0, width // PIECE)
    def _(j):
        c = lanes_of(j, PIECE)
        m.xp[:, c] = jnp.dot(m.to_time[...], m.x[:, c], preferred_element_type=F32).astype(BF16)

    @pl.loop(0, rows // BLOCK)
    def _(i):
        r = pl.ds(pl.multiple_of(i * BLOCK, BLOCK), BLOCK)
        m.xn[r, :] = statistics(m.xp[r, :].astype(F32))[0].astype(BF16)


def gate_chunk(m, j):
    rows, width = m.xn.shape
    slots = m.limit.shape[0]
    frames = rows // slots
    half = (m.spread.shape[0] - 1) // 2
    c = pl.ds(j * PIECE, PIECE)
    left = jnp.dot(m.xn[...], m.w_in[:, pl.ds(2 * j * PIECE, PIECE)], preferred_element_type=F32)
    gate = jnp.dot(m.xn[...], m.w_in[:, pl.ds((2 * j + 1) * PIECE, PIECE)], preferred_element_type=F32)
    sig = logistic(gate)
    m.sig[:, c] = sig
    time = lax.broadcasted_iota(jnp.int32, (frames, slots, PIECE), 0)
    limit = jnp.concatenate([m.limit[...]] * (PIECE // LANES), axis=1)
    glu = (left * sig).reshape(frames, slots, PIECE)
    m.glu[pl.ds(half, frames), :, c] = jnp.where(time < limit[None], glu, 0.0)


def slide(padded, spread, start, lanes, flip):
    taps = spread.shape[0]
    acc = None
    for k in range(taps):
        weight = spread[taps - 1 - k if flip else k, :, lanes]
        term = weight[None] * padded[pl.ds(start + k, CHUNK), :, lanes]
        acc = term if acc is None else acc + term
    return acc


def conv_chunk(m, j):
    rows, width = m.xn.shape
    slots = m.limit.shape[0]
    steps = rows // slots // CHUNK

    @pl.loop(0, PIECE // LANES * steps)
    def _(i):
        c = lanes_of(j * (PIECE // LANES) + i // steps)
        t = i % steps
        acc = slide(m.glu, m.spread, t * CHUNK, c, False)
        r = pl.ds(pl.multiple_of(t * CHUNK * slots, CHUNK * slots), CHUNK * slots)
        m.chat[r, c] = acc.reshape(CHUNK * slots, LANES)


def norm_conv(m):
    rows, width = m.xn.shape

    @pl.loop(0, rows // BLOCK)
    def _(i):
        r = pl.ds(pl.multiple_of(i * BLOCK, BLOCK), BLOCK)
        chat, rstd = statistics(m.chat[r, :])
        m.chat[r, :] = chat
        m.rstd[r, :] = jnp.broadcast_to(rstd, (BLOCK, LANES))
        z = chat * m.gain[...] + m.bias[...]
        m.sw[r, :] = (z * logistic(z)).astype(BF16)


def mix_out(m):
    rows, width = m.xn.shape
    slots = m.limit.shape[0]
    frames = rows // slots

    @pl.loop(0, width // PIECE)
    def _(j):
        c = lanes_of(j, PIECE)
        mixed = jnp.dot(m.sw[...], m.w_out[:, c], preferred_element_type=F32)
        time = lax.broadcasted_iota(jnp.int32, (frames, slots, PIECE), 0)
        limit = jnp.concatenate([m.limit[...]] * (PIECE // LANES), axis=1)
        out = (m.xp[:, c].astype(F32) + mixed).reshape(frames, slots, PIECE)
        m.dx[:, c] = jnp.where(time < limit[None], out, 0.0).reshape(rows, PIECE).astype(BF16)


def untime(m, dst):
    slots, frames, width = dst.shape

    @pl.loop(0, width // PIECE)
    def _(j):
        c = lanes_of(j, PIECE)
        line = jnp.dot(m.to_block[...], m.dx[:, c], preferred_element_type=F32).astype(BF16)
        for b in range(slots):
            dst[b, :, c] = line[b * frames : (b + 1) * frames, :]


def mask_cotangent(m):
    rows, width = m.xn.shape
    slots = m.limit.shape[0]
    frames = rows // slots

    @pl.loop(0, width // PIECE)
    def _(j):
        c = lanes_of(j, PIECE)
        g = jnp.dot(m.to_time[...], m.dx[:, c], preferred_element_type=F32)
        time = lax.broadcasted_iota(jnp.int32, (frames, slots, PIECE), 0)
        limit = jnp.concatenate([m.limit[...]] * (PIECE // LANES), axis=1)
        g = jnp.where(time < limit[None], g.reshape(frames, slots, PIECE), 0.0)
        m.gm[:, c] = g.reshape(rows, PIECE).astype(BF16)


def norm_conv_back(m):
    rows, width = m.xn.shape
    taps, slots, _ = m.spread.shape
    half = (taps - 1) // 2
    steps = BLOCK // slots
    m.sums[...] = jnp.zeros_like(m.sums)

    @pl.loop(0, width // PIECE)
    def _(j):
        c = lanes_of(j, PIECE)
        m.wide[:, c] = lax.dot_general(m.gm[...], m.w_out[c, :], NT, preferred_element_type=F32)

    @pl.loop(0, rows // BLOCK)
    def _(i):
        r = pl.ds(pl.multiple_of(i * BLOCK, BLOCK), BLOCK)
        ds = m.wide[r, :]
        chat = m.chat[r, :]
        gain = m.gain[...]
        z = chat * gain + m.bias[...]
        sigz = logistic(z)
        dz = ds * sigz * (1.0 + z * (1.0 - sigz))
        m.sums[0] += jnp.sum((dz * chat).reshape(steps, slots, width), axis=0)
        m.sums[1] += jnp.sum(dz.reshape(steps, slots, width), axis=0)
        dchat = dz * gain
        m1 = jnp.mean(dchat, axis=-1, keepdims=True)
        m2 = jnp.mean(dchat * chat, axis=-1, keepdims=True)
        dconv = m.rstd[r, :][:, :1] * (dchat - m1 - chat * m2)
        m.dconv[pl.ds(half + i * steps, steps)] = dconv.reshape(steps, slots, width)


def conv_back(m, side):
    rows, width = m.xn.shape
    taps, slots, _ = m.spread.shape
    frames = rows // slots
    half = (taps - 1) // 2
    steps = frames // CHUNK
    tiles = width // LANES // 2

    @pl.loop(0, tiles * steps)
    def _(i):
        l = side * tiles + i // steps
        t = i % steps
        c = lanes_of(l)
        acc = slide(m.dconv, m.spread, t * CHUNK, c, True)
        r = pl.ds(pl.multiple_of(t * CHUNK * slots, CHUNK * slots), CHUNK * slots)
        near = lax.broadcasted_iota(jnp.int32, (CHUNK, slots, LANES), 0) + t * CHUNK
        dglu = jnp.where(near < m.limit[...][None], acc, 0.0).reshape(CHUNK * slots, LANES)
        sig = m.sig[r, c]
        glu = m.glu[pl.ds(half + t * CHUNK, CHUNK), :, c].reshape(CHUNK * slots, LANES)
        place = (l // 2) * 4 + l % 2
        m.da[r, lanes_of(place)] = (dglu * sig).astype(BF16)
        m.da[r, lanes_of(place + 2)] = (dglu * glu * (1.0 - sig)).astype(BF16)


def taps_back(m):
    rows, width = m.xn.shape
    taps, slots, _ = m.spread.shape
    frames = rows // slots
    half = (taps - 1) // 2
    lanes_q = width // 8 // LANES
    step = 8

    @pl.loop(0, width // LANES)
    def _(l):
        c = lanes_of(l)
        for low in range(0, taps, 16):
            count = min(16, taps - low)

            def body(t, acc, low=low, count=count):
                base = t * step
                out = []
                d = m.dconv[pl.ds(half + base, step), :, c]
                for k in range(count):
                    row = m.glu[pl.ds(base + low + k, step), :, c]
                    out.append(acc[k] + jnp.sum(d * row, axis=0))
                return tuple(out)

            acc = lax.fori_loop(0, frames // step, body,
                                tuple(jnp.zeros((slots, LANES), F32) for _ in range(count)))
            for k in range(count):
                m.small[l // 4, l % 4, pl.ds(low + k, 1), :] = jnp.sum(acc[k], axis=0, keepdims=True)
        for k in range(2):
            m.small[l // 4, l % 4, pl.ds(taps + k, 1), :] = jnp.sum(m.sums[k, :, c], axis=0, keepdims=True)


def project_back(m):
    width = m.xn.shape[1]

    @pl.loop(0, width // PIECE)
    def _(j):
        c = lanes_of(j, PIECE)
        m.wide[:, c] = lax.dot_general(m.da[...], m.w_in[c, :], NT, preferred_element_type=F32)


def norm_input_back(m):
    rows, width = m.xn.shape

    @pl.loop(0, rows // BLOCK)
    def _(i):
        r = pl.ds(pl.multiple_of(i * BLOCK, BLOCK), BLOCK)
        dxn = m.wide[r, :]
        xhat, rstd = statistics(m.xp[r, :].astype(F32))
        m1 = jnp.mean(dxn, axis=-1, keepdims=True)
        m2 = jnp.mean(dxn * xhat, axis=-1, keepdims=True)
        dx = rstd * (dxn - m1 - xhat * m2) + m.gm[r, :].astype(F32)
        m.dx[r, :] = dx.astype(BF16)


def save_pieces(m, y, k, b, part):
    size = m.pieces.shape[4]
    for core in range(2):
        for a in range(RING):
            low = (core * RING + a) * size
            m.pieces[core, k, y, a * RING + b] = part[low : low + size, :]


def weight_in_grad(m, side):
    @pl.loop(0, RING)
    def _(y):
        xn = m.xn[:, lanes_of(y, PIECE)]
        for b in range(RING):
            cols = m.da[:, pl.ds((side * RING + b) * PIECE, PIECE)]
            part = lax.dot_general(xn, cols, TN, preferred_element_type=F32)
            save_pieces(m, y, side, b, part.astype(BF16))


def weight_out_grad(m):
    @pl.loop(0, RING)
    def _(y):
        sw = m.sw[:, lanes_of(y, PIECE)]
        for b in range(RING):
            part = lax.dot_general(sw, m.gm[:, pl.ds(b * PIECE, PIECE)], TN, preferred_element_type=F32)
            save_pieces(m, y, 2, b, part.astype(BF16))


def module_kernel(scale, names, *refs):
    m = types.SimpleNamespace(**dict(zip(names, refs)))
    data = lax.axis_index("dp")
    shard = lax.axis_index("fsdp")
    y, core = shard // 2, shard % 2
    n_data = m.sendb.shape[0]
    slots, frames, width = m.cot.shape
    rows = slots * frames
    per = m.w_in_shard.shape[0]
    ring_y = range(1, RING)
    ring_d = range(1, n_data)

    def at_y(offset):
        return lax.rem(y + offset, RING)

    def at_d(offset):
        return lax.rem(data + offset, n_data)

    partner = (data, y * 2 + (1 - core))

    def peer_y(offset):
        return (data, at_y(offset) * 2 + core)

    def peer_d(offset):
        return (at_d(offset), shard)

    barrier = pltpu.get_barrier_semaphore()
    pl.semaphore_signal(barrier, inc=1, device_id=partner, device_id_type=MESH)
    for o in ring_y:
        pl.semaphore_signal(barrier, inc=1, device_id=peer_y(o), device_id_type=MESH)
    for o in ring_d:
        pl.semaphore_signal(barrier, inc=1, device_id=peer_d(o), device_id_type=MESH)

    pending = []

    def push(src, dst, sems, place, device, keep=True):
        copy = pltpu.make_async_remote_copy(
            src_ref=src, dst_ref=dst, send_sem=sems[0].at[place], recv_sem=sems[1].at[place],
            device_id=device, device_id_type=MESH)
        copy.start()
        if keep:
            pending.append(copy)
        return copy

    def arrive(copies):
        for copy in copies:
            copy.wait_recv()

    def wide(a):
        return a.astype(F32)

    mine = pl.ds(pl.multiple_of(shard * per, per), per)
    chunks = width // PIECE
    for j in range(chunks):
        m.w_in[mine, pl.ds(2 * j * PIECE, PIECE)] = m.w_in_shard[:, pl.ds(j * PIECE, PIECE)]
        m.w_in[mine, pl.ds((2 * j + 1) * PIECE, PIECE)] = m.w_in_shard[:, pl.ds(width + j * PIECE, PIECE)]
    m.w_out[mine, :] = m.w_out_shard[...]

    n_shard = 2 * RING

    def base(p):
        return (p * n_shard + shard) * slots

    pl.semaphore_wait(barrier, 1 + len(ring_y) + len(ring_d))

    def part(j, owner_y):
        r = pl.ds(pl.multiple_of((owner_y * 2 + core) * per, per), per)
        if j < chunks:
            return m.w_in.at[r, pl.ds(2 * j * PIECE, 2 * PIECE)]
        return m.w_out.at[r, :]

    weights, passed = [], []
    right, left = 1, RING - 1

    def send_weights(j):
        src = part(j, y)
        weights.append([push(src, src, m.weight_sems, (j, i), peer_y(o)) for i, o in enumerate((right, left))])
        passed.append([push(src, src, m.pass_sems, (j, 0), partner)])

    ahead = 3
    for j in range(ahead):
        send_weights(j)

    @pl.loop(0, n_data)
    def _(p):
        found, place, out_block = 0, 0, 0
        for j in range(slots):
            hit = m.owner[base(p) + j] == data
            found = found + jnp.where(hit, 1, 0)
            place = place + jnp.where(hit, m.slot[base(p) + j], 0)
            out_block = out_block + jnp.where(m.owner[base(data) + j] == p, j, 0)
        m.place[p] = place - slots * (1 - found)
        m.block_for[p] = jnp.minimum(out_block, slots - 1)
        m.sendb[p] = m.cot[jnp.minimum(place, slots - 1)]

    def exchange(dst, sems):
        copies = [push(m.sendb.at[at_d(o)], dst.at[data], sems, o - 1, peer_d(o), False) for o in ring_d]
        dst[data] = m.sendb[data]
        return copies

    cot_copies = exchange(m.cot_recv, m.cot_sems)

    for b in range(slots):
        m.limit[pl.ds(b, 1), :] = jnp.full((1, LANES), m.lengths[base(data) + b], jnp.int32)
    prepare(m)
    norm_input(m)

    @pl.loop(0, slots)
    def _(s):
        source = 0
        for p in range(n_data):
            source = source + jnp.where(m.place[p] == s, p, 0)
        m.source_of[s] = jnp.minimum(source, n_data - 1)

    def weights_near(j):
        for i, (far, near) in enumerate(((left, right), (right, left))):
            weights[j][i].wait_recv()
            src = part(j, at_y(far))
            piece = src.at[pl.ds(i * (per // 2), per // 2), :]
            weights[j].append(push(piece, piece, m.weight_sems, (j, 2 + i), peer_y(near)))
            passed[j].append(push(src, src, m.pass_sems, (j, 1 + i), partner))
        if j + ahead <= chunks:
            send_weights(j + ahead)

    def weights_far(j):
        arrive(weights[j][2:])
        src = part(j, at_y(2))
        passed[j].append(push(src, src, m.pass_sems, (j, 3), partner))
        arrive(passed[j])

    weights_near(0)
    for j in range(chunks):
        weights_near(j + 1)
        weights_far(j)
        gate_chunk(m, j)
        conv_chunk(m, j)
    norm_conv(m)

    def core_start(k):
        return [push(m.pieces.at[1 - core, k], m.core_recv.at[k], m.core_sems, k, partner)]

    def first(k, copies):
        arrive(copies)

        @pl.loop(0, RING)
        def _(a):
            m.pieces[core, k, a] = (wide(m.pieces[core, k, a]) + wide(m.core_recv[k, a])).astype(BF16)

        return [push(m.pieces.at[core, k, at_y(o)], m.recv_y.at[k, o - 1], m.sum_y_sems,
                     (k, o - 1), peer_y(o)) for o in ring_y]

    def second(k, copies):
        arrive(copies)

        @pl.loop(0, n_data)
        def _(d):
            acc = wide(m.pieces[core, k, y, d])
            for o in ring_y:
                acc = acc + wide(m.recv_y[k, o - 1, d])
            m.pieces[core, k, y, d] = acc.astype(BF16)

        return [push(m.pieces.at[core, k, y, at_d(o)], m.last_d.at[k, o - 1], m.sum_d_sems,
                     (k, o - 1), peer_d(o)) for o in ring_d]

    def third(k, copies):
        arrive(copies)
        acc = wide(m.pieces[core, k, y, data])
        for o in ring_d:
            acc = acc + wide(m.last_d[k, o - 1])
        m.fin[k, data] = acc.astype(BF16)
        return [push(m.fin.at[k, data], m.fin.at[k, data], m.fin_sems, (k, o - 1), peer_d(o)) for o in ring_d]

    def last(k, copies):
        arrive(copies)
        size, cols = m.fin.shape[2], m.fin.shape[3]
        for a in range(RING):
            for b in range(RING):
                piece = wide(m.fin[k, a * RING + b]) * scale
                r = pl.ds(a * size, size)
                if k < 2:
                    m.grad_in[r, pl.ds((b % 2 * RING + k * 2 + b // 2) * cols, cols)] = piece
                else:
                    m.grad_out[r, pl.ds(b * cols, cols)] = piece

    arrive(cot_copies)
    for b in range(slots):
        m.dx[pl.ds(b * frames, frames), :] = m.cot_recv[m.owner[base(data) + b]]
    mask_cotangent(m)

    weight_out_grad(m)
    two = core_start(2)
    weights_far(chunks)
    mix_out(m)
    two = first(2, two)
    untime(m, m.lines)
    for copy in cot_copies:
        copy.wait_send()

    @pl.loop(0, n_data)
    def _(p):
        m.sendb[p] = m.lines[m.block_for[p]]

    out_copies = exchange(m.out_recv, m.out_sems)
    pending.extend(out_copies)

    norm_conv_back(m)
    conv_back(m, 0)
    weight_in_grad(m, 0)
    zero = core_start(0)
    two = second(2, two)
    zero = first(0, zero)
    conv_back(m, 1)
    weight_in_grad(m, 1)
    one = core_start(1)
    two = third(2, two)
    project_back(m)
    one = first(1, one)
    taps_back(m)

    small = [push(m.small.at[1 - core], m.small_core, m.small_sems, 0, partner)]
    norm_input_back(m)
    arrive(small)
    m.small_core[...] = m.small_core[...] + m.small[core]
    m.small_y[y] = m.small_core[y]
    small = [push(m.small_core.at[at_y(o)], m.small_y.at[y], m.small_sems, o, peer_y(o)) for o in ring_y]

    zero = second(0, zero)
    untime(m, m.grad_frames)
    last(2, two)
    arrive(out_copies)

    @pl.loop(0, slots)
    def _(s):
        m.out_frames[s] = m.out_recv[m.source_of[s]]

    zero = third(0, zero)
    one = second(1, one)

    arrive(small)
    m.small_d[data] = (m.small_y[0] + m.small_y[1]) + (m.small_y[2] + m.small_y[3])
    small = [push(m.small_d.at[data], m.small_d.at[data], m.small_d_sems, o - 1, peer_d(o)) for o in ring_d]
    last(0, zero)
    one = third(1, one)

    arrive(small)
    total = m.small_d[0]
    for d in range(1, n_data):
        total = total + m.small_d[d]
    m.small_all[core, y] = total
    own = m.small_all.at[core, y]
    small = [push(own, own, m.small_sems, RING + o, peer_y(o)) for o in ring_y]
    arrive(small)
    half = m.small_all.at[core]
    small = [push(half, half, m.small_sems, 2 * RING, partner)]
    last(1, one)

    arrive(small)
    lanes = m.small_all.shape[3]
    taps = m.taps.shape[0]
    for a in range(2):
        for b in range(RING):
            c = pl.ds((a * RING + b) * lanes, lanes)
            m.grad_taps[:, c] = m.small_all[a, b, pl.ds(0, taps), :] * scale
            m.grad_gain[:, c] = m.small_all[a, b, pl.ds(taps, 1), :] * scale
            m.grad_bias[:, c] = m.small_all[a, b, pl.ds(taps + 1, 1), :] * scale
    for copy in pending:
        copy.wait_send()


def module_call(scale, owner, slot, lengths, frames, cotangent, w_in, taps, gain, bias, w_out, n_data):
    slots, count, width = frames.shape
    rows = slots * count
    k = taps.shape[0]
    lines = -(-(k + 2) // 8) * 8
    size, cols = width // 32, width // RING
    lanes = width // 8
    shape = jax.ShapeDtypeStruct
    dma = pltpu.SemaphoreType.DMA
    inputs = dict(
        owner=owner, slot=slot, lengths=lengths,
        x=frames.reshape(rows, width), cot=cotangent, w_in_shard=w_in, taps=taps,
        gain=gain, bias=bias, w_out_shard=w_out)
    outputs = dict(
        out_frames=shape((slots, count, width), BF16),
        grad_frames=shape((slots, count, width), BF16),
        grad_in=shape((width // 8, 2 * width), F32),
        grad_out=shape((width // 8, width), F32),
        grad_taps=shape((k, width), F32),
        grad_gain=shape((1, width), F32),
        grad_bias=shape((1, width), F32))
    tables = dict(place=(n_data,), block_for=(n_data,), source_of=(slots,))
    buffers = dict(
        limit=((slots, LANES), jnp.int32),
        w_in=((width, 2 * width), BF16), w_out=((width, width), BF16),
        xp=((rows, width), BF16), xn=((rows, width), BF16), sig=((rows, width), F32),
        chat=((rows, width), F32), rstd=((rows, LANES), F32), sw=((rows, width), BF16),
        glu=((count + k - 1, slots, width), F32), dconv=((count + k - 1, slots, width), F32),
        spread=((k, slots, width), F32), gm=((rows, width), BF16), da=((rows, 2 * width), BF16),
        dx=((rows, width), BF16), wide=((rows, width), F32), sums=((2, slots, width), F32),
        to_time=((rows, rows), BF16), to_block=((rows, rows), BF16),
        lines=((slots, count, width), BF16), sendb=((n_data, count, width), BF16),
        cot_recv=((n_data, count, width), BF16), out_recv=((n_data, count, width), BF16),
        pieces=((2, 3, RING, n_data, size, cols), BF16),
        core_recv=((3, RING, n_data, size, cols), BF16),
        recv_y=((3, RING - 1, n_data, size, cols), BF16),
        last_d=((3, n_data - 1, size, cols), BF16),
        fin=((3, n_data, size, cols), BF16),
        small=((2, RING, lines, lanes), F32), small_core=((RING, lines, lanes), F32),
        small_y=((RING, lines, lanes), F32), small_d=((n_data, lines, lanes), F32),
        small_all=((2, RING, lines, lanes), F32))
    pairs = dict(
        weight_sems=(5, 4), pass_sems=(5, RING), cot_sems=(n_data - 1,), out_sems=(n_data - 1,),
        core_sems=(3,), sum_y_sems=(3, RING - 1), sum_d_sems=(3, n_data - 1), fin_sems=(3, n_data - 1),
        small_sems=(2 * RING + 1,), small_d_sems=(n_data - 1,))
    names = list(inputs) + list(outputs) + list(tables) + list(buffers)
    vmem = pl.BlockSpec(memory_space=pltpu.VMEM)
    smem = pl.BlockSpec(memory_space=pltpu.SMEM)

    def body(*refs):
        plain, sems = refs[: len(names)], refs[len(names) :]
        both = [(sems[2 * i], sems[2 * i + 1]) for i in range(len(pairs))]
        module_kernel(scale, names + list(pairs), *plain, *both)

    return pl.pallas_call(
        body,
        out_shape=tuple(outputs.values()),
        in_specs=[smem] * 3 + [vmem] * (len(inputs) - 3),
        out_specs=(vmem,) * len(outputs),
        scratch_shapes=[pltpu.SMEM(t, jnp.int32) for t in tables.values()]
        + [pltpu.VMEM(*b) for b in buffers.values()]
        + [dma(s) for s in pairs.values() for _ in range(2)],
        compiler_params=pltpu.CompilerParams(
            collective_id=0, has_side_effects=True, vmem_limit_bytes=VMEM_LIMIT),
        name="conv_module",
    )(*inputs.values())


VMEM_LIMIT = 63 * 2**20


def finish_kernel(*refs):
    count = len(refs) // 4
    plain, sems = refs[: 3 * count], refs[3 * count :]
    loads, stores = [], []
    for i in range(count):
        loads.append(pltpu.make_async_copy(plain[i], plain[2 * count + i], sems[i].at[0]))
        loads[-1].start()
    for i in range(count):
        loads[i].wait()
        stores.append(pltpu.make_async_copy(plain[2 * count + i], plain[count + i], sems[i].at[1]))
        stores[-1].start()
    for copy in stores:
        copy.wait()


def finish(arrays):
    hbm = pl.BlockSpec(memory_space=pl.ANY)
    return pl.pallas_call(
        finish_kernel,
        out_shape=tuple(jax.ShapeDtypeStruct(a.shape, a.dtype) for a in arrays),
        in_specs=[hbm] * len(arrays),
        out_specs=(hbm,) * len(arrays),
        scratch_shapes=[pltpu.VMEM(a.shape, a.dtype) for a in arrays]
        + [pltpu.SemaphoreType.DMA((2,)) for _ in arrays],
        compiler_params=pltpu.CompilerParams(vmem_limit_bytes=VMEM_LIMIT),
        name="finish",
    )(*arrays)


def shards(frames, lengths, owner, slot, w_in, kernel, dw_gain, dw_bias, w_out, cotangent):
    n_data = lax.axis_size("dp")
    n_shard = lax.axis_size("fsdp")
    slots, count, width = frames.shape
    scale = 1.0 / math.sqrt(slots * count * n_data * n_shard)
    results = module_call(
        scale, owner, slot, lengths, frames, cotangent, w_in, kernel, dw_gain[None], dw_bias[None], w_out,
        n_data)
    out_frames, grad_frames, grad_in, grad_out, grad_taps, grad_gain, grad_bias = finish(results)
    return (
        out_frames,
        grad_frames,
        grad_in,
        grad_taps,
        grad_gain[0],
        grad_bias[0],
        grad_out,
    )


def solution(mesh):
    placed = (
        P(("dp", "fsdp"), None, None),
        P(),
        P(),
        P(),
        P("fsdp", None),
        P(),
        P(),
        P(),
        P("fsdp", None),
        P(("dp", "fsdp"), None, None),
    )
    return jax.shard_map(
        shards,
        mesh=mesh,
        in_specs=placed,
        out_specs=(
            P(("dp", "fsdp"), None, None),
            P(("dp", "fsdp"), None, None),
            P("fsdp", None),
            P(),
            P(),
            P(),
            P("fsdp", None),
        ),
        check_vma=False,
    )
```

```python
import math
import types

import jax
import jax.numpy as jnp
from jax import lax
from jax.experimental import pallas as pl
from jax.experimental.pallas import tpu as pltpu
from jax.sharding import PartitionSpec as P

MESH = pl.DeviceIdType.MESH

LANES = 128
CHUNK = 16
PIECE = 256
BLOCK = 64
RING = 4
EPS = 1e-05
NT = (((1,), (1,)), ((), ()))
TN = (((0,), (0,)), ((), ()))
BF16 = jnp.bfloat16
F32 = jnp.float32


def lanes_of(i, width=LANES):
    return pl.ds(pl.multiple_of(i * width, width), width)


def statistics(values):
    center = values - jnp.mean(values, axis=-1, keepdims=True)
    rstd = lax.rsqrt(jnp.mean(center * center, axis=-1, keepdims=True) + EPS)
    return center * rstd, rstd


def logistic(v):
    return 1.0 / (1.0 + jnp.exp(-v))


def order_matrix(rows, slots, to_time):
    r = lax.broadcasted_iota(jnp.int32, (rows, rows), 0)
    c = lax.broadcasted_iota(jnp.int32, (rows, rows), 1)
    frames = rows // slots
    if to_time:
        place = (r % slots) * frames + r // slots
    else:
        place = (r % frames) * slots + r // frames
    return jnp.where(c == place, 1.0, 0.0).astype(BF16)


def prepare(m):
    m.small[...] = jnp.zeros_like(m.small)
    taps, slots, width = m.spread.shape
    half = (taps - 1) // 2
    frames = m.glu.shape[0] - 2 * half
    for k in range(taps):
        m.spread[k] = jnp.broadcast_to(m.taps[k : k + 1, :], (slots, width))
    m.to_time[...] = order_matrix(m.xn.shape[0], slots, True)
    m.to_block[...] = order_matrix(m.xn.shape[0], slots, False)
    edge = jnp.zeros((half, slots, width), F32)
    for ref in (m.glu, m.dconv):
        ref[pl.ds(0, half)] = edge
        ref[pl.ds(half + frames, half)] = edge


def norm_input(m):
    rows, width = m.xp.shape

    @pl.loop(0, width // PIECE)
    def _(j):
        c = lanes_of(j, PIECE)
        m.xp[:, c] = jnp.dot(m.to_time[...], m.x[:, c], preferred_element_type=F32).astype(BF16)

    @pl.loop(0, rows // BLOCK)
    def _(i):
        r = pl.ds(pl.multiple_of(i * BLOCK, BLOCK), BLOCK)
        m.xn[r, :] = statistics(m.xp[r, :].astype(F32))[0].astype(BF16)


def gate_chunk(m, j):
    rows, width = m.xn.shape
    slots = m.limit.shape[0]
    frames = rows // slots
    half = (m.spread.shape[0] - 1) // 2
    c = pl.ds(j * PIECE, PIECE)
    left = jnp.dot(m.xn[...], m.w_in[:, pl.ds(2 * j * PIECE, PIECE)], preferred_element_type=F32)
    gate = jnp.dot(m.xn[...], m.w_in[:, pl.ds((2 * j + 1) * PIECE, PIECE)], preferred_element_type=F32)
    sig = logistic(gate)
    m.sig[:, c] = sig
    time = lax.broadcasted_iota(jnp.int32, (frames, slots, PIECE), 0)
    limit = jnp.concatenate([m.limit[...]] * (PIECE // LANES), axis=1)
    glu = (left * sig).reshape(frames, slots, PIECE)
    m.glu[pl.ds(half, frames), :, c] = jnp.where(time < limit[None], glu, 0.0)


def slide(padded, spread, start, lanes, flip):
    taps = spread.shape[0]
    acc = None
    for k in range(taps):
        weight = spread[taps - 1 - k if flip else k, :, lanes]
        term = weight[None] * padded[pl.ds(start + k, CHUNK), :, lanes]
        acc = term if acc is None else acc + term
    return acc


def conv_chunk(m, j):
    rows, width = m.xn.shape
    slots = m.limit.shape[0]
    steps = rows // slots // CHUNK

    @pl.loop(0, PIECE // LANES * steps)
    def _(i):
        c = lanes_of(j * (PIECE // LANES) + i // steps)
        t = i % steps
        acc = slide(m.glu, m.spread, t * CHUNK, c, False)
        r = pl.ds(pl.multiple_of(t * CHUNK * slots, CHUNK * slots), CHUNK * slots)
        m.chat[r, c] = acc.reshape(CHUNK * slots, LANES)


def norm_conv(m):
    rows, width = m.xn.shape

    @pl.loop(0, rows // BLOCK)
    def _(i):
        r = pl.ds(pl.multiple_of(i * BLOCK, BLOCK), BLOCK)
        chat, rstd = statistics(m.chat[r, :])
        m.chat[r, :] = chat
        m.rstd[r, :] = jnp.broadcast_to(rstd, (BLOCK, LANES))
        z = chat * m.gain[...] + m.bias[...]
        m.sw[r, :] = (z * logistic(z)).astype(BF16)


def mix_out(m):
    rows, width = m.xn.shape
    slots = m.limit.shape[0]
    frames = rows // slots

    @pl.loop(0, width // PIECE)
    def _(j):
        c = lanes_of(j, PIECE)
        mixed = jnp.dot(m.sw[...], m.w_out[:, c], preferred_element_type=F32)
        time = lax.broadcasted_iota(jnp.int32, (frames, slots, PIECE), 0)
        limit = jnp.concatenate([m.limit[...]] * (PIECE // LANES), axis=1)
        out = (m.xp[:, c].astype(F32) + mixed).reshape(frames, slots, PIECE)
        m.dx[:, c] = jnp.where(time < limit[None], out, 0.0).reshape(rows, PIECE).astype(BF16)


def untime(m, dst):
    slots, frames, width = dst.shape

    @pl.loop(0, width // PIECE)
    def _(j):
        c = lanes_of(j, PIECE)
        line = jnp.dot(m.to_block[...], m.dx[:, c], preferred_element_type=F32).astype(BF16)
        for b in range(slots):
            dst[b, :, c] = line[b * frames : (b + 1) * frames, :]


def mask_cotangent(m):
    rows, width = m.xn.shape
    slots = m.limit.shape[0]
    frames = rows // slots

    @pl.loop(0, width // PIECE)
    def _(j):
        c = lanes_of(j, PIECE)
        g = jnp.dot(m.to_time[...], m.dx[:, c], preferred_element_type=F32)
        time = lax.broadcasted_iota(jnp.int32, (frames, slots, PIECE), 0)
        limit = jnp.concatenate([m.limit[...]] * (PIECE // LANES), axis=1)
        g = jnp.where(time < limit[None], g.reshape(frames, slots, PIECE), 0.0)
        m.gm[:, c] = g.reshape(rows, PIECE).astype(BF16)


def norm_conv_back(m):
    rows, width = m.xn.shape
    taps, slots, _ = m.spread.shape
    half = (taps - 1) // 2
    steps = BLOCK // slots
    m.sums[...] = jnp.zeros_like(m.sums)

    @pl.loop(0, width // PIECE)
    def _(j):
        c = lanes_of(j, PIECE)
        m.wide[:, c] = lax.dot_general(m.gm[...], m.w_out[c, :], NT, preferred_element_type=F32)

    @pl.loop(0, rows // BLOCK)
    def _(i):
        r = pl.ds(pl.multiple_of(i * BLOCK, BLOCK), BLOCK)
        ds = m.wide[r, :]
        chat = m.chat[r, :]
        gain = m.gain[...]
        z = chat * gain + m.bias[...]
        sigz = logistic(z)
        dz = ds * sigz * (1.0 + z * (1.0 - sigz))
        m.sums[0] += jnp.sum((dz * chat).reshape(steps, slots, width), axis=0)
        m.sums[1] += jnp.sum(dz.reshape(steps, slots, width), axis=0)
        dchat = dz * gain
        m1 = jnp.mean(dchat, axis=-1, keepdims=True)
        m2 = jnp.mean(dchat * chat, axis=-1, keepdims=True)
        dconv = m.rstd[r, :][:, :1] * (dchat - m1 - chat * m2)
        m.dconv[pl.ds(half + i * steps, steps)] = dconv.reshape(steps, slots, width)


def conv_back(m, side):
    rows, width = m.xn.shape
    taps, slots, _ = m.spread.shape
    frames = rows // slots
    half = (taps - 1) // 2
    steps = frames // CHUNK
    tiles = width // LANES // 2

    @pl.loop(0, tiles * steps)
    def _(i):
        l = side * tiles + i // steps
        t = i % steps
        c = lanes_of(l)
        acc = slide(m.dconv, m.spread, t * CHUNK, c, True)
        r = pl.ds(pl.multiple_of(t * CHUNK * slots, CHUNK * slots), CHUNK * slots)
        near = lax.broadcasted_iota(jnp.int32, (CHUNK, slots, LANES), 0) + t * CHUNK
        dglu = jnp.where(near < m.limit[...][None], acc, 0.0).reshape(CHUNK * slots, LANES)
        sig = m.sig[r, c]
        glu = m.glu[pl.ds(half + t * CHUNK, CHUNK), :, c].reshape(CHUNK * slots, LANES)
        place = (l // 2) * 4 + l % 2
        m.da[r, lanes_of(place)] = (dglu * sig).astype(BF16)
        m.da[r, lanes_of(place + 2)] = (dglu * glu * (1.0 - sig)).astype(BF16)


def taps_back(m):
    rows, width = m.xn.shape
    taps, slots, _ = m.spread.shape
    frames = rows // slots
    half = (taps - 1) // 2
    lanes_q = width // 8 // LANES
    step = 8

    @pl.loop(0, width // LANES)
    def _(l):
        c = lanes_of(l)
        for low in range(0, taps, 16):
            count = min(16, taps - low)

            def body(t, acc, low=low, count=count):
                base = t * step
                out = []
                d = m.dconv[pl.ds(half + base, step), :, c]
                for k in range(count):
                    row = m.glu[pl.ds(base + low + k, step), :, c]
                    out.append(acc[k] + jnp.sum(d * row, axis=0))
                return tuple(out)

            acc = lax.fori_loop(0, frames // step, body,
                                tuple(jnp.zeros((slots, LANES), F32) for _ in range(count)))
            for k in range(count):
                m.small[l // 4, l % 4, pl.ds(low + k, 1), :] = jnp.sum(acc[k], axis=0, keepdims=True)
        for k in range(2):
            m.small[l // 4, l % 4, pl.ds(taps + k, 1), :] = jnp.sum(m.sums[k, :, c], axis=0, keepdims=True)


def project_back(m):
    width = m.xn.shape[1]

    @pl.loop(0, width // PIECE)
    def _(j):
        c = lanes_of(j, PIECE)
        m.wide[:, c] = lax.dot_general(m.da[...], m.w_in[c, :], NT, preferred_element_type=F32)


def norm_input_back(m):
    rows, width = m.xn.shape

    @pl.loop(0, rows // BLOCK)
    def _(i):
        r = pl.ds(pl.multiple_of(i * BLOCK, BLOCK), BLOCK)
        dxn = m.wide[r, :]
        xhat, rstd = statistics(m.xp[r, :].astype(F32))
        m1 = jnp.mean(dxn, axis=-1, keepdims=True)
        m2 = jnp.mean(dxn * xhat, axis=-1, keepdims=True)
        dx = rstd * (dxn - m1 - xhat * m2) + m.gm[r, :].astype(F32)
        m.dx[r, :] = dx.astype(BF16)


def save_pieces(m, y, k, b, part):
    size = m.pieces.shape[4]
    for core in range(2):
        for a in range(RING):
            low = (core * RING + a) * size
            m.pieces[core, k, y, a * RING + b] = part[low : low + size, :]


def weight_in_grad(m, side):
    @pl.loop(0, RING)
    def _(y):
        xn = m.xn[:, lanes_of(y, PIECE)]
        for b in range(RING):
            cols = m.da[:, pl.ds((side * RING + b) * PIECE, PIECE)]
            part = lax.dot_general(xn, cols, TN, preferred_element_type=F32)
            save_pieces(m, y, side, b, part.astype(BF16))


def weight_out_grad(m):
    @pl.loop(0, RING)
    def _(y):
        sw = m.sw[:, lanes_of(y, PIECE)]
        for b in range(RING):
            part = lax.dot_general(sw, m.gm[:, pl.ds(b * PIECE, PIECE)], TN, preferred_element_type=F32)
            save_pieces(m, y, 2, b, part.astype(BF16))


def module_kernel(scale, names, *refs):
    m = types.SimpleNamespace(**dict(zip(names, refs)))
    data = lax.axis_index("dp")
    shard = lax.axis_index("fsdp")
    y, core = shard // 2, shard % 2
    n_data = m.sendb.shape[0]
    slots, frames, width = m.cot.shape
    rows = slots * frames
    per = m.w_in_shard.shape[0]
    ring_y = range(1, RING)
    ring_d = range(1, n_data)

    def at_y(offset):
        return lax.rem(y + offset, RING)

    def at_d(offset):
        return lax.rem(data + offset, n_data)

    partner = (data, y * 2 + (1 - core))

    def peer_y(offset):
        return (data, at_y(offset) * 2 + core)

    def peer_d(offset):
        return (at_d(offset), shard)

    barrier = pltpu.get_barrier_semaphore()
    pl.semaphore_signal(barrier, inc=1, device_id=partner, device_id_type=MESH)
    for o in ring_y:
        pl.semaphore_signal(barrier, inc=1, device_id=peer_y(o), device_id_type=MESH)
    for o in ring_d:
        pl.semaphore_signal(barrier, inc=1, device_id=peer_d(o), device_id_type=MESH)

    pending = []

    def push(src, dst, sems, place, device, keep=True):
        copy = pltpu.make_async_remote_copy(
            src_ref=src, dst_ref=dst, send_sem=sems[0].at[place], recv_sem=sems[1].at[place],
            device_id=device, device_id_type=MESH)
        copy.start()
        if keep:
            pending.append(copy)
        return copy

    def arrive(copies):
        for copy in copies:
            copy.wait_recv()

    def wide(a):
        return a.astype(F32)

    mine = pl.ds(pl.multiple_of(shard * per, per), per)
    chunks = width // PIECE
    for j in range(chunks):
        m.w_in[mine, pl.ds(2 * j * PIECE, PIECE)] = m.w_in_shard[:, pl.ds(j * PIECE, PIECE)]
        m.w_in[mine, pl.ds((2 * j + 1) * PIECE, PIECE)] = m.w_in_shard[:, pl.ds(width + j * PIECE, PIECE)]
    m.w_out[mine, :] = m.w_out_shard[...]

    n_shard = 2 * RING

    def base(p):
        return (p * n_shard + shard) * slots

    @pl.loop(0, n_data)
    def _(p):
        found, place, out_block = 0, 0, 0
        for j in range(slots):
            hit = m.owner[base(p) + j] == data
            found = found + jnp.where(hit, 1, 0)
            place = place + jnp.where(hit, m.slot[base(p) + j], 0)
            out_block = out_block + jnp.where(m.owner[base(data) + j] == p, j, 0)
        m.place[p] = place - slots * (1 - found)
        m.block_for[p] = jnp.minimum(out_block, slots - 1)
        m.sendb[p] = m.cot[jnp.minimum(place, slots - 1)]

    pl.semaphore_wait(barrier, 1 + len(ring_y) + len(ring_d))

    def part(j, owner_y):
        r = pl.ds(pl.multiple_of((owner_y * 2 + core) * per, per), per)
        if j < chunks:
            return m.w_in.at[r, pl.ds(2 * j * PIECE, 2 * PIECE)]
        return m.w_out.at[r, :]

    weights, passed = [], []
    right, left = 1, RING - 1

    def send_weights(j):
        src = part(j, y)
        weights.append([push(src, src, m.weight_sems, (j, i), peer_y(o)) for i, o in enumerate((right, left))])
        passed.append([push(src, src, m.pass_sems, (j, 0), partner)])

    ahead = 3
    for j in range(ahead):
        send_weights(j)

    def exchange(dst, sems):
        copies = [push(m.sendb.at[at_d(o)], dst.at[data], sems, o - 1, peer_d(o), False) for o in ring_d]
        dst[data] = m.sendb[data]
        return copies

    cot_copies = exchange(m.cot_recv, m.cot_sems)

    for b in range(slots):
        m.limit[pl.ds(b, 1), :] = jnp.full((1, LANES), m.lengths[base(data) + b], jnp.int32)
    prepare(m)
    norm_input(m)

    @pl.loop(0, slots)
    def _(s):
        source = 0
        for p in range(n_data):
            source = source + jnp.where(m.place[p] == s, p, 0)
        m.source_of[s] = jnp.minimum(source, n_data - 1)

    def weights_near(j):
        for i, (far, near) in enumerate(((left, right), (right, left))):
            weights[j][i].wait_recv()
            src = part(j, at_y(far))
            piece = src.at[pl.ds(i * (per // 2), per // 2), :]
            weights[j].append(push(piece, piece, m.weight_sems, (j, 2 + i), peer_y(near)))
            passed[j].append(push(src, src, m.pass_sems, (j, 1 + i), partner))
        if j + ahead <= chunks:
            send_weights(j + ahead)

    def weights_far(j):
        arrive(weights[j][2:])
        src = part(j, at_y(2))
        passed[j].append(push(src, src, m.pass_sems, (j, 3), partner))
        arrive(passed[j])

    weights_near(0)
    for j in range(chunks):
        weights_near(j + 1)
        weights_far(j)
        gate_chunk(m, j)
        conv_chunk(m, j)
    norm_conv(m)

    def core_start(k):
        return [push(m.pieces.at[1 - core, k], m.core_recv.at[k], m.core_sems, k, partner)]

    def first(k, copies):
        arrive(copies)

        @pl.loop(0, RING)
        def _(a):
            m.pieces[core, k, a] = (wide(m.pieces[core, k, a]) + wide(m.core_recv[k, a])).astype(BF16)

        return [push(m.pieces.at[core, k, at_y(o)], m.recv_y.at[k, o - 1], m.sum_y_sems,
                     (k, o - 1), peer_y(o)) for o in ring_y]

    def second(k, copies):
        arrive(copies)

        @pl.loop(0, n_data)
        def _(d):
            acc = wide(m.pieces[core, k, y, d])
            for o in ring_y:
                acc = acc + wide(m.recv_y[k, o - 1, d])
            m.pieces[core, k, y, d] = acc.astype(BF16)

        return [push(m.pieces.at[core, k, y, at_d(o)], m.last_d.at[k, o - 1], m.sum_d_sems,
                     (k, o - 1), peer_d(o)) for o in ring_d]

    def third(k, copies):
        arrive(copies)
        acc = wide(m.pieces[core, k, y, data])
        for o in ring_d:
            acc = acc + wide(m.last_d[k, o - 1])
        m.fin[k, data] = acc.astype(BF16)
        return [push(m.fin.at[k, data], m.fin.at[k, data], m.fin_sems, (k, o - 1), peer_d(o)) for o in ring_d]

    def last(k, copies):
        arrive(copies)
        size, cols = m.fin.shape[2], m.fin.shape[3]
        for a in range(RING):
            for b in range(RING):
                piece = wide(m.fin[k, a * RING + b]) * scale
                r = pl.ds(a * size, size)
                if k < 2:
                    m.grad_in[r, pl.ds((b % 2 * RING + k * 2 + b // 2) * cols, cols)] = piece
                else:
                    m.grad_out[r, pl.ds(b * cols, cols)] = piece

    arrive(cot_copies)
    for b in range(slots):
        m.dx[pl.ds(b * frames, frames), :] = m.cot_recv[m.owner[base(data) + b]]
    mask_cotangent(m)

    weight_out_grad(m)
    two = core_start(2)
    weights_far(chunks)
    mix_out(m)
    two = first(2, two)
    untime(m, m.lines)
    for copy in cot_copies:
        copy.wait_send()

    @pl.loop(0, n_data)
    def _(p):
        m.sendb[p] = m.lines[m.block_for[p]]

    out_copies = exchange(m.out_recv, m.out_sems)
    pending.extend(out_copies)

    norm_conv_back(m)
    conv_back(m, 0)
    weight_in_grad(m, 0)
    zero = core_start(0)
    two = second(2, two)
    zero = first(0, zero)
    conv_back(m, 1)
    weight_in_grad(m, 1)
    one = core_start(1)
    project_back(m)
    one = first(1, one)
    taps_back(m)

    small = [push(m.small.at[1 - core], m.small_core, m.small_sems, 0, partner)]
    norm_input_back(m)
    arrive(small)
    m.small_core[...] = m.small_core[...] + m.small[core]
    m.small_y[y] = m.small_core[y]
    small = [push(m.small_core.at[at_y(o)], m.small_y.at[y], m.small_sems, o, peer_y(o)) for o in ring_y]

    zero = second(0, zero)
    untime(m, m.grad_frames)
    two = third(2, two)
    arrive(out_copies)

    @pl.loop(0, slots)
    def _(s):
        m.out_frames[s] = m.out_recv[m.source_of[s]]

    zero = third(0, zero)
    one = second(1, one)

    arrive(small)
    m.small_d[data] = (m.small_y[0] + m.small_y[1]) + (m.small_y[2] + m.small_y[3])
    small = [push(m.small_d.at[data], m.small_d.at[data], m.small_d_sems, o - 1, peer_d(o)) for o in ring_d]
    last(2, two)
    last(0, zero)
    one = third(1, one)

    arrive(small)
    total = m.small_d[0]
    for d in range(1, n_data):
        total = total + m.small_d[d]
    m.small_all[core, y] = total
    own = m.small_all.at[core, y]
    small = [push(own, own, m.small_sems, RING + o, peer_y(o)) for o in ring_y]
    arrive(small)
    half = m.small_all.at[core]
    small = [push(half, half, m.small_sems, 2 * RING, partner)]
    last(1, one)

    arrive(small)
    lanes = m.small_all.shape[3]
    taps = m.taps.shape[0]
    for a in range(2):
        for b in range(RING):
            c = pl.ds((a * RING + b) * lanes, lanes)
            m.grad_taps[:, c] = m.small_all[a, b, pl.ds(0, taps), :] * scale
            m.grad_gain[:, c] = m.small_all[a, b, pl.ds(taps, 1), :] * scale
            m.grad_bias[:, c] = m.small_all[a, b, pl.ds(taps + 1, 1), :] * scale
    for copy in pending:
        copy.wait_send()


def module_call(scale, owner, slot, lengths, frames, cotangent, w_in, taps, gain, bias, w_out, n_data):
    slots, count, width = frames.shape
    rows = slots * count
    k = taps.shape[0]
    lines = -(-(k + 2) // 8) * 8
    size, cols = width // 32, width // RING
    lanes = width // 8
    shape = jax.ShapeDtypeStruct
    dma = pltpu.SemaphoreType.DMA
    inputs = dict(
        owner=owner, slot=slot, lengths=lengths,
        x=frames.reshape(rows, width), cot=cotangent, w_in_shard=w_in, taps=taps,
        gain=gain, bias=bias, w_out_shard=w_out)
    outputs = dict(
        out_frames=shape((slots, count, width), BF16),
        grad_frames=shape((slots, count, width), BF16),
        grad_in=shape((width // 8, 2 * width), F32),
        grad_out=shape((width // 8, width), F32),
        grad_taps=shape((k, width), F32),
        grad_gain=shape((1, width), F32),
        grad_bias=shape((1, width), F32))
    tables = dict(place=(n_data,), block_for=(n_data,), source_of=(slots,))
    buffers = dict(
        limit=((slots, LANES), jnp.int32),
        w_in=((width, 2 * width), BF16), w_out=((width, width), BF16),
        xp=((rows, width), BF16), xn=((rows, width), BF16), sig=((rows, width), F32),
        chat=((rows, width), F32), rstd=((rows, LANES), F32), sw=((rows, width), BF16),
        glu=((count + k - 1, slots, width), F32), dconv=((count + k - 1, slots, width), F32),
        spread=((k, slots, width), F32), gm=((rows, width), BF16), da=((rows, 2 * width), BF16),
        dx=((rows, width), BF16), wide=((rows, width), F32), sums=((2, slots, width), F32),
        to_time=((rows, rows), BF16), to_block=((rows, rows), BF16),
        lines=((slots, count, width), BF16), sendb=((n_data, count, width), BF16),
        cot_recv=((n_data, count, width), BF16), out_recv=((n_data, count, width), BF16),
        pieces=((2, 3, RING, n_data, size, cols), BF16),
        core_recv=((3, RING, n_data, size, cols), BF16),
        recv_y=((3, RING - 1, n_data, size, cols), BF16),
        last_d=((3, n_data - 1, size, cols), BF16),
        fin=((3, n_data, size, cols), BF16),
        small=((2, RING, lines, lanes), F32), small_core=((RING, lines, lanes), F32),
        small_y=((RING, lines, lanes), F32), small_d=((n_data, lines, lanes), F32),
        small_all=((2, RING, lines, lanes), F32))
    pairs = dict(
        weight_sems=(5, 4), pass_sems=(5, RING), cot_sems=(n_data - 1,), out_sems=(n_data - 1,),
        core_sems=(3,), sum_y_sems=(3, RING - 1), sum_d_sems=(3, n_data - 1), fin_sems=(3, n_data - 1),
        small_sems=(2 * RING + 1,), small_d_sems=(n_data - 1,))
    names = list(inputs) + list(outputs) + list(tables) + list(buffers)
    vmem = pl.BlockSpec(memory_space=pltpu.VMEM)
    smem = pl.BlockSpec(memory_space=pltpu.SMEM)

    def body(*refs):
        plain, sems = refs[: len(names)], refs[len(names) :]
        both = [(sems[2 * i], sems[2 * i + 1]) for i in range(len(pairs))]
        module_kernel(scale, names + list(pairs), *plain, *both)

    return pl.pallas_call(
        body,
        out_shape=tuple(outputs.values()),
        in_specs=[smem] * 3 + [vmem] * (len(inputs) - 3),
        out_specs=(vmem,) * len(outputs),
        scratch_shapes=[pltpu.SMEM(t, jnp.int32) for t in tables.values()]
        + [pltpu.VMEM(*b) for b in buffers.values()]
        + [dma(s) for s in pairs.values() for _ in range(2)],
        compiler_params=pltpu.CompilerParams(
            collective_id=0, has_side_effects=True, vmem_limit_bytes=VMEM_LIMIT),
        name="conv_module",
    )(*inputs.values())


VMEM_LIMIT = 63 * 2**20


def finish_kernel(*refs):
    count = len(refs) // 4
    plain, sems = refs[: 3 * count], refs[3 * count :]
    loads, stores = [], []
    for i in range(count):
        loads.append(pltpu.make_async_copy(plain[i], plain[2 * count + i], sems[i].at[0]))
        loads[-1].start()
    for i in range(count):
        loads[i].wait()
        stores.append(pltpu.make_async_copy(plain[2 * count + i], plain[count + i], sems[i].at[1]))
        stores[-1].start()
    for copy in stores:
        copy.wait()


def finish(arrays):
    hbm = pl.BlockSpec(memory_space=pl.ANY)
    return pl.pallas_call(
        finish_kernel,
        out_shape=tuple(jax.ShapeDtypeStruct(a.shape, a.dtype) for a in arrays),
        in_specs=[hbm] * len(arrays),
        out_specs=(hbm,) * len(arrays),
        scratch_shapes=[pltpu.VMEM(a.shape, a.dtype) for a in arrays]
        + [pltpu.SemaphoreType.DMA((2,)) for _ in arrays],
        compiler_params=pltpu.CompilerParams(vmem_limit_bytes=VMEM_LIMIT),
        name="finish",
    )(*arrays)


def shards(frames, lengths, owner, slot, w_in, kernel, dw_gain, dw_bias, w_out, cotangent):
    n_data = lax.axis_size("dp")
    n_shard = lax.axis_size("fsdp")
    slots, count, width = frames.shape
    scale = 1.0 / math.sqrt(slots * count * n_data * n_shard)
    results = module_call(
        scale, owner, slot, lengths, frames, cotangent, w_in, kernel, dw_gain[None], dw_bias[None], w_out,
        n_data)
    out_frames, grad_frames, grad_in, grad_out, grad_taps, grad_gain, grad_bias = finish(results)
    return (
        out_frames,
        grad_frames,
        grad_in,
        grad_taps,
        grad_gain[0],
        grad_bias[0],
        grad_out,
    )


def solution(mesh):
    placed = (
        P(("dp", "fsdp"), None, None),
        P(),
        P(),
        P(),
        P("fsdp", None),
        P(),
        P(),
        P(),
        P("fsdp", None),
        P(("dp", "fsdp"), None, None),
    )
    return jax.shard_map(
        shards,
        mesh=mesh,
        in_specs=placed,
        out_specs=(
            P(("dp", "fsdp"), None, None),
            P(("dp", "fsdp"), None, None),
            P("fsdp", None),
            P(),
            P(),
            P(),
            P("fsdp", None),
        ),
        check_vma=False,
    )
```

```python
import math
import types

import jax
import jax.numpy as jnp
from jax import lax
from jax.experimental import pallas as pl
from jax.experimental.pallas import tpu as pltpu
from jax.sharding import PartitionSpec as P

MESH = pl.DeviceIdType.MESH

LANES = 128
CHUNK = 16
PIECE = 256
BLOCK = 128
RING = 4
EPS = 1e-05
NT = (((1,), (1,)), ((), ()))
TN = (((0,), (0,)), ((), ()))
BF16 = jnp.bfloat16
F32 = jnp.float32


def lanes_of(i, width=LANES):
    return pl.ds(pl.multiple_of(i * width, width), width)


def statistics(values):
    center = values - jnp.mean(values, axis=-1, keepdims=True)
    rstd = lax.rsqrt(jnp.mean(center * center, axis=-1, keepdims=True) + EPS)
    return center * rstd, rstd


def logistic(v):
    return 1.0 / (1.0 + jnp.exp(-v))


def order_matrix(rows, slots, to_time):
    r = lax.broadcasted_iota(jnp.int32, (rows, rows), 0)
    c = lax.broadcasted_iota(jnp.int32, (rows, rows), 1)
    frames = rows // slots
    if to_time:
        place = (r % slots) * frames + r // slots
    else:
        place = (r % frames) * slots + r // frames
    return jnp.where(c == place, 1.0, 0.0).astype(BF16)


def prepare(m):
    m.small[...] = jnp.zeros_like(m.small)
    taps, slots, width = m.spread.shape
    half = (taps - 1) // 2
    frames = m.glu.shape[0] - 2 * half
    for k in range(taps):
        m.spread[k] = jnp.broadcast_to(m.taps[k : k + 1, :], (slots, width))
    m.to_time[...] = order_matrix(m.xn.shape[0], slots, True)
    m.to_block[...] = order_matrix(m.xn.shape[0], slots, False)
    edge = jnp.zeros((half, slots, width), F32)
    for ref in (m.glu, m.dconv):
        ref[pl.ds(0, half)] = edge
        ref[pl.ds(half + frames, half)] = edge


def norm_input(m):
    rows, width = m.xp.shape

    @pl.loop(0, width // PIECE)
    def _(j):
        c = lanes_of(j, PIECE)
        m.xp[:, c] = jnp.dot(m.to_time[...], m.x[:, c], preferred_element_type=F32).astype(BF16)

    @pl.loop(0, rows // BLOCK)
    def _(i):
        r = pl.ds(pl.multiple_of(i * BLOCK, BLOCK), BLOCK)
        m.xn[r, :] = statistics(m.xp[r, :].astype(F32))[0].astype(BF16)


def gate_chunk(m, j):
    rows, width = m.xn.shape
    slots = m.limit.shape[0]
    frames = rows // slots
    half = (m.spread.shape[0] - 1) // 2
    c = pl.ds(j * PIECE, PIECE)
    left = jnp.dot(m.xn[...], m.w_in[:, pl.ds(2 * j * PIECE, PIECE)], preferred_element_type=F32)
    gate = jnp.dot(m.xn[...], m.w_in[:, pl.ds((2 * j + 1) * PIECE, PIECE)], preferred_element_type=F32)
    sig = logistic(gate)
    m.sig[:, c] = sig
    time = lax.broadcasted_iota(jnp.int32, (frames, slots, PIECE), 0)
    limit = jnp.concatenate([m.limit[...]] * (PIECE // LANES), axis=1)
    glu = (left * sig).reshape(frames, slots, PIECE)
    m.glu[pl.ds(half, frames), :, c] = jnp.where(time < limit[None], glu, 0.0)


def slide(padded, spread, start, lanes, flip):
    taps = spread.shape[0]
    acc = None
    for k in range(taps):
        weight = spread[taps - 1 - k if flip else k, :, lanes]
        term = weight[None] * padded[pl.ds(start + k, CHUNK), :, lanes]
        acc = term if acc is None else acc + term
    return acc


def conv_chunk(m, j):
    rows, width = m.xn.shape
    slots = m.limit.shape[0]
    steps = rows // slots // CHUNK

    @pl.loop(0, PIECE // LANES * steps)
    def _(i):
        c = lanes_of(j * (PIECE // LANES) + i // steps)
        t = i % steps
        acc = slide(m.glu, m.spread, t * CHUNK, c, False)
        r = pl.ds(pl.multiple_of(t * CHUNK * slots, CHUNK * slots), CHUNK * slots)
        m.chat[r, c] = acc.reshape(CHUNK * slots, LANES)


def norm_conv(m):
    rows, width = m.xn.shape

    @pl.loop(0, rows // BLOCK)
    def _(i):
        r = pl.ds(pl.multiple_of(i * BLOCK, BLOCK), BLOCK)
        chat, rstd = statistics(m.chat[r, :])
        m.chat[r, :] = chat
        m.rstd[r, :] = jnp.broadcast_to(rstd, (BLOCK, LANES))
        z = chat * m.gain[...] + m.bias[...]
        m.sw[r, :] = (z * logistic(z)).astype(BF16)


def mix_out(m):
    rows, width = m.xn.shape
    slots = m.limit.shape[0]
    frames = rows // slots

    @pl.loop(0, width // PIECE)
    def _(j):
        c = lanes_of(j, PIECE)
        mixed = jnp.dot(m.sw[...], m.w_out[:, c], preferred_element_type=F32)
        time = lax.broadcasted_iota(jnp.int32, (frames, slots, PIECE), 0)
        limit = jnp.concatenate([m.limit[...]] * (PIECE // LANES), axis=1)
        out = (m.xp[:, c].astype(F32) + mixed).reshape(frames, slots, PIECE)
        m.dx[:, c] = jnp.where(time < limit[None], out, 0.0).reshape(rows, PIECE).astype(BF16)


def untime(m, dst):
    slots, frames, width = dst.shape

    @pl.loop(0, width // PIECE)
    def _(j):
        c = lanes_of(j, PIECE)
        line = jnp.dot(m.to_block[...], m.dx[:, c], preferred_element_type=F32).astype(BF16)
        for b in range(slots):
            dst[b, :, c] = line[b * frames : (b + 1) * frames, :]


def mask_cotangent(m):
    rows, width = m.xn.shape
    slots = m.limit.shape[0]
    frames = rows // slots

    @pl.loop(0, width // PIECE)
    def _(j):
        c = lanes_of(j, PIECE)
        g = jnp.dot(m.to_time[...], m.dx[:, c], preferred_element_type=F32)
        time = lax.broadcasted_iota(jnp.int32, (frames, slots, PIECE), 0)
        limit = jnp.concatenate([m.limit[...]] * (PIECE // LANES), axis=1)
        g = jnp.where(time < limit[None], g.reshape(frames, slots, PIECE), 0.0)
        m.gm[:, c] = g.reshape(rows, PIECE).astype(BF16)


def norm_conv_back(m):
    rows, width = m.xn.shape
    taps, slots, _ = m.spread.shape
    half = (taps - 1) // 2
    steps = BLOCK // slots
    m.sums[...] = jnp.zeros_like(m.sums)

    @pl.loop(0, width // PIECE)
    def _(j):
        c = lanes_of(j, PIECE)
        m.wide[:, c] = lax.dot_general(m.gm[...], m.w_out[c, :], NT, preferred_element_type=F32)

    @pl.loop(0, rows // BLOCK)
    def _(i):
        r = pl.ds(pl.multiple_of(i * BLOCK, BLOCK), BLOCK)
        ds = m.wide[r, :]
        chat = m.chat[r, :]
        gain = m.gain[...]
        z = chat * gain + m.bias[...]
        sigz = logistic(z)
        dz = ds * sigz * (1.0 + z * (1.0 - sigz))
        m.sums[0] += jnp.sum((dz * chat).reshape(steps, slots, width), axis=0)
        m.sums[1] += jnp.sum(dz.reshape(steps, slots, width), axis=0)
        dchat = dz * gain
        m1 = jnp.mean(dchat, axis=-1, keepdims=True)
        m2 = jnp.mean(dchat * chat, axis=-1, keepdims=True)
        dconv = m.rstd[r, :][:, :1] * (dchat - m1 - chat * m2)
        m.dconv[pl.ds(half + i * steps, steps)] = dconv.reshape(steps, slots, width)


def conv_back(m, side):
    rows, width = m.xn.shape
    taps, slots, _ = m.spread.shape
    frames = rows // slots
    half = (taps - 1) // 2
    steps = frames // CHUNK
    tiles = width // LANES // 2

    @pl.loop(0, tiles * steps)
    def _(i):
        l = side * tiles + i // steps
        t = i % steps
        c = lanes_of(l)
        acc = slide(m.dconv, m.spread, t * CHUNK, c, True)
        r = pl.ds(pl.multiple_of(t * CHUNK * slots, CHUNK * slots), CHUNK * slots)
        near = lax.broadcasted_iota(jnp.int32, (CHUNK, slots, LANES), 0) + t * CHUNK
        dglu = jnp.where(near < m.limit[...][None], acc, 0.0).reshape(CHUNK * slots, LANES)
        sig = m.sig[r, c]
        glu = m.glu[pl.ds(half + t * CHUNK, CHUNK), :, c].reshape(CHUNK * slots, LANES)
        place = (l // 2) * 4 + l % 2
        m.da[r, lanes_of(place)] = (dglu * sig).astype(BF16)
        m.da[r, lanes_of(place + 2)] = (dglu * glu * (1.0 - sig)).astype(BF16)


def taps_back(m):
    rows, width = m.xn.shape
    taps, slots, _ = m.spread.shape
    frames = rows // slots
    half = (taps - 1) // 2
    lanes_q = width // 8 // LANES
    step = 8

    @pl.loop(0, width // LANES)
    def _(l):
        c = lanes_of(l)
        for low in range(0, taps, 16):
            count = min(16, taps - low)

            def body(t, acc, low=low, count=count):
                base = t * step
                out = []
                d = m.dconv[pl.ds(half + base, step), :, c]
                for k in range(count):
                    row = m.glu[pl.ds(base + low + k, step), :, c]
                    out.append(acc[k] + jnp.sum(d * row, axis=0))
                return tuple(out)

            acc = lax.fori_loop(0, frames // step, body,
                                tuple(jnp.zeros((slots, LANES), F32) for _ in range(count)))
            for k in range(count):
                m.small[l // 4, l % 4, pl.ds(low + k, 1), :] = jnp.sum(acc[k], axis=0, keepdims=True)
        for k in range(2):
            m.small[l // 4, l % 4, pl.ds(taps + k, 1), :] = jnp.sum(m.sums[k, :, c], axis=0, keepdims=True)


def project_back(m):
    width = m.xn.shape[1]

    @pl.loop(0, width // PIECE)
    def _(j):
        c = lanes_of(j, PIECE)
        m.wide[:, c] = lax.dot_general(m.da[...], m.w_in[c, :], NT, preferred_element_type=F32)


def norm_input_back(m):
    rows, width = m.xn.shape

    @pl.loop(0, rows // BLOCK)
    def _(i):
        r = pl.ds(pl.multiple_of(i * BLOCK, BLOCK), BLOCK)
        dxn = m.wide[r, :]
        xhat, rstd = statistics(m.xp[r, :].astype(F32))
        m1 = jnp.mean(dxn, axis=-1, keepdims=True)
        m2 = jnp.mean(dxn * xhat, axis=-1, keepdims=True)
        dx = rstd * (dxn - m1 - xhat * m2) + m.gm[r, :].astype(F32)
        m.dx[r, :] = dx.astype(BF16)


def save_pieces(m, y, k, b, part):
    size = m.pieces.shape[4]
    for core in range(2):
        for a in range(RING):
            low = (core * RING + a) * size
            m.pieces[core, k, y, a * RING + b] = part[low : low + size, :]


def weight_in_grad(m, side):
    @pl.loop(0, RING)
    def _(y):
        xn = m.xn[:, lanes_of(y, PIECE)]
        for b in range(RING):
            cols = m.da[:, pl.ds((side * RING + b) * PIECE, PIECE)]
            part = lax.dot_general(xn, cols, TN, preferred_element_type=F32)
            save_pieces(m, y, side, b, part.astype(BF16))


def weight_out_grad(m):
    @pl.loop(0, RING)
    def _(y):
        sw = m.sw[:, lanes_of(y, PIECE)]
        for b in range(RING):
            part = lax.dot_general(sw, m.gm[:, pl.ds(b * PIECE, PIECE)], TN, preferred_element_type=F32)
            save_pieces(m, y, 2, b, part.astype(BF16))


def module_kernel(scale, names, *refs):
    m = types.SimpleNamespace(**dict(zip(names, refs)))
    data = lax.axis_index("dp")
    shard = lax.axis_index("fsdp")
    y, core = shard // 2, shard % 2
    n_data = m.sendb.shape[0]
    slots, frames, width = m.cot.shape
    rows = slots * frames
    per = m.w_in_shard.shape[0]
    ring_y = range(1, RING)
    ring_d = range(1, n_data)

    def at_y(offset):
        return lax.rem(y + offset, RING)

    def at_d(offset):
        return lax.rem(data + offset, n_data)

    partner = (data, y * 2 + (1 - core))

    def peer_y(offset):
        return (data, at_y(offset) * 2 + core)

    def peer_d(offset):
        return (at_d(offset), shard)

    barrier = pltpu.get_barrier_semaphore()
    pl.semaphore_signal(barrier, inc=1, device_id=partner, device_id_type=MESH)
    for o in ring_y:
        pl.semaphore_signal(barrier, inc=1, device_id=peer_y(o), device_id_type=MESH)
    for o in ring_d:
        pl.semaphore_signal(barrier, inc=1, device_id=peer_d(o), device_id_type=MESH)

    pending = []

    def push(src, dst, sems, place, device, keep=True):
        copy = pltpu.make_async_remote_copy(
            src_ref=src, dst_ref=dst, send_sem=sems[0].at[place], recv_sem=sems[1].at[place],
            device_id=device, device_id_type=MESH)
        copy.start()
        if keep:
            pending.append(copy)
        return copy

    def arrive(copies):
        for copy in copies:
            copy.wait_recv()

    def wide(a):
        return a.astype(F32)

    mine = pl.ds(pl.multiple_of(shard * per, per), per)
    chunks = width // PIECE
    for j in range(chunks):
        m.w_in[mine, pl.ds(2 * j * PIECE, PIECE)] = m.w_in_shard[:, pl.ds(j * PIECE, PIECE)]
        m.w_in[mine, pl.ds((2 * j + 1) * PIECE, PIECE)] = m.w_in_shard[:, pl.ds(width + j * PIECE, PIECE)]
    m.w_out[mine, :] = m.w_out_shard[...]

    n_shard = 2 * RING

    def base(p):
        return (p * n_shard + shard) * slots

    @pl.loop(0, n_data)
    def _(p):
        found, place, out_block = 0, 0, 0
        for j in range(slots):
            hit = m.owner[base(p) + j] == data
            found = found + jnp.where(hit, 1, 0)
            place = place + jnp.where(hit, m.slot[base(p) + j], 0)
            out_block = out_block + jnp.where(m.owner[base(data) + j] == p, j, 0)
        m.place[p] = place - slots * (1 - found)
        m.block_for[p] = jnp.minimum(out_block, slots - 1)
        m.sendb[p] = m.cot[jnp.minimum(place, slots - 1)]

    pl.semaphore_wait(barrier, 1 + len(ring_y) + len(ring_d))

    def part(j, owner_y):
        r = pl.ds(pl.multiple_of((owner_y * 2 + core) * per, per), per)
        if j < chunks:
            return m.w_in.at[r, pl.ds(2 * j * PIECE, 2 * PIECE)]
        return m.w_out.at[r, :]

    weights, passed = [], []
    right, left = 1, RING - 1

    def send_weights(j):
        src = part(j, y)
        weights.append([push(src, src, m.weight_sems, (j, i), peer_y(o)) for i, o in enumerate((right, left))])
        passed.append([push(src, src, m.pass_sems, (j, 0), partner)])

    ahead = 3
    for j in range(ahead):
        send_weights(j)

    def exchange(dst, sems):
        copies = [push(m.sendb.at[at_d(o)], dst.at[data], sems, o - 1, peer_d(o), False) for o in ring_d]
        dst[data] = m.sendb[data]
        return copies

    cot_copies = exchange(m.cot_recv, m.cot_sems)

    for b in range(slots):
        m.limit[pl.ds(b, 1), :] = jnp.full((1, LANES), m.lengths[base(data) + b], jnp.int32)
    prepare(m)
    norm_input(m)

    @pl.loop(0, slots)
    def _(s):
        source = 0
        for p in range(n_data):
            source = source + jnp.where(m.place[p] == s, p, 0)
        m.source_of[s] = jnp.minimum(source, n_data - 1)

    def weights_near(j):
        for i, (far, near) in enumerate(((left, right), (right, left))):
            weights[j][i].wait_recv()
            src = part(j, at_y(far))
            piece = src.at[pl.ds(i * (per // 2), per // 2), :]
            weights[j].append(push(piece, piece, m.weight_sems, (j, 2 + i), peer_y(near)))
            passed[j].append(push(src, src, m.pass_sems, (j, 1 + i), partner))
        if j + ahead <= chunks:
            send_weights(j + ahead)

    def weights_far(j):
        arrive(weights[j][2:])
        src = part(j, at_y(2))
        passed[j].append(push(src, src, m.pass_sems, (j, 3), partner))
        arrive(passed[j])

    weights_near(0)
    for j in range(chunks):
        weights_near(j + 1)
        weights_far(j)
        gate_chunk(m, j)
        conv_chunk(m, j)
    norm_conv(m)

    def core_start(k):
        return [push(m.pieces.at[1 - core, k], m.core_recv.at[k], m.core_sems, k, partner)]

    def first(k, copies):
        arrive(copies)

        @pl.loop(0, RING)
        def _(a):
            m.pieces[core, k, a] = (wide(m.pieces[core, k, a]) + wide(m.core_recv[k, a])).astype(BF16)

        return [push(m.pieces.at[core, k, at_y(o)], m.recv_y.at[k, o - 1], m.sum_y_sems,
                     (k, o - 1), peer_y(o)) for o in ring_y]

    def second(k, copies):
        arrive(copies)

        @pl.loop(0, n_data)
        def _(d):
            acc = wide(m.pieces[core, k, y, d])
            for o in ring_y:
                acc = acc + wide(m.recv_y[k, o - 1, d])
            m.pieces[core, k, y, d] = acc.astype(BF16)

        return [push(m.pieces.at[core, k, y, at_d(o)], m.last_d.at[k, o - 1], m.sum_d_sems,
                     (k, o - 1), peer_d(o)) for o in ring_d]

    def third(k, copies):
        arrive(copies)
        acc = wide(m.pieces[core, k, y, data])
        for o in ring_d:
            acc = acc + wide(m.last_d[k, o - 1])
        m.fin[k, data] = acc.astype(BF16)
        return [push(m.fin.at[k, data], m.fin.at[k, data], m.fin_sems, (k, o - 1), peer_d(o)) for o in ring_d]

    def last(k, copies):
        arrive(copies)
        size, cols = m.fin.shape[2], m.fin.shape[3]
        for a in range(RING):
            for b in range(RING):
                piece = wide(m.fin[k, a * RING + b]) * scale
                r = pl.ds(a * size, size)
                if k < 2:
                    m.grad_in[r, pl.ds((b % 2 * RING + k * 2 + b // 2) * cols, cols)] = piece
                else:
                    m.grad_out[r, pl.ds(b * cols, cols)] = piece

    arrive(cot_copies)
    for b in range(slots):
        m.dx[pl.ds(b * frames, frames), :] = m.cot_recv[m.owner[base(data) + b]]
    mask_cotangent(m)

    weight_out_grad(m)
    two = core_start(2)
    weights_far(chunks)
    mix_out(m)
    two = first(2, two)
    untime(m, m.lines)
    for copy in cot_copies:
        copy.wait_send()

    @pl.loop(0, n_data)
    def _(p):
        m.sendb[p] = m.lines[m.block_for[p]]

    out_copies = exchange(m.out_recv, m.out_sems)
    pending.extend(out_copies)

    norm_conv_back(m)
    conv_back(m, 0)
    weight_in_grad(m, 0)
    zero = core_start(0)
    two = second(2, two)
    zero = first(0, zero)
    conv_back(m, 1)
    weight_in_grad(m, 1)
    one = core_start(1)
    project_back(m)
    one = first(1, one)
    taps_back(m)

    small = [push(m.small.at[1 - core], m.small_core, m.small_sems, 0, partner)]
    norm_input_back(m)
    arrive(small)
    m.small_core[...] = m.small_core[...] + m.small[core]
    m.small_y[y] = m.small_core[y]
    small = [push(m.small_core.at[at_y(o)], m.small_y.at[y], m.small_sems, o, peer_y(o)) for o in ring_y]

    zero = second(0, zero)
    untime(m, m.grad_frames)
    two = third(2, two)
    arrive(out_copies)

    @pl.loop(0, slots)
    def _(s):
        m.out_frames[s] = m.out_recv[m.source_of[s]]

    zero = third(0, zero)
    one = second(1, one)

    arrive(small)
    m.small_d[data] = (m.small_y[0] + m.small_y[1]) + (m.small_y[2] + m.small_y[3])
    small = [push(m.small_d.at[data], m.small_d.at[data], m.small_d_sems, o - 1, peer_d(o)) for o in ring_d]
    last(2, two)
    last(0, zero)
    one = third(1, one)

    arrive(small)
    total = m.small_d[0]
    for d in range(1, n_data):
        total = total + m.small_d[d]
    m.small_all[core, y] = total
    own = m.small_all.at[core, y]
    small = [push(own, own, m.small_sems, RING + o, peer_y(o)) for o in ring_y]
    arrive(small)
    half = m.small_all.at[core]
    small = [push(half, half, m.small_sems, 2 * RING, partner)]
    last(1, one)

    arrive(small)
    lanes = m.small_all.shape[3]
    taps = m.taps.shape[0]
    for a in range(2):
        for b in range(RING):
            c = pl.ds((a * RING + b) * lanes, lanes)
            m.grad_taps[:, c] = m.small_all[a, b, pl.ds(0, taps), :] * scale
            m.grad_gain[:, c] = m.small_all[a, b, pl.ds(taps, 1), :] * scale
            m.grad_bias[:, c] = m.small_all[a, b, pl.ds(taps + 1, 1), :] * scale
    for copy in pending:
        copy.wait_send()


def module_call(scale, owner, slot, lengths, frames, cotangent, w_in, taps, gain, bias, w_out, n_data):
    slots, count, width = frames.shape
    rows = slots * count
    k = taps.shape[0]
    lines = -(-(k + 2) // 8) * 8
    size, cols = width // 32, width // RING
    lanes = width // 8
    shape = jax.ShapeDtypeStruct
    dma = pltpu.SemaphoreType.DMA
    inputs = dict(
        owner=owner, slot=slot, lengths=lengths,
        x=frames.reshape(rows, width), cot=cotangent, w_in_shard=w_in, taps=taps,
        gain=gain, bias=bias, w_out_shard=w_out)
    outputs = dict(
        out_frames=shape((slots, count, width), BF16),
        grad_frames=shape((slots, count, width), BF16),
        grad_in=shape((width // 8, 2 * width), F32),
        grad_out=shape((width // 8, width), F32),
        grad_taps=shape((k, width), F32),
        grad_gain=shape((1, width), F32),
        grad_bias=shape((1, width), F32))
    tables = dict(place=(n_data,), block_for=(n_data,), source_of=(slots,))
    buffers = dict(
        limit=((slots, LANES), jnp.int32),
        w_in=((width, 2 * width), BF16), w_out=((width, width), BF16),
        xp=((rows, width), BF16), xn=((rows, width), BF16), sig=((rows, width), F32),
        chat=((rows, width), F32), rstd=((rows, LANES), F32), sw=((rows, width), BF16),
        glu=((count + k - 1, slots, width), F32), dconv=((count + k - 1, slots, width), F32),
        spread=((k, slots, width), F32), gm=((rows, width), BF16), da=((rows, 2 * width), BF16),
        dx=((rows, width), BF16), wide=((rows, width), F32), sums=((2, slots, width), F32),
        to_time=((rows, rows), BF16), to_block=((rows, rows), BF16),
        lines=((slots, count, width), BF16), sendb=((n_data, count, width), BF16),
        cot_recv=((n_data, count, width), BF16), out_recv=((n_data, count, width), BF16),
        pieces=((2, 3, RING, n_data, size, cols), BF16),
        core_recv=((3, RING, n_data, size, cols), BF16),
        recv_y=((3, RING - 1, n_data, size, cols), BF16),
        last_d=((3, n_data - 1, size, cols), BF16),
        fin=((3, n_data, size, cols), BF16),
        small=((2, RING, lines, lanes), F32), small_core=((RING, lines, lanes), F32),
        small_y=((RING, lines, lanes), F32), small_d=((n_data, lines, lanes), F32),
        small_all=((2, RING, lines, lanes), F32))
    pairs = dict(
        weight_sems=(5, 4), pass_sems=(5, RING), cot_sems=(n_data - 1,), out_sems=(n_data - 1,),
        core_sems=(3,), sum_y_sems=(3, RING - 1), sum_d_sems=(3, n_data - 1), fin_sems=(3, n_data - 1),
        small_sems=(2 * RING + 1,), small_d_sems=(n_data - 1,))
    names = list(inputs) + list(outputs) + list(tables) + list(buffers)
    vmem = pl.BlockSpec(memory_space=pltpu.VMEM)
    smem = pl.BlockSpec(memory_space=pltpu.SMEM)

    def body(*refs):
        plain, sems = refs[: len(names)], refs[len(names) :]
        both = [(sems[2 * i], sems[2 * i + 1]) for i in range(len(pairs))]
        module_kernel(scale, names + list(pairs), *plain, *both)

    return pl.pallas_call(
        body,
        out_shape=tuple(outputs.values()),
        in_specs=[smem] * 3 + [vmem] * (len(inputs) - 3),
        out_specs=(vmem,) * len(outputs),
        scratch_shapes=[pltpu.SMEM(t, jnp.int32) for t in tables.values()]
        + [pltpu.VMEM(*b) for b in buffers.values()]
        + [dma(s) for s in pairs.values() for _ in range(2)],
        compiler_params=pltpu.CompilerParams(
            collective_id=0, has_side_effects=True, vmem_limit_bytes=VMEM_LIMIT),
        name="conv_module",
    )(*inputs.values())


VMEM_LIMIT = 63 * 2**20


def finish_kernel(*refs):
    count = len(refs) // 4
    plain, sems = refs[: 3 * count], refs[3 * count :]
    loads, stores = [], []
    for i in range(count):
        loads.append(pltpu.make_async_copy(plain[i], plain[2 * count + i], sems[i].at[0]))
        loads[-1].start()
    for i in range(count):
        loads[i].wait()
        stores.append(pltpu.make_async_copy(plain[2 * count + i], plain[count + i], sems[i].at[1]))
        stores[-1].start()
    for copy in stores:
        copy.wait()


def finish(arrays):
    hbm = pl.BlockSpec(memory_space=pl.ANY)
    return pl.pallas_call(
        finish_kernel,
        out_shape=tuple(jax.ShapeDtypeStruct(a.shape, a.dtype) for a in arrays),
        in_specs=[hbm] * len(arrays),
        out_specs=(hbm,) * len(arrays),
        scratch_shapes=[pltpu.VMEM(a.shape, a.dtype) for a in arrays]
        + [pltpu.SemaphoreType.DMA((2,)) for _ in arrays],
        compiler_params=pltpu.CompilerParams(vmem_limit_bytes=VMEM_LIMIT),
        name="finish",
    )(*arrays)


def shards(frames, lengths, owner, slot, w_in, kernel, dw_gain, dw_bias, w_out, cotangent):
    n_data = lax.axis_size("dp")
    n_shard = lax.axis_size("fsdp")
    slots, count, width = frames.shape
    scale = 1.0 / math.sqrt(slots * count * n_data * n_shard)
    results = module_call(
        scale, owner, slot, lengths, frames, cotangent, w_in, kernel, dw_gain[None], dw_bias[None], w_out,
        n_data)
    out_frames, grad_frames, grad_in, grad_out, grad_taps, grad_gain, grad_bias = finish(results)
    return (
        out_frames,
        grad_frames,
        grad_in,
        grad_taps,
        grad_gain[0],
        grad_bias[0],
        grad_out,
    )


def solution(mesh):
    placed = (
        P(("dp", "fsdp"), None, None),
        P(),
        P(),
        P(),
        P("fsdp", None),
        P(),
        P(),
        P(),
        P("fsdp", None),
        P(("dp", "fsdp"), None, None),
    )
    return jax.shard_map(
        shards,
        mesh=mesh,
        in_specs=placed,
        out_specs=(
            P(("dp", "fsdp"), None, None),
            P(("dp", "fsdp"), None, None),
            P("fsdp", None),
            P(),
            P(),
            P(),
            P("fsdp", None),
        ),
        check_vma=False,
    )
```
